32 devices in a mesh: dp: 8 (over z, y), mp: 4 (over x, core).
Axes of the slice: x: 2, y: 2, z: 4, core: 2. Of those that a mesh axis runs over, the one named last changes fastest.
Arguments:
- streams: bfloat16 [8, 1024, 768], P('dp', 'mp'), may hold values from -6 to 6
- page_lengths: int32 [4, 16], replicated, may hold values from 50 to 100
- attn_in: bfloat16 [2, 2, 3, 768, 768], P(None, None, None, 'mp'), may hold values from -0.21875 to 0.21875
- attn_out: bfloat16 [2, 2, 768, 768], P(None, None, 'mp'), may hold values from -0.875 to 0.875
- ffn_in: bfloat16 [2, 3072, 768], P(None, 'mp'), may hold values from -0.21875 to 0.21875
- ffn_bias: float32 [2, 3072], P(None, 'mp'), may hold values from -3 to 3
- ffn_out: bfloat16 [2, 3072, 768], P(None, 'mp'), may hold values from -0.109375 to 0.109375
- out_bias: float32 [2, 768], replicated, may hold values from -3 to 3
- norm_gain: float32 [2, 3, 768], replicated, may hold values from 0.5 to 1.5
- norm_bias: float32 [2, 3, 768], replicated, may hold values from -3 to 3
- gate_weight: bfloat16 [2, 768, 768], replicated, may hold values from -0.21875 to 0.21875
- gate_bias: float32 [768], replicated, may hold values from -3 to 3
- united_grad: bfloat16 [4, 4, 256, 768], P(None, 'mp', 'dp'), may hold values from -6 to 6
Outputs:
- united: float32 [4, 4, 256, 768], P(None, 'mp', 'dp')
- streams_grad: float32 [8, 1024, 768], P('dp', 'mp')
- attn_in_grad: float32 [2, 2, 3, 768, 768], P(None, None, None, 'mp')
- attn_out_grad: float32 [2, 2, 768, 768], P(None, None, 'mp')
- ffn_in_grad: float32 [2, 3072, 768], P(None, 'mp')
- ffn_bias_grad: float32 [2, 3072], P(None, 'mp')
- ffn_out_grad: float32 [2, 3072, 768], P(None, 'mp')
- out_bias_grad: float32 [2, 768], replicated
- norm_gain_grad: float32 [2, 3, 768], replicated
- norm_bias_grad: float32 [2, 3, 768], replicated
- gate_weight_grad: float32 [2, 768, 768], replicated
- gate_bias_grad: float32 [768], replicated
The draws below stay inside these ranges and needn't reach their ends.
All inputs are finite; a program needn't handle non-finite values.
Results may differ from the reference program's by a relative error of at most 0.022.
Values may be sent and summed in bfloat16 or wider, within the bound.
No kernel may reach another device: no remote copies, remote signals or barrier semaphores. Data moves between devices by JAX's collectives and lax.ppermute only.
A program may use at most 192 MiB of HBM per device.

```python
import jax
import jax.numpy as jnp
from jax import lax

D = 768
H = 12
DH = 64
FF = 3072
L = 1024
PAGES = 16
PAGE_MIN = 50
PAGE_MAX = 100
SEQS = 4
N_MP = 4


def place_ends(result, own_key, least, top_value):
    longest = result.shape.index(max(result.shape))
    spots = []
    for shift in (0, 1):
        where = [jax.random.randint(jax.random.fold_in(own_key, axis), (), 0, length) for axis, length in enumerate(result.shape)]
        where[longest] = (where[longest] + shift) % result.shape[longest]
        spots.append(tuple(where))
    return result.at[spots[0]].set(least).at[spots[1]].set(top_value)


def shard_levels(stream_key, shape, shards, least, largest):
    def one(dim, parts):
        heights = jax.random.uniform(jax.random.fold_in(jax.random.fold_in(stream_key, 6), dim), (parts,), jnp.float32, least / len(shards), largest / len(shards))
        return jnp.repeat(jnp.exp(heights), shape[dim] // parts).reshape((-1,) + (1,) * (len(shape) - dim - 1))

    level = one(*shards[0])
    for cut in shards[1:]:
        level = level * one(*cut)
    return level


def normal_values(stream_key, shape, spread, most, split=(), kind=jnp.bfloat16):
    factor_of = shard_levels(stream_key, shape, split, -0.22, 0.18) if split else 1.0
    result = jax.random.normal(stream_key, shape, jnp.float32) * spread * factor_of
    return jnp.minimum(jnp.maximum(result, -most), most).astype(kind)


def setup_inputs(seed: int = 0) -> dict:
    arg_keys = jax.random.split(jax.random.key(seed), 14)
    streams = normal_values(arg_keys[0], (2 * SEQS, L, D), 1.0, 6.0, ((0, 8), (1, 4)))
    page_lengths = place_ends(jax.random.randint(arg_keys[1], (SEQS, PAGES), PAGE_MIN, PAGE_MAX + 1), jax.random.fold_in(arg_keys[1], 1), PAGE_MIN, PAGE_MAX).astype(jnp.int32)
    attn_in = normal_values(arg_keys[2], (2, 2, 3, D, D), D ** -0.5, 0.21875, ((3, 4),))
    attn_out = normal_values(arg_keys[3], (2, 2, D, D), (D // 16) ** -0.5, 0.875, ((2, 4),))
    ffn_in = normal_values(arg_keys[4], (2, FF, D), D ** -0.5, 0.21875, ((1, 4),))
    ffn_bias = normal_values(arg_keys[5], (2, FF), 0.5, 3.0, ((1, 4),), jnp.float32)
    ffn_out = normal_values(arg_keys[6], (2, FF, D), FF ** -0.5, 0.109375, ((1, 4),))
    out_bias = normal_values(arg_keys[7], (2, D), 0.5, 3.0, (), jnp.float32)
    norm_gain = jnp.clip(1.0 + 0.1 * jax.random.normal(arg_keys[8], (2, 3, D), jnp.float32), 0.5, 1.5)
    norm_bias = normal_values(arg_keys[9], (2, 3, D), 0.5, 3.0, (), jnp.float32)
    gate_weight = normal_values(arg_keys[10], (2, D, D), D ** -0.5, 0.21875)
    gate_bias = normal_values(arg_keys[11], (D,), 0.5, 3.0, (), jnp.float32)
    united_grad = normal_values(arg_keys[12], (SEQS, N_MP, L // N_MP, D), 1.0, 6.0, ((1, 4), (2, 8)))
    return {"streams": streams, "page_lengths": page_lengths, "attn_in": attn_in, "attn_out": attn_out, "ffn_in": ffn_in, "ffn_bias": ffn_bias, "ffn_out": ffn_out, "out_bias": out_bias, "norm_gain": norm_gain, "norm_bias": norm_bias, "gate_weight": gate_weight, "gate_bias": gate_bias, "united_grad": united_grad}


@jax.custom_vjp
def low(v):
    return lax.optimization_barrier(v.astype(jnp.bfloat16)).astype(jnp.float32)

@jax.custom_vjp
def low_back(v):
    return v

def low_keep(v):
    return (low(v), None)

def low_pass(kept, grad):
    return (grad,)

def back_keep(v):
    return (v, None)

def back_low(kept, grad):
    return (low(grad),)
low.defvjp(low_keep, low_pass)
low_back.defvjp(back_keep, back_low)
EPS = 1e-05
SCALE = 0.125
MASKED = -1e+30
HIGH = lax.Precision.HIGHEST

def page_segments(lengths):
    page_ends = jnp.cumsum(lengths).astype(jnp.int32)
    page_fits = page_ends <= L
    position = jnp.arange(L, dtype=jnp.int32)
    before = (page_ends[None, :] <= position[:, None]) & page_fits[None, :]
    segment = lax.optimization_barrier(jnp.sum(before.astype(jnp.int32), axis=1)).astype(jnp.int32)
    used_rows = jnp.max(jnp.where(page_fits, page_ends, 0))
    return (segment, (position < used_rows).astype(jnp.float32))

def layer_norm(residual, gain_row, shift_row):
    center = residual - lax.optimization_barrier(jnp.mean(residual, axis=-1, keepdims=True))
    return center * lax.rsqrt(lax.optimization_barrier(jnp.mean(center * center, axis=-1, keepdims=True)) + EPS) * gain_row + shift_row

def project(inputs, weights):
    return jnp.dot(inputs, weights.T, precision=HIGH, preferred_element_type=jnp.float32)

def attention(query_in, key_in, w_in, w_out, segment):
    queries = low_back(low(project(query_in, w_in[0]))).reshape(L, H, DH)
    key_heads = low_back(low(project(key_in, w_in[1]))).reshape(L, H, DH)
    values = low_back(low(project(key_in, w_in[2]))).reshape(L, H, DH)
    block_rows = min(L, 512)

    def one_block(offset):
        query_block = lax.dynamic_slice_in_dim(queries, offset, block_rows, 0)
        seg_block = lax.dynamic_slice_in_dim(segment, offset, block_rows, 0)
        scores = low_back(jnp.einsum('qhd,khd->hqk', query_block, key_heads, precision=HIGH) * SCALE)
        allowed = seg_block[:, None] == segment[None, :]
        scores = jnp.where(allowed[None], scores, MASKED)
        top_score = lax.optimization_barrier(jnp.max(scores, axis=-1, keepdims=True))
        expo = jnp.exp(scores - top_score)
        weights = expo / lax.optimization_barrier(jnp.sum(expo, axis=-1, keepdims=True))
        return jnp.einsum('hqk,khd->qhd', low(weights), values, precision=HIGH)
    offsets = jnp.arange(L // block_rows, dtype=jnp.int32) * block_rows
    outputs = lax.map(jax.checkpoint(one_block), offsets).reshape(L, H * DH)
    outputs = low_back(low(outputs))
    return low_back(jnp.dot(outputs, w_out, precision=HIGH, preferred_element_type=jnp.float32))

def stream_layer(own_in, partner_in, segment, params, modality):
    attn_in, attn_out, ffn_in, ffn_bias, ffn_out, out_bias, norm_gain, norm_bias = params
    cross = attention(own_in, low_back(partner_in), attn_in[modality, 0], attn_out[modality, 0], segment)
    first_norm = layer_norm(own_in + cross, norm_gain[modality, 0], norm_bias[modality, 0])
    first_low = low(first_norm)
    self_branch = attention(first_low, first_low, attn_in[modality, 1], attn_out[modality, 1], segment)
    second_norm = layer_norm(first_norm + self_branch, norm_gain[modality, 1], norm_bias[modality, 1])
    pre_act = low_back(project(low(second_norm), ffn_in[modality]) + ffn_bias[modality])
    act_low = low(jax.nn.gelu(pre_act))
    branch = low_back(jnp.dot(act_low, ffn_out[modality], precision=HIGH, preferred_element_type=jnp.float32)) + out_bias[modality]
    stream_out = layer_norm(second_norm + branch, norm_gain[modality, 2], norm_bias[modality, 2])
    return low_back(low(stream_out))

def reference(streams, page_lengths, attn_in, attn_out, ffn_in, ffn_bias, ffn_out, out_bias, norm_gain, norm_bias, gate_weight, gate_bias, united_grad):

    def forward(streams_f, attn_in_f, attn_out_f, ffn_in_f, ffn_bias_f, ffn_out_f, out_bias_f, norm_gain_f, norm_bias_f, gate_weight_f, gate_bias_f):
        params = (attn_in_f, attn_out_f, ffn_in_f, ffn_bias_f, ffn_out_f, out_bias_f, norm_gain_f, norm_bias_f)

        def one_pair(sequence):
            segment, valid_rows = page_segments(page_lengths[sequence])
            text_in = streams_f[sequence]
            vision_in = streams_f[SEQS + sequence]
            text_out = stream_layer(text_in, vision_in, segment, params, 0)
            vision_out = stream_layer(vision_in, text_in, segment, params, 1)
            gate_pre = low_back(project(text_out, gate_weight_f[0]) + project(vision_out, gate_weight_f[1]) + gate_bias_f)
            gate_value = jax.nn.sigmoid(gate_pre)
            return valid_rows[:, None] * (gate_value * text_out + (1.0 - gate_value) * vision_out)
        united_all = lax.map(jax.checkpoint(one_pair), jnp.arange(SEQS, dtype=jnp.int32))
        return united_all.reshape(SEQS, N_MP, L // N_MP, D)
    united_value, pull = jax.vjp(forward, streams.astype(jnp.float32), attn_in.astype(jnp.float32), attn_out.astype(jnp.float32), ffn_in.astype(jnp.float32), ffn_bias.astype(jnp.float32), ffn_out.astype(jnp.float32), out_bias.astype(jnp.float32), norm_gain.astype(jnp.float32), norm_bias.astype(jnp.float32), gate_weight.astype(jnp.float32), gate_bias.astype(jnp.float32))
    grads = pull(united_grad.astype(jnp.float32))
    return (united_value, grads[0], grads[1], grads[2], grads[3], grads[4], grads[5], grads[6], grads[7], grads[8], grads[9], grads[10])
```

```python
import functools

import jax
import jax.numpy as jnp
from jax import lax
from jax.experimental import pallas as pl
from jax.experimental.pallas import tpu as pltpu
from jax.sharding import PartitionSpec as P

DH = 64
L = 1024
PAGES = 16
EPS = 1e-05
SCALE = 0.125
LOG2E = 1.4426950408889634
MASKED = -1e30
HALO = 128
PIECES = 4
BF = jnp.bfloat16
F32 = jnp.float32
VMEM_LIMIT = 60 * 1024 * 1024

VM = pl.BlockSpec(memory_space=pltpu.VMEM)
SM = pl.BlockSpec(memory_space=pltpu.SMEM)
ANY = pl.BlockSpec(memory_space=pl.ANY)


def nn(a, b):
    return lax.dot_general(a, b, (((1,), (0,)), ((), ())), preferred_element_type=F32)


def nt(a, b):
    return lax.dot_general(a, b, (((1,), (1,)), ((), ())), preferred_element_type=F32)


def tn(a, b):
    return lax.dot_general(a, b, (((0,), (0,)), ((), ())), preferred_element_type=F32)


def call(body, outs, scratch=(), flops=0, traffic=0, name=None, specs=None, out_specs=None, aliases=None):
    def run(*args):
        return pl.pallas_call(
            body,
            out_shape=outs,
            in_specs=specs if specs is not None else [SM] + [VM] * (len(args) - 1),
            out_specs=out_specs if out_specs is not None else jax.tree.map(lambda _: VM, outs),
            scratch_shapes=list(scratch),
            input_output_aliases=aliases or {},
            compiler_params=pltpu.CompilerParams(vmem_limit_bytes=VMEM_LIMIT),
            cost_estimate=pl.CostEstimate(flops=flops, bytes_accessed=traffic, transcendentals=0),
            name=name,
        )(*args)

    return run


def struct(shape, dtype):
    return jax.ShapeDtypeStruct(shape, dtype)


def segment_of(position, info):
    segment = jnp.zeros_like(position)
    for page in range(PAGES):
        segment = segment + (info[page] <= position).astype(jnp.int32)
    return segment


def block_bias(info, block, keys):
    base = info[PAGES]
    query = base + block * HALO + lax.broadcasted_iota(jnp.int32, (HALO, 1), 0)
    key = base + (block - 1) * HALO + lax.broadcasted_iota(jnp.int32, (1, keys), 1)
    query_seg = segment_of(query, info)
    key_seg = segment_of(key, info)
    key_seg = jnp.where((key >= 0) & (key < L), key_seg, -1)
    return jnp.where(query_seg == key_seg, 0.0, MASKED)


def normalise(residual, gain, shift):
    center = residual - jnp.mean(residual, axis=-1, keepdims=True)
    inverse = lax.rsqrt(jnp.mean(center * center, axis=-1, keepdims=True) + EPS)
    normed = center * inverse
    return normed * gain + shift, normed, inverse


def norm_back(cot, gain, normed, inverse):
    grad = cot * gain
    back = inverse * (
        grad
        - jnp.mean(grad, axis=-1, keepdims=True)
        - normed * jnp.mean(grad * normed, axis=-1, keepdims=True)
    )
    return back, jnp.sum(cot * normed, axis=0, keepdims=True), jnp.sum(cot, axis=0, keepdims=True)


def load_matrix(which, turn, near, far, buffer):
    rows = near.shape[1]
    spots = ((near, which), (near, PIECES + (which ^ turn)), (far, which), (far, PIECES + (which ^ turn)))
    for place, (source, index) in enumerate(spots):
        buffer[place * rows : (place + 1) * rows, :] = source[index]


def store_matrix(which, turn, value, near, far):
    rows = near.shape[1]
    spots = ((near, 0), (near, PIECES), (far, 0), (far, PIECES))
    for place, (target, start) in enumerate(spots):
        target[start + (which ^ turn)] = value[place * rows : (place + 1) * rows, :].astype(BF)


def attention_forward(
    info, query_in, left, own, right, near, far, resid, gain, shift,
    q_out, k_out, v_out, o_out, log_out, norm_out, inv_out, full_out, low_out,
    extended, matrix,
):
    turn = info[PAGES + 1]
    rows, width = query_in.shape
    keys = rows + 2 * HALO
    window = 3 * HALO
    extended[0:HALO, :] = left[...]
    extended[HALO : HALO + rows, :] = own[...]
    extended[HALO + rows : keys, :] = right[...]
    load_matrix(0, turn, near, far, matrix)
    q_out[...] = nt(query_in[...], matrix[...]).astype(BF)
    load_matrix(1, turn, near, far, matrix)
    k_out[...] = nt(extended[...], matrix[...]).astype(BF)
    load_matrix(2, turn, near, far, matrix)
    v_out[...] = nt(extended[...], matrix[...]).astype(BF)
    lane = lax.broadcasted_iota(jnp.int32, (1, 2 * DH), 1)
    first = lane < DH
    for block in range(rows // HALO):
        bias = block_bias(info, block, window)
        row = slice(block * HALO, (block + 1) * HALO)
        span = slice(block * HALO, block * HALO + window)
        logs = jnp.zeros((HALO, 2 * DH), F32)
        for pair in range(width // (2 * DH)):
            cols = slice(pair * 2 * DH, (pair + 1) * 2 * DH)
            queries = q_out[row, cols]
            key_pair = k_out[span, cols]
            value_pair = v_out[span, cols]
            mixed = []
            for half in range(2):
                mine = first if half == 0 else ~first
                scores = nt(jnp.where(mine, queries, jnp.zeros_like(queries)), key_pair)
                scores = scores * (SCALE * LOG2E) + bias
                top = jnp.max(scores, axis=-1, keepdims=True)
                expo = jnp.exp2(scores - top)
                total = jnp.sum(expo, axis=-1, keepdims=True)
                mixed.append(nn(expo.astype(BF), value_pair) / total)
                logs = jnp.where(lane == 2 * pair + half, top + jnp.log2(total), logs)
            o_out[row, cols] = jnp.where(first, mixed[0], mixed[1]).astype(BF)
        log_out[row, :] = logs
    load_matrix(3, turn, near, far, matrix)
    residual = resid[...].astype(F32) + nn(o_out[...], matrix[...])
    full, normed, inverse = normalise(residual, gain[...], shift[...])
    norm_out[...] = normed
    inv_out[...] = inverse
    full_out[...] = full
    low_out[...] = full.astype(BF)


def attention_backward(
    same_input, info, cot_in, from_left, from_right, normed, inverse, gain,
    q_in, k_in, v_in, o_in, log_in, query_in, left, own, right, near, far,
    query_cot, key_cot, to_left, to_right, near_out, far_out, gain_out, shift_out,
    extended, matrix, low, o_cot, dq, dk, dv, dkl, dvl,
):
    turn = info[PAGES + 1]
    rows, width = query_in.shape
    keys = rows + 2 * HALO
    window = 3 * HALO
    if same_input:
        cot = cot_in[...]
    else:
        cot = cot_in[...] + jnp.concatenate([from_left[...], from_right[...]], axis=0).astype(F32)
    back, gain_grad, shift_grad = norm_back(cot, gain[...], normed[...], inverse[...])
    gain_out[...] = gain_grad
    shift_out[...] = shift_grad
    query_cot[...] = back
    low[...] = back.astype(BF)
    load_matrix(3, turn, near, far, matrix)
    o_cot[...] = nt(low[...], matrix[...]).astype(BF)
    store_matrix(3, turn, tn(o_in[...], low[...]), near_out, far_out)
    dk[...] = jnp.zeros_like(dk)
    dv[...] = jnp.zeros_like(dv)
    lane = lax.broadcasted_iota(jnp.int32, (1, 2 * DH), 1)
    first = lane < DH
    for block in range(rows // HALO):
        bias = block_bias(info, block, window)
        row = slice(block * HALO, (block + 1) * HALO)
        span = slice(block * HALO, block * HALO + window)
        logs = log_in[row, :]
        for pair in range(width // (2 * DH)):
            cols = slice(pair * 2 * DH, (pair + 1) * 2 * DH)
            queries = q_in[row, cols]
            cots = o_cot[row, cols]
            key_pair = k_in[span, cols]
            value_pair = v_in[span, cols]
            grads = []
            key_sum = None
            for half in range(2):
                mine = first if half == 0 else ~first
                own_q = jnp.where(mine, queries, jnp.zeros_like(queries))
                own_c = jnp.where(mine, cots, jnp.zeros_like(cots))
                scores = nt(own_q, key_pair) * (SCALE * LOG2E) + bias
                which = 2 * pair + half
                weights = jnp.exp2(scores - logs[:, which : which + 1])
                weight_cot = nt(own_c, value_pair)
                inner = jnp.sum(weights * weight_cot, axis=-1, keepdims=True)
                score_cot = (weights * (weight_cot - inner)).astype(BF)
                grads.append(nn(score_cot, key_pair))
                part_k = tn(score_cot, own_q)
                part_v = tn(weights.astype(BF), own_c)
                key_sum = (part_k, part_v) if key_sum is None else (key_sum[0] + part_k, key_sum[1] + part_v)
            dq[row, cols] = (jnp.where(first, grads[0], grads[1]) * SCALE).astype(BF)
            dk[span, cols] += key_sum[0]
            dv[span, cols] += key_sum[1]
    extended[0:HALO, :] = left[...]
    extended[HALO : HALO + rows, :] = own[...]
    extended[HALO + rows : keys, :] = right[...]
    dkl[...] = (dk[...] * SCALE).astype(BF)
    dvl[...] = dv[...].astype(BF)
    load_matrix(0, turn, near, far, matrix)
    query_cot[...] += nn(dq[...], matrix[...])
    store_matrix(0, turn, tn(dq[...], query_in[...]), near_out, far_out)
    load_matrix(1, turn, near, far, matrix)
    dk[...] = nn(dkl[...], matrix[...])
    store_matrix(1, turn, tn(dkl[...], extended[...]), near_out, far_out)
    load_matrix(2, turn, near, far, matrix)
    dk[...] += nn(dvl[...], matrix[...])
    store_matrix(2, turn, tn(dvl[...], extended[...]), near_out, far_out)
    to_left[...] = dk[0:HALO, :].astype(BF)
    to_right[...] = dk[HALO + rows : keys, :].astype(BF)
    middle = dk[HALO : HALO + rows, :]
    if same_input:
        query_cot[...] += middle
        key_cot[...] = jnp.zeros_like(key_cot)
    else:
        key_cot[...] = middle


def gelu_parts(value):
    root = 0.7978845608028654
    square = value * value
    inner = jnp.tanh(root * (value + 0.044715 * value * square))
    half = 0.5 * (1.0 + inner)
    slope = half + 0.5 * value * (1.0 - inner * inner) * (root * (1.0 + 3.0 * 0.044715 * square))
    return value * half, slope


def ffn_forward(
    low, full, near_up, far_up, near_down, far_down, up_bias, down_bias, gain, shift,
    act_out, slope_out, norm_out, inv_out, low_out, total,
):
    step = pl.program_id(0)
    half = pl.num_programs(0) // 2

    @pl.when(step == 0)
    def _():
        total[...] = full[...] + down_bias[...]

    def chunk(up, down):
        rows = up.shape[0] * up.shape[1]
        pre = nt(low[...], up[...].reshape(rows, up.shape[2])) + up_bias[...]
        value, slope = gelu_parts(pre)
        value = value.astype(BF)
        act_out[...] = value
        slope_out[...] = slope
        total[...] += nn(value, down[...].reshape(rows, down.shape[2]))

    @pl.when(step < half)
    def _():
        chunk(near_up, near_down)

    @pl.when(step >= half)
    def _():
        chunk(far_up, far_down)

    @pl.when(step == pl.num_programs(0) - 1)
    def _():
        out, normed, inverse = normalise(total[...], gain[...], shift[...])
        norm_out[...] = normed
        inv_out[...] = inverse
        low_out[...] = out.astype(BF)


def ffn_backward(
    cot_in, normed, inverse, gain, low, act, slope, near_up, far_up, near_down, far_down,
    total, near_up_out, far_up_out, near_down_out, far_down_out,
    bias_out, down_bias_out, gain_out, shift_out, branch,
):
    step = pl.program_id(0)
    half = pl.num_programs(0) // 2

    @pl.when(step == 0)
    def _():
        back, gain_grad, shift_grad = norm_back(cot_in[...].astype(F32), gain[...], normed[...], inverse[...])
        gain_out[...] = gain_grad
        shift_out[...] = shift_grad
        down_bias_out[...] = jnp.sum(back, axis=0, keepdims=True)
        total[...] = back
        branch[...] = back.astype(BF)

    def chunk(up, down, up_out, down_out):
        rows = up.shape[0] * up.shape[1]
        act_cot = nt(branch[...], down[...].reshape(rows, down.shape[2]))
        pre_cot = (act_cot * slope[...]).astype(BF)
        bias_out[...] = jnp.sum(pre_cot.astype(F32), axis=0, keepdims=True)
        down_out[...] = tn(act[...], branch[...]).astype(BF).reshape(down_out.shape)
        up_out[...] = tn(pre_cot, low[...]).astype(BF).reshape(up_out.shape)
        total[...] += nn(pre_cot, up[...].reshape(rows, up.shape[2]))

    @pl.when(step < half)
    def _():
        chunk(near_up, near_down, near_up_out, near_down_out)

    @pl.when(step >= half)
    def _():
        chunk(far_up, far_down, far_up_out, far_down_out)


def gate_kernel(
    info, text, vision, weight, bias, valid, cot_in,
    united, text_out, vision_out, near_out, far_out, bias_out, grads,
):
    turn = info[PAGES + 1]
    place = info[PAGES + 2]
    text_low = text[...]
    vision_low = vision[...]
    gate = jax.nn.sigmoid(nt(text_low, weight[0]) + nt(vision_low, weight[1]) + bias[...])
    text_full = text_low.astype(F32)
    vision_full = vision_low.astype(F32)
    mask = valid[...]
    united[...] = mask * (gate * text_full + (1.0 - gate) * vision_full)
    cot = cot_in[...].astype(F32) * mask
    gate_cot = (cot * (text_full - vision_full) * gate * (1.0 - gate)).astype(BF)
    text_out[...] = (cot * gate + nn(gate_cot, weight[0])).astype(BF)
    vision_out[...] = (cot * (1.0 - gate) + nn(gate_cot, weight[1])).astype(BF)
    bias_out[...] = jnp.sum(gate_cot.astype(F32), axis=0, keepdims=True)
    width = text_low.shape[1]
    grads[0:width, :] = tn(gate_cot, text_low)
    grads[width : 2 * width, :] = tn(gate_cot, vision_low)
    rows = near_out.shape[1]
    for spot, (target, start) in enumerate(((near_out, 0), (near_out, PIECES), (far_out, 0), (far_out, PIECES))):
        shard = place ^ (0, 2, 1, 3)[spot]
        for piece in range(PIECES):
            at = pl.multiple_of((shard * PIECES + (piece ^ turn)) * rows, rows)
            target[start + piece] = grads[pl.ds(at, rows), :].astype(BF)


def place_gate(info, parts, out):
    out[...] = parts[...].astype(F32)


def place_ffn(order, info, first, second, out, wide, sems):
    turn = info[PAGES + 1]
    flip = info[PAGES + 3]
    copies = []
    for side, source in enumerate((first, second)):
        for index in range(2):
            piece = order[side][index] ^ turn
            for kind in range(2):
                slot = (side * 2 + index) * 2 + kind
                wide[slot] = source[index, kind].astype(F32)
                copy = pltpu.make_async_copy(wide.at[slot], out.at[kind ^ flip, piece], sems.at[slot])
                copy.start()
                copies.append(copy)
    for copy in copies:
        copy.wait()


def place_attention(order, layer, info, first, second, *rest):
    in_out, out_out, wide, sems = rest[-4:]
    turn = info[PAGES + 1]
    flip = info[PAGES + 3]
    for side, source in enumerate((first, second)):
        for index in range(2):
            piece = order[side][index] ^ turn
            for kind in range(2):
                slot = (side * 2 + index) * 2 + kind
                wide[slot] = source[index, kind].astype(F32)

                @pl.when(piece < 3)
                def _():
                    pltpu.make_async_copy(wide.at[slot], in_out.at[kind ^ flip, layer, piece], sems.at[slot]).start()

                @pl.when(piece == 3)
                def _():
                    pltpu.make_async_copy(wide.at[slot], out_out.at[kind ^ flip, layer], sems.at[slot]).start()

    for slot in range(8):
        pltpu.make_async_copy(wide.at[slot], out_out.at[0, layer], sems.at[slot]).wait()


def body(
    streams, page_lengths, attn_in, attn_out, ffn_in, ffn_bias, ffn_out, out_bias,
    norm_gain, norm_bias, gate_weight, gate_bias, united_grad,
):
    devices = lax.axis_size("dp")
    half_axis = devices // 2
    group_bits = half_axis.bit_length() - 1
    data_index = lax.axis_index("dp")
    place = lax.axis_index("mp")
    modality = data_index // half_axis
    sequence = data_index % half_axis
    turn = data_index % PIECES
    own = streams[0]
    rows, width = own.shape
    keys = rows + 2 * HALO
    shard = attn_in.shape[3]

    def swap(value, axis, mask):
        pairs = [(source, source ^ mask) for source in range(lax.axis_size(axis))]
        return lax.ppermute(value, axis, pairs)

    def mp(value, mask):
        return swap(value, "mp", mask)

    def dp(value, mask):
        return swap(value, "dp", mask)

    count = lax.axis_size("mp")

    def to_next(value):
        return lax.ppermute(value, "mp", [(index, index + 1) for index in range(count - 1)])

    def to_previous(value):
        return lax.ppermute(value, "mp", [(index + 1, index) for index in range(count - 1)])

    def choose(stacked):
        return lax.dynamic_index_in_dim(stacked, modality, 0, keepdims=False)

    def pick(stacked, index):
        return lax.dynamic_index_in_dim(stacked, index, 0, keepdims=False)

    def turned(stacked):
        return jnp.stack([pick(stacked, piece ^ turn) for piece in range(PIECES)])

    lengths = pick(page_lengths, sequence)
    below = jnp.arange(PAGES)[:, None] >= jnp.arange(PAGES)[None, :]
    ends = jnp.sum(jnp.where(below, lengths[None, :], 0), axis=1)
    ends = jnp.where(ends <= L, ends, 2 * L)
    info = jnp.concatenate(
        [ends, jnp.stack([place * rows, turn, place, modality])]
    ).astype(jnp.int32)

    modal_in = choose(attn_in)
    modal_out = choose(attn_out)
    gains = choose(norm_gain)[:, None, :]
    shifts = choose(norm_bias)[:, None, :]

    def spread(mine, rel_order):
        part = mp(pick(mine, turn), 2)
        if rel_order == "yz":
            other = dp(part, 1)
            pair = jnp.stack([part, other])
            pair_far = dp(pair, 2)
            pieces = [pair[0], pair[1], pair_far[0], pair_far[1]]
        else:
            other = dp(part, 2)
            pair = jnp.stack([part, other])
            pair_far = dp(pair, 1)
            pieces = [pair[0], pair_far[0], pair[1], pair_far[1]]
        return pieces

    def both_cores(mine, pieces):
        near = jnp.concatenate([mine, jnp.stack(pieces)], axis=0)
        return near, mp(near, 1)

    partner = dp(own, half_axis)
    cross_own = jnp.concatenate([modal_in[0], modal_out[0][None]], axis=0)
    self_own = jnp.concatenate([modal_in[1], modal_out[1][None]], axis=0)
    up_own = turned(choose(ffn_in).reshape(PIECES, -1, width))
    down_own = turned(choose(ffn_out).reshape(PIECES, -1, width))
    bias_own = turned(choose(ffn_bias).reshape(PIECES, -1))
    cross_near, cross_far = both_cores(cross_own, spread(cross_own, "yz"))
    partner_left = to_next(partner[rows - HALO :])
    partner_right = to_previous(partner[:HALO])
    self_near, self_far = both_cores(self_own, spread(self_own, "zy"))

    def spread_turned(mine, rel_order):
        part = mp(mine[0], 2)
        if rel_order == "yz":
            pair = jnp.stack([part, dp(part, 1)])
            pair_far = dp(pair, 2)
            pieces = [pair[0], pair[1], pair_far[0], pair_far[1]]
        else:
            pair = jnp.stack([part, dp(part, 2)])
            pair_far = dp(pair, 1)
            pieces = [pair[0], pair_far[0], pair[1], pair_far[1]]
        return pieces

    up_near, up_far = both_cores(up_own, spread_turned(up_own, "yz"))
    down_near, down_far = both_cores(down_own, spread_turned(down_own, "zy"))
    bias_near = jnp.concatenate([bias_own, mp(bias_own, 2)], axis=0)
    up_bias = jnp.concatenate([bias_near, mp(bias_near, 1)], axis=0).reshape(1, -1)

    rows_f = struct((rows, width), F32)
    rows_b = struct((rows, width), BF)
    keys_b = struct((keys, width), BF)
    row_f = struct((1, width), F32)
    column_f = struct((rows, 1), F32)
    halo_b = struct((HALO, width), BF)
    attn_flops = 2 * width * width * (2 * rows + 2 * keys)

    def attend(query_in, left, mine, right, near, far, resid, layer):
        return call(
            attention_forward,
            [rows_b, keys_b, keys_b, rows_b, struct((rows, 2 * DH), F32), rows_f, column_f, rows_f, rows_b],
            [pltpu.VMEM((keys, width), BF), pltpu.VMEM((width, width), BF)],
            attn_flops * 2, 12 << 20, "attend",
        )(info, query_in, left, mine, right, near, far, resid, gains[layer], shifts[layer])

    cross_q, cross_k, cross_v, cross_o, cross_log, norm_1, inv_1, full_1, low_1 = attend(
        own, partner_left, partner, partner_right, cross_near, cross_far, own, 0
    )
    left_1 = to_next(low_1[rows - HALO :])
    right_1 = to_previous(low_1[:HALO])
    self_q, self_k, self_v, self_o, self_log, norm_2, inv_2, full_2, low_2 = attend(
        low_1, left_1, low_1, right_1, self_near, self_far, full_1, 1
    )

    hidden = up_bias.shape[1]
    piece_rows = hidden // (4 * PIECES)
    steps = 8
    chunk = hidden // steps
    weight_near = pl.BlockSpec((2, piece_rows, width), lambda step: (jnp.minimum(step, steps // 2 - 1), 0, 0))
    weight_far = pl.BlockSpec((2, piece_rows, width), lambda step: (jnp.maximum(step - steps // 2, 0), 0, 0))
    chunk_spec = pl.BlockSpec((rows, chunk), lambda step: (0, step))
    bias_spec = pl.BlockSpec((1, chunk), lambda step: (0, step))

    def whole(shape):
        return pl.BlockSpec(shape, lambda step: (0,) * len(shape))

    full_spec, line_spec, col_spec = whole((rows, width)), whole((1, width)), whole((rows, 1))
    act, slope, norm_3, inv_3, low_3 = pl.pallas_call(
        ffn_forward,
        grid=(steps,),
        out_shape=[struct((rows, hidden), BF), struct((rows, hidden), F32), rows_f, column_f, rows_b],
        in_specs=[full_spec, full_spec, weight_near, weight_far, weight_near, weight_far, bias_spec, line_spec, line_spec, line_spec],
        out_specs=[chunk_spec, chunk_spec, full_spec, col_spec, full_spec],
        scratch_shapes=[pltpu.VMEM((rows, width), F32)],
        compiler_params=pltpu.CompilerParams(vmem_limit_bytes=VMEM_LIMIT),
        cost_estimate=pl.CostEstimate(flops=4 * rows * hidden * width, bytes_accessed=18 << 20, transcendentals=0),
        name="feed_forward",
    )(low_2, full_2, up_near, up_far, down_near, down_far, up_bias, choose(out_bias)[None], gains[2], shifts[2])

    regrouped = lax.all_to_all(low_3[None], "dp", split_axis=1, concat_axis=0, tiled=True)
    slice_rows = regrouped.shape[1]
    gate_rows = half_axis * slice_rows
    all_ends = jnp.cumsum(page_lengths, axis=1)
    used_rows = jnp.max(jnp.where(all_ends <= L, all_ends, 0), axis=1)
    position = place * rows + data_index * slice_rows + jnp.arange(slice_rows, dtype=jnp.int32)
    valid = (position[None, :] < used_rows[:, None]).astype(F32).reshape(gate_rows, 1)
    gate_shape = struct((gate_rows, width), BF)
    gate_piece = 2 * width // (4 * PIECES)
    gate_half = struct((2 * PIECES, gate_piece, width), BF)
    united, text_cot, vision_cot, gate_near, gate_far, gate_bias_part = call(
        gate_kernel,
        [struct((gate_rows, width), F32), gate_shape, gate_shape, gate_half, gate_half, row_f],
        [pltpu.VMEM((2 * width, width), F32)],
        12 * gate_rows * width * width, 8 << 20, "gate",
    )(
        info, regrouped[:half_axis].reshape(gate_rows, width), regrouped[half_axis:].reshape(gate_rows, width),
        gate_weight, gate_bias[None], valid, united_grad[:, 0].reshape(gate_rows, width),
    )
    returned = lax.all_to_all(
        jnp.concatenate([text_cot, vision_cot], axis=0).reshape(devices, slice_rows, width),
        "dp", split_axis=0, concat_axis=1, tiled=True,
    )
    out_cot = returned[0]

    def add(left, right):
        return (left.astype(F32) + right.astype(F32)).astype(BF)

    def fold(near, far):
        near = add(near, mp(far, 1))
        return add(near[:PIECES], mp(near[PIECES:], 2))

    def scatter_sum(parts, order):
        if order == "yz":
            got = dp(jnp.stack([parts[1], parts[3]]), 1)
            keep, send = add(parts[0], got[0]), add(parts[2], got[1])
            piece = add(keep, dp(send, 2))
        else:
            got = dp(parts[2:], 2)
            keep, send = add(parts[0], got[0]), add(parts[1], got[1])
            piece = add(keep, dp(send, 1))
        for bit in range(2, group_bits):
            piece = add(piece, dp(piece, 1 << bit))
        return piece

    def gather(piece, order):
        if order == "zy":
            pair = jnp.stack([piece, dp(piece, 2)])
            return pair, dp(pair, 1), ((0, 2), (1, 3))
        pair = jnp.stack([piece, dp(piece, 1)])
        return pair, dp(pair, 2), ((0, 1), (2, 3))

    up_specs_out = [
        weight_near, weight_far, weight_near, weight_far,
    ]
    half_b = struct((2 * PIECES, piece_rows, width), BF)
    cot_2, up_g_near, up_g_far, down_g_near, down_g_far, up_bias_part, down_bias_part, gain_3, shift_3 = pl.pallas_call(
        ffn_backward,
        grid=(steps,),
        out_shape=[rows_f, half_b, half_b, half_b, half_b, struct((1, hidden), F32), row_f, row_f, row_f],
        in_specs=[full_spec, full_spec, col_spec, line_spec, full_spec, chunk_spec, chunk_spec, weight_near, weight_far, weight_near, weight_far],
        out_specs=[full_spec] + up_specs_out + [bias_spec, line_spec, line_spec, line_spec],
        scratch_shapes=[pltpu.VMEM((rows, width), BF)],
        compiler_params=pltpu.CompilerParams(vmem_limit_bytes=VMEM_LIMIT),
        cost_estimate=pl.CostEstimate(flops=8 * rows * hidden * width, bytes_accessed=28 << 20, transcendentals=0),
        name="feed_forward_back",
    )(out_cot, norm_3, inv_3, gains[2], low_2, act, slope, up_near, up_far, down_near, down_far)

    attn_half = struct((2 * PIECES, shard, width), BF)

    def attend_back(same_input, cot_in, from_left, from_right, normed, inverse, layer, saved, query_in, left, mine, right, near, far):
        return call(
            functools.partial(attention_backward, same_input),
            [rows_f, rows_f, halo_b, halo_b, attn_half, attn_half, row_f, row_f],
            [
                pltpu.VMEM((keys, width), BF), pltpu.VMEM((width, width), BF), pltpu.VMEM((rows, width), BF),
                pltpu.VMEM((rows, width), BF), pltpu.VMEM((rows, width), BF), pltpu.VMEM((keys, width), F32),
                pltpu.VMEM((keys, width), F32), pltpu.VMEM((keys, width), BF), pltpu.VMEM((keys, width), BF),
            ],
            attn_flops * 4, 20 << 20, "attend_back",
        )(info, cot_in, from_left, from_right, normed, inverse, gains[layer], *saved, query_in, left, mine, right, near, far)

    none = jnp.zeros((HALO, width), BF)
    cot_1, _, self_to_left, self_to_right, self_g_near, self_g_far, gain_2, shift_2 = attend_back(
        True, cot_2, none, none, norm_2, inv_2, 1, (self_q, self_k, self_v, self_o, self_log),
        low_1, left_1, low_1, right_1, self_near, self_far,
    )
    self_from_right = to_previous(self_to_left)
    self_from_left = to_next(self_to_right)
    own_cot, partner_cot, cross_to_left, cross_to_right, cross_g_near, cross_g_far, gain_1, shift_1 = attend_back(
        False, cot_1, self_from_left, self_from_right, norm_1, inv_1, 0, (cross_q, cross_k, cross_v, cross_o, cross_log),
        own, partner_left, partner, partner_right, cross_near, cross_far,
    )
    cross_from_right = to_previous(cross_to_left)
    cross_from_left = to_next(cross_to_right)
    partner_cot = (partner_cot + jnp.concatenate([cross_from_left, cross_from_right], axis=0).astype(F32)).astype(BF)
    stream_grad = (own_cot + dp(partner_cot, half_axis).astype(F32))[None]

    down_parts = fold(down_g_near, down_g_far)
    gate_parts = fold(gate_near, gate_far)
    first_piece = scatter_sum(jnp.concatenate([down_parts, gate_parts], axis=1), "yz")
    first_other = dp(first_piece, half_axis)
    down_first, down_second, down_order = gather(
        jnp.concatenate([first_piece[:piece_rows], first_other[:piece_rows], add(first_piece[piece_rows:], first_other[piece_rows:])], axis=0), "zy"
    )
    up_piece = scatter_sum(fold(up_g_near, up_g_far), "zy")
    up_first, up_second, up_order = gather(jnp.concatenate([up_piece, dp(up_piece, half_axis)], axis=0), "zy")
    self_piece = scatter_sum(fold(self_g_near, self_g_far), "zy")
    self_first, self_second, self_order = gather(jnp.concatenate([self_piece, dp(self_piece, half_axis)], axis=0), "yz")
    cross_piece = scatter_sum(fold(cross_g_near, cross_g_far), "yz")
    cross_first, cross_second, cross_order = gather(jnp.concatenate([cross_piece, dp(cross_piece, half_axis)], axis=0), "zy")

    gate_pieces = [None] * PIECES
    for source, names in ((down_first, down_order[0]), (down_second, down_order[1])):
        for index, name in enumerate(names):
            gate_pieces[name] = source[index, 2 * piece_rows :]
    gate_pieces = jnp.stack(gate_pieces)
    gate_pieces = jnp.concatenate([gate_pieces, mp(gate_pieces, 2)], axis=0)
    gate_pieces = jnp.concatenate([gate_pieces, mp(gate_pieces, 1)], axis=0)

    def gate_target(step, info_ref):
        spot = step // PIECES
        shift_by = jnp.where(spot == 1, 2, jnp.where(spot == 2, 1, spot))
        return ((info_ref[PAGES + 2] ^ shift_by) * PIECES + ((step % PIECES) ^ info_ref[PAGES + 1]), 0, 0)

    gate_weight_grad = pl.pallas_call(
        place_gate,
        grid_spec=pltpu.PrefetchScalarGridSpec(
            num_scalar_prefetch=1,
            grid=(4 * PIECES,),
            in_specs=[pl.BlockSpec((1, gate_piece, width), lambda step, info_ref: (step, 0, 0))],
            out_specs=pl.BlockSpec((1, gate_piece, width), gate_target),
        ),
        out_shape=struct((4 * PIECES, gate_piece, width), F32),
        name="place_gate",
    )(info, gate_pieces).reshape(2, width, width)

    wide = [pltpu.VMEM((8, piece_rows, width), F32), pltpu.SemaphoreType.DMA((8,))]

    def split(parts):
        return parts[:, : 2 * piece_rows].reshape(2, 2, piece_rows, width)

    def place_hidden(first, second, order):
        return call(
            functools.partial(place_ffn, order), struct((2, PIECES, piece_rows, width), F32), wide,
            0, 12 << 20, "place_hidden", [SM, VM, VM], ANY,
        )(info, split(first), split(second)).reshape(2, PIECES * piece_rows, width)

    ffn_out_grad = place_hidden(down_first, down_second, down_order)
    ffn_in_grad = place_hidden(up_first, up_second, up_order)
    attn_shapes = [struct((2, 2, 3, shard, width), F32), struct((2, 2, shard, width), F32)]
    placed = call(
        functools.partial(place_attention, self_order, 1), attn_shapes, wide, 0, 12 << 20, "place_self", [SM, VM, VM], [ANY, ANY],
    )(info, split(self_first), split(self_second))
    attn_in_grad, attn_out_grad = call(
        functools.partial(place_attention, cross_order, 0), attn_shapes, wide, 0, 12 << 20, "place_cross",
        [SM, VM, VM, ANY, ANY], [ANY, ANY], {3: 0, 4: 1},
    )(info, split(cross_first), split(cross_second), *placed)

    small = jnp.concatenate([gain_1, gain_2, gain_3, shift_1, shift_2, shift_3, down_bias_part, gate_bias_part], axis=0)
    bias_parts = up_bias_part.reshape(4, -1)
    got = mp(jnp.concatenate([bias_parts[2:], small], axis=0), 1)
    small = jnp.concatenate([bias_parts[:2] + got[:2], small + got[2:]], axis=0)
    got = mp(small[1:], 2)
    bias_row = turned((small[0] + got[0]).reshape(PIECES, -1)).reshape(1, width)
    small = jnp.concatenate([bias_row, small[2:] + got[1:]], axis=0)
    for bit in range(group_bits):
        small = small + dp(small, 1 << bit)
    others = dp(small, half_axis)
    is_text = modality == 0
    both = jnp.stack([jnp.where(is_text, small, others), jnp.where(is_text, others, small)])
    return (
        united.reshape(half_axis, 1, slice_rows, width),
        stream_grad,
        attn_in_grad,
        attn_out_grad,
        ffn_in_grad,
        both[:, 0],
        ffn_out_grad,
        both[:, 7],
        both[:, 1:4],
        both[:, 4:7],
        gate_weight_grad,
        small[8] + others[8],
    )


def solution(mesh):
    placed = (
        P("dp", "mp", None),
        P(),
        P(None, None, None, "mp", None),
        P(None, None, "mp", None),
        P(None, "mp", None),
        P(None, "mp"),
        P(None, "mp", None),
        P(),
        P(),
        P(),
        P(),
        P(),
        P(None, "mp", "dp", None),
    )
    return jax.shard_map(
        body,
        mesh=mesh,
        in_specs=placed,
        out_specs=(
            P(None, "mp", "dp", None),
            P("dp", "mp", None),
            P(None, None, None, "mp", None),
            P(None, None, "mp", None),
            P(None, "mp", None),
            P(None, "mp"),
            P(None, "mp", None),
            P(),
            P(),
            P(),
            P(),
            P(),
        ),
        check_vma=False,
    )
```

```python
import functools

import jax
import jax.numpy as jnp
from jax import lax
from jax.experimental import pallas as pl
from jax.experimental.pallas import tpu as pltpu
from jax.sharding import PartitionSpec as P

DH = 64
L = 1024
PAGES = 16
EPS = 1e-05
SCALE = 0.125
LOG2E = 1.4426950408889634
MASKED = -1e30
HALO = 128
PIECES = 4
BF = jnp.bfloat16
F32 = jnp.float32
VMEM_LIMIT = 16 * 1024 * 1024

VM = pl.BlockSpec(memory_space=pltpu.VMEM)
SM = pl.BlockSpec(memory_space=pltpu.SMEM)
HBM = pl.BlockSpec(memory_space=pltpu.HBM)


def nn(a, b):
    return lax.dot_general(a, b, (((1,), (0,)), ((), ())), preferred_element_type=F32)


def nt(a, b):
    return lax.dot_general(a, b, (((1,), (1,)), ((), ())), preferred_element_type=F32)


def tn(a, b):
    return lax.dot_general(a, b, (((0,), (0,)), ((), ())), preferred_element_type=F32)


def call(body, outs, scratch=(), flops=0, traffic=0, name=None, specs=None, out_specs=None, aliases=None):
    def run(*args):
        return pl.pallas_call(
            body,
            out_shape=outs,
            in_specs=specs if specs is not None else [SM] + [VM] * (len(args) - 1),
            out_specs=out_specs if out_specs is not None else jax.tree.map(lambda _: VM, outs),
            scratch_shapes=list(scratch),
            input_output_aliases=aliases or {},
            compiler_params=pltpu.CompilerParams(vmem_limit_bytes=VMEM_LIMIT),
            cost_estimate=pl.CostEstimate(flops=flops, bytes_accessed=traffic, transcendentals=0),
            name=name,
        )(*args)

    return run


def struct(shape, dtype):
    return jax.ShapeDtypeStruct(shape, dtype)


def after(value, *deps):
    return lax.optimization_barrier((value,) + deps)[0]


class Where:
    def __init__(self, scal, half_axis):
        self.modality = scal[0] // half_axis
        self.sequence = scal[0] % half_axis
        self.turn = scal[0] % PIECES
        self.place = scal[1]


def page_ends(pages, sequence):
    ends = []
    used = jnp.int32(0)
    running = jnp.int32(0)
    for page in range(PAGES):
        running = running + pages[sequence, page]
        fits = running <= L
        ends.append(jnp.where(fits, running, 2 * L))
        used = jnp.where(fits, running, used)
    return ends, used


def segment_of(position, ends):
    segment = jnp.zeros_like(position)
    for end in ends:
        segment = segment + (end <= position).astype(jnp.int32)
    return segment


def block_bias(ends, base, block, keys):
    query = base + block * HALO + lax.broadcasted_iota(jnp.int32, (HALO, 1), 0)
    key = base + (block - 1) * HALO + lax.broadcasted_iota(jnp.int32, (1, keys), 1)
    query_seg = segment_of(query, ends)
    key_seg = segment_of(key, ends)
    key_seg = jnp.where((key >= 0) & (key < L), key_seg, -1)
    return jnp.where(query_seg == key_seg, 0.0, MASKED)


def normalise(residual, gain, shift):
    center = residual - jnp.mean(residual, axis=-1, keepdims=True)
    inverse = lax.rsqrt(jnp.mean(center * center, axis=-1, keepdims=True) + EPS)
    normed = center * inverse
    return normed * gain + shift, normed, inverse


def norm_back(cot, gain, normed, inverse):
    grad = cot * gain
    back = inverse * (
        grad
        - jnp.mean(grad, axis=-1, keepdims=True)
        - normed * jnp.mean(grad * normed, axis=-1, keepdims=True)
    )
    return back, jnp.sum(cot * normed, axis=0, keepdims=True), jnp.sum(cot, axis=0, keepdims=True)


def fetch_attention(layer, turn, mine, far, near_pieces, far_pieces, matrices, sems):
    rows = mine.shape[2]

    def spot(which, place):
        return matrices.at[which, pl.ds(place * rows, rows), :]

    for relative in range(PIECES):
        which = relative ^ turn
        pltpu.make_async_copy(near_pieces[relative], spot(which, 1), sems.at[which]).start()
        pltpu.make_async_copy(far_pieces.at[relative], spot(which, 3), sems.at[which]).start()
    for which in range(4):
        for place, source in ((0, mine), (2, far)):
            pltpu.make_async_copy(source.at[layer, which], spot(which, place), sems.at[which]).start()

    def wait(which):
        pltpu.make_async_copy(matrices.at[which], matrices.at[which], sems.at[which]).wait()

    return wait


def stack_heads(pair, first):
    zero = jnp.zeros_like(pair)
    return jnp.concatenate([jnp.where(first, pair, zero), jnp.where(first, zero, pair)], axis=0)


def extend(left, own, right, extended):
    rows = own.shape[0]
    extended[0:HALO, :] = left[...]
    extended[HALO : HALO + rows, :] = own[...]
    extended[HALO + rows : 2 * HALO + rows, :] = right[...]


def attention_forward(half_axis, layer, *refs):
    scal, pages, query_in, left, own, right, resid, params = refs[:8]
    mine, far, near_pieces, far_pieces = refs[8], refs[9], refs[10:14], refs[14]
    q_out, k_out, v_out, o_out, log_out, norm_out, inv_out, full_out, low_out = refs[15:24]
    extended, matrices, sems = refs[24:]
    where = Where(scal, half_axis)
    rows, width = query_in.shape
    window = 3 * HALO
    wait = fetch_attention(layer, where.turn, mine, far, near_pieces, far_pieces, matrices, sems)
    extend(left, own, right, extended)
    ends, _ = page_ends(pages, where.sequence)
    base = where.place * rows
    wait(0)
    q_out[...] = nt(query_in[...], matrices[0]).astype(BF)
    wait(1)
    k_out[...] = nt(extended[...], matrices[1]).astype(BF)
    wait(2)
    v_out[...] = nt(extended[...], matrices[2]).astype(BF)
    lane = lax.broadcasted_iota(jnp.int32, (1, 2 * DH), 1)
    first = lane < DH
    for block in range(rows // HALO):
        bias = block_bias(ends, base, block, window)
        bias = jnp.concatenate([bias, bias], axis=0)
        row = slice(block * HALO, (block + 1) * HALO)
        span = slice(block * HALO, block * HALO + window)
        logs = jnp.zeros((HALO, 2 * DH), F32)
        for pair in range(width // (2 * DH)):
            cols = slice(pair * 2 * DH, (pair + 1) * 2 * DH)
            scores = nt(stack_heads(q_out[row, cols], first), k_out[span, cols])
            scores = scores * (SCALE * LOG2E) + bias
            top = jnp.max(scores, axis=-1, keepdims=True)
            expo = jnp.exp2(scores - top)
            total = jnp.sum(expo, axis=-1, keepdims=True)
            mixed = nn(expo.astype(BF), v_out[span, cols]) / total
            log = top + jnp.log2(total)
            logs = jnp.where(lane == 2 * pair, log[:HALO], jnp.where(lane == 2 * pair + 1, log[HALO:], logs))
            o_out[row, cols] = jnp.where(first, mixed[:HALO], mixed[HALO:]).astype(BF)
        log_out[row, :] = logs
    wait(3)
    residual = resid[...].astype(F32) + nn(o_out[...], matrices[3])
    full, normed, inverse = normalise(residual, params[layer : layer + 1, :], params[3 + layer : 4 + layer, :])
    norm_out[...] = normed
    inv_out[...] = inverse
    full_out[...] = full
    low_out[...] = full.astype(BF)


def attention_backward(half_axis, layer, same_input, *refs):
    scal, pages, cot_in, normed, inverse, params = refs[:6]
    q_in, k_in, v_in, log_in = refs[6:10]
    refs = refs[10:]
    halos = ()
    if not same_input:
        halos, refs = refs[:2], refs[2:]
    mine, far, near_pieces, far_pieces = refs[0], refs[1], refs[2:6], refs[6]
    refs = refs[7:]
    query_cot, to_left, to_right, gain_out, shift_out, low, dq, dkl, dvl = refs[:9]
    refs = refs[9:]
    if not same_input:
        key_cot, refs = refs[0], refs[1:]
    matrices, o_cot, dk, dv, sems = refs
    where = Where(scal, half_axis)
    rows, width = cot_in.shape
    keys = rows + 2 * HALO
    window = 3 * HALO
    wait = fetch_attention(layer, where.turn, mine, far, near_pieces, far_pieces, matrices, sems)
    cot = cot_in[...]
    if halos:
        cot = cot + jnp.concatenate([halos[0][...], halos[1][...]], axis=0).astype(F32)
    back, gain_grad, shift_grad = norm_back(cot, params[layer : layer + 1, :], normed[...], inverse[...])
    gain_out[...] = gain_grad
    shift_out[...] = shift_grad
    query_cot[...] = back
    low[...] = back.astype(BF)
    wait(3)
    o_cot[...] = nt(low[...], matrices[3]).astype(BF)
    ends, _ = page_ends(pages, where.sequence)
    base = where.place * rows
    lane = lax.broadcasted_iota(jnp.int32, (1, 2 * DH), 1)
    first = lane < DH
    dk[...] = jnp.zeros_like(dk)
    dv[...] = jnp.zeros_like(dv)
    for block in range(rows // HALO):
        bias = block_bias(ends, base, block, window)
        bias = jnp.concatenate([bias, bias], axis=0)
        row = slice(block * HALO, (block + 1) * HALO)
        span = slice(block * HALO, block * HALO + window)
        logs = log_in[row, :]
        for pair in range(width // (2 * DH)):
            cols = slice(pair * 2 * DH, (pair + 1) * 2 * DH)
            queries = stack_heads(q_in[row, cols], first)
            cots = stack_heads(o_cot[row, cols], first)
            key_pair = k_in[span, cols]
            log = jnp.concatenate([logs[:, 2 * pair : 2 * pair + 1], logs[:, 2 * pair + 1 : 2 * pair + 2]], axis=0)
            weights = jnp.exp2(nt(queries, key_pair) * (SCALE * LOG2E) + bias - log)
            weight_cot = nt(cots, v_in[span, cols])
            inner = jnp.sum(weights * weight_cot, axis=-1, keepdims=True)
            score_cot = (weights * (weight_cot - inner)).astype(BF)
            grads = nn(score_cot, key_pair)
            dq[row, cols] = (jnp.where(first, grads[:HALO], grads[HALO:]) * SCALE).astype(BF)
            dk[span, cols] += tn(score_cot, queries)
            dv[span, cols] += tn(weights.astype(BF), cots)
    dkl[...] = (dk[...] * SCALE).astype(BF)
    dvl[...] = dv[...].astype(BF)
    wait(1)
    wait(2)
    back = nn(dkl[...], matrices[1]) + nn(dvl[...], matrices[2])
    to_left[...] = back[0:HALO, :].astype(BF)
    to_right[...] = back[HALO + rows : keys, :].astype(BF)
    middle = back[HALO : HALO + rows, :]
    wait(0)
    direct = nn(dq[...], matrices[0])
    if same_input:
        query_cot[...] += direct + middle
    else:
        query_cot[...] += direct
        key_cot[...] = middle


def attention_weights(half_axis, scal, o_in, low, dq, dk, dv, query_in, left, own, right, near_out, far_out, extended):
    turn = Where(scal, half_axis).turn
    extend(left, own, right, extended)
    piece = near_out.shape[1]
    jobs = ((0, dq, query_in), (1, dk, extended), (2, dv, extended), (3, o_in, low))
    for which, cots, inputs in jobs:
        value = tn(cots[...], inputs[...]).astype(BF)
        for place, (target, start) in enumerate(((near_out, 0), (near_out, PIECES), (far_out, 0), (far_out, PIECES))):
            target[start + (which ^ turn)] = value[place * piece : (place + 1) * piece]


def gelu_parts(value):
    root = 0.7978845608028654
    square = value * value
    inner = jnp.tanh(root * (value + 0.044715 * value * square))
    half = 0.5 * (1.0 + inner)
    slope = half + 0.5 * value * (1.0 - inner * inner) * (root * (1.0 + 3.0 * 0.044715 * square))
    return value * half, slope


def fetch_hidden(turn, refs, ups, downs, up_sems, down_sems, downs_first=False):
    mine, far, x, y, z, up_last, down_last, far_three, far_last = refs
    jobs = [(0, ups, up_sems, up_last), (1, downs, down_sems, down_last)]
    for place in range(4):
        for kind, buffer, sems, last in jobs[::-1] if downs_first else jobs:
            if place % 2 == 0:
                source = (mine, far)[place // 2]
                pltpu.make_async_copy(source.at[kind], buffer.at[place], sems.at[place]).start()
                continue
            if place == 1:
                pieces = (x.at[kind], y.at[kind], z.at[kind], last)
            else:
                pieces = tuple(far_three.at[index, kind] for index in range(3)) + (far_last.at[kind],)
            for relative, piece in enumerate(pieces):
                pltpu.make_async_copy(piece, buffer.at[place, relative ^ turn], sems.at[place]).start()

    def wait(buffer, sems, place):
        pltpu.make_async_copy(buffer.at[place], buffer.at[place], sems.at[place]).wait()

    return functools.partial(wait, ups, up_sems), functools.partial(wait, downs, down_sems)


def ffn_forward(half_axis, *refs):
    scal, low, full, bias_own, bias_x, bias_far, params = refs[:7]
    act_own, act_over, act_core, slope_out, norm_out, inv_out, keep_out, send_out = refs[16:24]
    ups, downs, up_sems, down_sems = refs[24:]
    where = Where(scal, half_axis)
    wait_up, wait_down = fetch_hidden(where.turn, refs[7:16], ups, downs, up_sems, down_sems)
    rows, width = low.shape
    total = full[...] + params[6:7, :]
    biases = (bias_own[...], bias_x[...], bias_far[0:1, :], bias_far[1:2, :])
    for place in range(4):
        cols = slice(place * width, (place + 1) * width)
        wait_up(place)
        pre = nt(low[...], ups[place].reshape(width, width)) + biases[place]
        value, slope = gelu_parts(pre)
        value = value.astype(BF)
        if place % 2 == 0:
            (act_own, act_core)[place // 2][...] = value
        else:
            act_over[place // 2] = value
        slope_out[:, cols] = slope
        wait_down(place)
        total = total + nn(value, downs[place].reshape(width, width))
    out, normed, inverse = normalise(total, params[2:3, :], params[5:6, :])
    norm_out[...] = normed
    inv_out[...] = inverse
    out = out.astype(BF)
    half = rows // 2
    is_text = where.modality == 0
    keep_out[...] = jnp.where(is_text, out[:half], out[half:])
    send_out[...] = jnp.where(is_text, out[half:], out[:half])


def last_norm_backward(half_axis, scal, keep, got, normed, inverse, params, back_out, branch_out, gain_out, shift_out, bias_out):
    where = Where(scal, half_axis)
    is_text = where.modality == 0
    kept, other = keep[...], got[...]
    cot = jnp.concatenate([jnp.where(is_text, kept, other), jnp.where(is_text, other, kept)], axis=0).astype(F32)
    back, gain_grad, shift_grad = norm_back(cot, params[2:3, :], normed[...], inverse[...])
    back_out[...] = back
    branch_out[...] = back.astype(BF)
    gain_out[...] = gain_grad
    shift_out[...] = shift_grad
    bias_out[...] = jnp.sum(back, axis=0, keepdims=True)


def ffn_backward(half_axis, *refs):
    scal, back, branch, slope = refs[:4]
    cot_out, pre_own, pre_over, pre_core, bias_out = refs[13:18]
    ups, downs, up_sems, down_sems = refs[18:]
    where = Where(scal, half_axis)
    wait_up, wait_down = fetch_hidden(where.turn, refs[4:13], ups, downs, up_sems, down_sems, True)
    rows, width = branch.shape
    total = back[...]
    for place in range(4):
        cols = slice(place * width, (place + 1) * width)
        wait_down(place)
        act_cot = nt(branch[...], downs[place].reshape(width, width))
        pre_cot = (act_cot * slope[:, cols]).astype(BF)
        if place % 2 == 0:
            (pre_own, pre_core)[place // 2][...] = pre_cot
        else:
            pre_over[place // 2] = pre_cot
        bias_out[:, cols] = jnp.sum(pre_cot.astype(F32), axis=0, keepdims=True)
        wait_up(place)
        total = total + nn(pre_cot, ups[place].reshape(width, width))
    cot_out[...] = total


def rows_product(half_axis, scal, left_own, left_over, left_core, left_relay, *refs):
    rights, out = refs[:4], refs[4]
    turn = Where(scal, half_axis).turn
    total = tn(left_own[...], rights[0][...])
    for left, right in ((left_over[0], rights[1]), (left_core[...], rights[2]), (left_relay[...], rights[3])):
        total = total + tn(left, right[...])
    total = total.astype(BF)
    rows = out.shape[1]
    for piece in range(PIECES):
        out[piece ^ turn] = total[piece * rows : (piece + 1) * rows]


def gate_kernel(
    half_axis, scal, pages, keep, got, weight, params, cot_in,
    united, keep_out, send_out, near_out, far_out, bias_out, grads,
):
    where = Where(scal, half_axis)
    is_text = where.modality == 0
    kept, other = keep[...], got[...]
    text_low = jnp.where(is_text, kept, other)
    vision_low = jnp.where(is_text, other, kept)
    half, width = kept.shape
    _, used = page_ends(pages, where.sequence)
    position = where.place * (2 * half) + where.modality * half + lax.broadcasted_iota(jnp.int32, (half, 1), 0)
    mask = (position < used).astype(F32)
    gate = jax.nn.sigmoid(nt(text_low, weight[0]) + nt(vision_low, weight[1]) + params[7:8, :])
    text_full = text_low.astype(F32)
    vision_full = vision_low.astype(F32)
    united[...] = (mask * (gate * text_full + (1.0 - gate) * vision_full)).astype(BF)
    cot = cot_in[...].astype(F32) * mask
    gate_cot = (cot * (text_full - vision_full) * gate * (1.0 - gate)).astype(BF)
    text_cot = (cot * gate + nn(gate_cot, weight[0])).astype(BF)
    vision_cot = (cot * (1.0 - gate) + nn(gate_cot, weight[1])).astype(BF)
    keep_out[...] = jnp.where(is_text, text_cot, vision_cot)
    send_out[...] = jnp.where(is_text, vision_cot, text_cot)
    bias_out[...] = jnp.sum(gate_cot.astype(F32), axis=0, keepdims=True)
    grads[0:width, :] = tn(gate_cot, text_low)
    grads[width : 2 * width, :] = tn(gate_cot, vision_low)
    rows = near_out.shape[1]
    for spot, (target, start) in enumerate(((near_out, 0), (near_out, PIECES), (far_out, 0), (far_out, PIECES))):
        shard = where.place ^ (0, 2, 1, 3)[spot]
        for piece in range(PIECES):
            at = pl.multiple_of((shard * PIECES + (piece ^ where.turn)) * rows, rows)
            target[start + piece] = grads[pl.ds(at, rows), :].astype(BF)


def place_gate(half_axis, start, scal, *refs):
    near, over, far, out, wide, sems = refs[:4], *refs[4:]
    where = Where(scal, half_axis)
    rows = over.shape[1]
    copies = []
    for spot in range(4):
        shard = where.place ^ (0, 2, 1, 3)[spot]
        for piece in range(PIECES):
            if spot == 0:
                source = near[piece][start : start + rows, :]
            else:
                source = (over[piece], far[piece], far[PIECES + piece])[spot - 1]
            slot = spot * PIECES + piece
            wide[slot] = source.astype(F32)
            copy = pltpu.make_async_copy(wide.at[slot], out.at[shard * PIECES + (piece ^ where.turn)], sems.at[slot])
            copy.start()
            copies.append(copy)
    for copy in copies:
        copy.wait()


def place_pieces(half_axis, layer, scal, *refs):
    wide, sems = refs[-2:]
    where = Where(scal, half_axis)
    sources, outs = refs[:4], refs[-3:-2] if layer is None else refs[-4:-2]
    rows = wide.shape[1]
    for relative, source in enumerate(sources):
        piece = relative ^ where.turn
        for kind in range(2):
            slot = relative * 2 + kind
            target = kind ^ where.modality
            wide[slot] = source[kind * rows : (kind + 1) * rows, :].astype(F32)

            def send(place, slot=slot):
                pltpu.make_async_copy(wide.at[slot], place, sems.at[slot]).start()

            if layer is None:
                send(outs[0].at[target, piece])
            else:
                pl.when(piece < 3)(lambda: send(outs[0].at[target, layer, piece]))
                pl.when(piece == 3)(lambda: send(outs[1].at[target, layer]))
    for slot in range(8):
        landing = outs[0].at[0, 0] if layer is None else outs[1].at[0, layer]
        pltpu.make_async_copy(wide.at[slot], landing, sems.at[slot]).wait()


def pack_small(scal, bias, *refs):
    out = refs[-1]
    width = out.shape[1]
    out[...] = jnp.zeros_like(out)
    for shard in range(4):
        out[shard : shard + 1, :] = bias[:, shard * width : (shard + 1) * width]
    for row, ref in enumerate(refs[:-1]):
        out[4 + row : 5 + row, :] = ref[...]


def add_small(scal, mine, got, out):
    out[...] = jnp.zeros_like(out)
    out[0:2, :] = mine[0:2, :] + got[2:4, :]
    out[4:12, :] = mine[4:12, :] + got[4:12, :]


def spread_small(scal, parts, mine, got, out):
    rows = parts.shape[1]
    total = mine[4:12, :] + got[4:12, :]
    bias = mine[0:1, :] + got[1:2, :]
    small = jnp.concatenate([total, bias, jnp.zeros((7, total.shape[1]), F32)], axis=0).astype(BF)
    for piece in range(PIECES):
        out[piece, 0:rows, :] = parts[piece]
        out[piece, rows : rows + 16, :] = small


ORDER = (
    "branch_x", "ffn_back", "pre_x", "branch_core", "pre_core", "self_back", "branch_relay", "gate_over",
    "self_weights", "self_core", "self_halo", "down_weights", "pre_relay", "down_first", "self_over",
    "up_weights", "up_first", "cross_back", "cross_weights", "small_core", "cross_core", "down_second",
    "small_over", "up_second", "cross_over", "down_third", "self_first", "up_third", "down_fourth", "self_second",
    "cross_first", "up_fourth", "cross_second", "self_third", "cross_halo", "up_fifth", "cross_third",
    "self_fourth", "partner", "cross_fourth", "self_fifth", "up_place", "down_fifth", "gate_x", "cross_fifth",
    "gate_core", "partner_end", "self_place", "gate_place", "cross_place", "down_place",
)


def body(
    streams, page_lengths, attn_in, attn_out, ffn_in, ffn_bias, ffn_out, out_bias,
    norm_gain, norm_bias, gate_weight, gate_bias, united_grad,
):
    devices = lax.axis_size("dp")
    half_axis = devices // 2
    group_bits = half_axis.bit_length() - 1
    data_index = lax.axis_index("dp")
    place = lax.axis_index("mp")
    modality = data_index // half_axis
    sequence = data_index % half_axis
    turn = data_index % PIECES
    own = streams[0]
    rows, width = own.shape
    keys = rows + 2 * HALO
    shard = attn_in.shape[3]

    def swap(value, axis, mask):
        pairs = [(source, source ^ mask) for source in range(lax.axis_size(axis))]
        return lax.ppermute(value, axis, pairs)

    def mp(value, mask):
        return swap(value, "mp", mask)

    def dp(value, mask):
        return swap(value, "dp", mask)

    count = lax.axis_size("mp")

    def to_next(value):
        return lax.ppermute(value, "mp", [(index, index + 1) for index in range(count - 1)])

    def to_previous(value):
        return lax.ppermute(value, "mp", [(index + 1, index) for index in range(count - 1)])

    def pick(stacked, index):
        return lax.dynamic_index_in_dim(stacked, index, 0, keepdims=False)

    scal = jnp.stack([data_index, place]).astype(jnp.int32)
    clock = [scal]

    def event(*values):
        fenced = lax.optimization_barrier(values + (clock[0],))[:-1]
        return fenced if len(fenced) > 1 else fenced[0]

    def mark(value):
        clock[0] = value
        return value

    def kernel(run, *args, due=()):
        now = after(scal, clock[0], *due)
        results = run(now, *args)
        mark(results[-1] if isinstance(results, (list, tuple)) else results)
        return results

    def add(left, right):
        return (left.astype(F32) + right.astype(F32)).astype(BF)

    piece_rows = ffn_in.shape[1] // PIECES
    half_rows = rows // 2
    slice_rows = united_grad.shape[2]

    def attention_piece(layer, index):
        inner = lax.dynamic_slice(
            attn_in, (index, layer, jnp.minimum(turn, 2), 0, 0), (1, 1, 1, shard, width)
        ).reshape(shard, width)
        outer = lax.dynamic_slice(attn_out, (index, layer, 0, 0), (1, 1, shard, width)).reshape(shard, width)
        return jnp.where(turn < 3, inner, outer)

    def group_exchange(blocks):
        moved = jnp.stack([pick(blocks, index ^ sequence) for index in range(half_axis)])
        shape = moved.shape
        for bit in range(group_bits):
            view = moved.reshape((half_axis >> (bit + 1), 2, 1 << bit) + shape[1:])
            got = dp(view[:, 1], 1 << bit)
            moved = jnp.stack([view[:, 0], got], axis=1).reshape(shape)
        return jnp.stack([pick(moved, index ^ sequence) for index in range(half_axis)])

    cross_x = mp(mark(attention_piece(0, modality)), 2)
    partner = dp(own, half_axis)
    self_x = mp(mark(attention_piece(1, event(modality))), 2)
    index = event(modality)
    hidden_part = jnp.stack([
        lax.dynamic_slice(weight, (index, turn * piece_rows, 0), (1, piece_rows, width))[0] for weight in (ffn_in, ffn_out)
    ])
    cross_x, hidden_part = event(cross_x, hidden_part)
    hidden_x = mp(mark(hidden_part), 2)
    cross_y, cross_z = dp(cross_x, 1), dp(cross_x, 2)
    index = event(modality)
    mine = mark(jnp.concatenate([pick(attn_in, index), pick(attn_out, index)[:, None]], axis=1))
    far = mp(mine, 1)
    cross_y = mark(event(cross_y))
    cross_yz = dp(cross_y, 2)
    partner = event(partner)
    partner_left = to_next(partner[rows - HALO :])
    partner_right = to_previous(mark(partner[:HALO]))
    self_x = mark(event(self_x))
    self_y, self_z = dp(self_x, 1), dp(self_x, 2)
    cross_z, cross_yz = event(cross_z, cross_yz)
    cross_far = mp(mark(jnp.stack([cross_x, cross_y, cross_z, cross_yz])), 1)
    index = event(modality)
    hidden_mine = mark(jnp.stack([pick(ffn_in, index), pick(ffn_out, index)]).reshape(2, PIECES, piece_rows, width))
    bias_own = lax.dynamic_slice(ffn_bias, (index, 0), (1, width))
    params = jnp.concatenate(
        [pick(norm_gain, index), pick(norm_bias, index), pick(out_bias, index)[None], gate_bias[None]], axis=0
    )
    hidden_x, self_y, self_z = event(hidden_x, self_y, self_z)
    hidden_y, hidden_z = dp(mark(hidden_x), 1), dp(hidden_x, 2)
    self_yz = dp(self_z, 1)
    hidden_far_mine = mp(hidden_mine, 1)
    cross_near = (cross_x, cross_y, cross_z, cross_yz)

    rows_f = struct((rows, width), F32)
    rows_b = struct((rows, width), BF)
    keys_b = struct((keys, width), BF)
    row_f = struct((1, width), F32)
    column_f = struct((rows, 1), F32)
    halo_b = struct((HALO, width), BF)
    half_b = struct((half_rows, width), BF)
    attn_flops = 2 * width * width * (2 * rows + 2 * keys)
    matrix_scratch = [pltpu.VMEM((4, width, width), BF), pltpu.SemaphoreType.DMA((4,))]

    def attend(now, query_in, left, own_rows, right, resid, layer, near, far_pieces):
        return call(
            functools.partial(attention_forward, half_axis, layer),
            [rows_b, keys_b, keys_b, rows_b, struct((rows, 2 * DH), F32), rows_f, column_f, rows_f, rows_b],
            [pltpu.VMEM((keys, width), BF)] + matrix_scratch,
            attn_flops, 12 << 20, "attend", [SM, SM] + [VM] * 6 + [HBM] * 7,
        )(now, page_lengths, query_in, left, own_rows, right, resid, params, mine, far, *near, far_pieces)

    cross_q, cross_k, cross_v, cross_o, cross_log, norm_1, inv_1, full_1, low_1 = kernel(
        attend, own, partner_left, partner, partner_right, own, 0, cross_near, cross_far
    )
    left_1 = to_next(low_1[rows - HALO :])
    right_1 = to_previous(low_1[:HALO])
    self_yz = event(self_yz)
    self_near = (self_x, self_y, self_z, self_yz)
    self_far = mp(mark(jnp.stack(self_near)), 1)
    hidden_y, hidden_z = event(hidden_y, hidden_z)
    up_yz = dp(hidden_y[0], 2)
    down_yz = dp(mark(hidden_z[1]), 1)
    hidden_three = mark(jnp.stack([hidden_x, hidden_y, hidden_z]))
    hidden_far_three = mp(hidden_three, 1)
    bias_x = mp(event(bias_own), 2)
    self_q, self_k, self_v, self_o, self_log, norm_2, inv_2, full_2, low_2 = kernel(
        attend, low_1, left_1, low_1, right_1, full_1, 1, self_near, self_far
    )
    up_yz, down_yz = event(up_yz, down_yz)
    hidden_far_last = mp(mark(jnp.stack([up_yz, down_yz])), 1)
    bias_x = event(bias_x)
    bias_far = mp(mark(jnp.concatenate([bias_own, bias_x], axis=0)), 1)
    gate_cot_in = group_exchange(event(united_grad[:, 0])).reshape(half_rows, width)

    hidden = 4 * PIECES * piece_rows
    hidden_scratch = [
        pltpu.VMEM((4, PIECES, piece_rows, width), BF), pltpu.VMEM((4, PIECES, piece_rows, width), BF),
        pltpu.SemaphoreType.DMA((4,)), pltpu.SemaphoreType.DMA((4,)),
    ]
    hidden_weights = (
        hidden_mine, hidden_far_mine, hidden_x, hidden_y, hidden_z, up_yz, down_yz, hidden_far_three, hidden_far_last
    )
    over_b = struct((2, rows, width), BF)

    def feed_forward(now, *args):
        return call(
            functools.partial(ffn_forward, half_axis),
            [rows_b, over_b, rows_b, struct((rows, hidden), F32), rows_f, column_f, half_b, half_b],
            hidden_scratch, 4 * rows * hidden * width, 18 << 20, "feed_forward", [SM] + [VM] * 6 + [HBM] * 9,
        )(now, *args)

    act_own, act_over, act_core, slope, norm_3, inv_3, keep_3, send_3 = kernel(
        feed_forward, low_2, full_2, bias_own, bias_x, bias_far, params, *hidden_weights
    )

    got_3 = dp(send_3, half_axis)
    act_core, act_over, low_2f = event(act_core, act_over, low_2)
    act_over = mp(act_over, 2)
    low_x = mp(low_2f, 2)
    act_core = mp(act_core, 1)
    low_core = mp(low_2f, 1)
    gate_piece = 2 * width // (4 * PIECES)
    gate_half = struct((2 * PIECES, gate_piece, width), BF)

    def gate_call(now, *args):
        return call(
            functools.partial(gate_kernel, half_axis),
            [half_b, half_b, half_b, gate_half, gate_half, row_f],
            [pltpu.VMEM((2 * width, width), F32)],
            12 * half_rows * width * width, 8 << 20, "gate", [SM, SM] + [VM] * 5,
        )(now, *args)

    united, keep_cot, send_cot, gate_near, gate_far, gate_bias_part = kernel(
        gate_call, page_lengths, keep_3, got_3, gate_weight, params, gate_cot_in
    )
    got_cot = dp(send_cot, half_axis)
    gate_got = mp(gate_far, 1)
    act_over, low_x = event(act_over, low_x)
    act_relay = mp(act_over[1], 1)
    low_relay = mp(mark(low_x), 1)

    def last_norm(now, *args):
        return call(
            functools.partial(last_norm_backward, half_axis),
            [rows_f, rows_b, row_f, row_f, row_f], [], 1 << 20, 3 << 20, "last_norm_back", [SM] + [VM] * 5,
        )(now, *args)

    back_3, branch, gain_3, shift_3, down_bias_part = kernel(last_norm, keep_cot, got_cot, norm_3, inv_3, params)

    class Sum:
        def __init__(self, order, last):
            self.order, self.last = order, last

        def core(self, near, far):
            self.near = near
            self.got = mp(mark(event(far)), 1)

        def over(self):
            near, self.got = event(self.near, self.got)
            self.near = near
            self.from_x = mp(mark(add(near[PIECES:], self.got[PIECES:])), 2)

        def fold(self):
            near, got, over = event(self.near, self.got, self.from_x)
            kept = near[:PIECES].astype(F32) + got[:PIECES].astype(F32)
            return mark((kept + over.astype(F32)).astype(BF))

        def first(self, parts):
            self.parts = parts = event(parts)
            sent = jnp.stack([parts[1], parts[3]]) if self.order == "yz" else parts[2:]
            self.got = dp(mark(sent), 1 if self.order == "yz" else 2)

        def second(self):
            parts, got = event(self.parts, self.got)
            self.keep = parts[0], got[0]
            other = parts[2] if self.order == "yz" else parts[1]
            self.got = dp(mark(add(other, got[1])), 2 if self.order == "yz" else 1)

        def third(self):
            first, second, got = event(*self.keep, self.got)
            piece = (first.astype(F32) + second.astype(F32) + got.astype(F32)).astype(BF)
            for bit in range(2, group_bits):
                piece = add(piece, dp(piece, 1 << bit))
            self.piece = mark(piece)
            self.other = dp(piece, half_axis)

        def fourth(self, shared=0):
            piece, other = event(self.piece, self.other)
            self.piece, self.other = piece, other
            joined = [piece[:piece_rows], other[:piece_rows]]
            if shared:
                joined.append(add(piece[piece_rows:], other[piece_rows:]))
            self.pair = mark(jnp.concatenate(joined, axis=0))
            self.y, self.z = dp(self.pair, 1), dp(self.pair, 2)

        def fifth(self):
            if self.last == "y":
                self.z = event(self.z)
                self.far = dp(mark(self.z), 1)
            else:
                self.y = event(self.y)
                self.far = dp(mark(self.y), 2)

        def sources(self):
            return self.pair, self.y, self.z, self.far

    down_sum, up_sum, self_sum, cross_sum = Sum("yz", "y"), Sum("zy", "y"), Sum("yz", "y"), Sum("yz", "z")
    attn_half = struct((2 * PIECES, shard, width), BF)
    quarter = struct((PIECES, piece_rows, width), BF)
    small_shape = struct((16, width), F32)
    wide = [pltpu.VMEM((8, piece_rows, width), F32), pltpu.SemaphoreType.DMA((8,))]

    def ffn_back(now, *args):
        return call(
            functools.partial(ffn_backward, half_axis),
            [rows_f, rows_b, over_b, rows_b, struct((1, hidden), F32)],
            hidden_scratch, 4 * rows * hidden * width, 16 << 20, "feed_forward_back", [SM] + [VM] * 3 + [HBM] * 9,
        )(now, *args)

    def weight_product(name, now, *args):
        return call(
            functools.partial(rows_product, half_axis), quarter, [], 8 * rows * width * width, 5 << 20, name, [SM] + [VM] * 8,
        )(now, *args)

    def attend_back(now, same_input, cot_in, halos, normed, inverse, layer, saved, near, far_pieces):
        outs = [rows_f, halo_b, halo_b, row_f, row_f, rows_b, rows_b, keys_b, keys_b] + [rows_f] * (not same_input)
        return call(
            functools.partial(attention_backward, half_axis, layer, same_input),
            outs,
            [
                pltpu.VMEM((4, width, width), BF), pltpu.VMEM((rows, width), BF), pltpu.VMEM((keys, width), F32),
                pltpu.VMEM((keys, width), F32), pltpu.SemaphoreType.DMA((4,)),
            ],
            attn_flops, 14 << 20, "attend_back", [SM, SM] + [VM] * (8 + len(halos)) + [HBM] * 7,
        )(now, page_lengths, cot_in, normed, inverse, params, *saved, *halos, mine, far, *near, far_pieces)

    def attend_weights(now, *args):
        return call(
            functools.partial(attention_weights, half_axis),
            [attn_half, attn_half], [pltpu.VMEM((keys, width), BF)],
            attn_flops, 10 << 20, "attend_weights", [SM] + [VM] * 9,
        )(now, *args)

    def place_hidden(now, *sources):
        return call(
            functools.partial(place_pieces, half_axis, None), struct((2, PIECES, piece_rows, width), F32), wide,
            0, 7 << 20, "place_hidden", [SM] + [VM] * 4, HBM,
        )(now, *sources)

    attn_shapes = [struct((2, 2, 3, shard, width), F32), struct((2, 2, shard, width), F32)]

    def place_layer(now, layer, sources, previous):
        return call(
            functools.partial(place_pieces, half_axis, layer), attn_shapes, wide, 0, 7 << 20, "place_layer",
            [SM] + [VM] * 4 + [HBM] * len(previous), [HBM, HBM], {5: 0, 6: 1} if previous else None,
        )(now, *sources, *previous)

    def place_gate_call(now, *args):
        return call(
            functools.partial(place_gate, half_axis, 2 * piece_rows), struct((4 * PIECES, gate_piece, width), F32),
            [pltpu.VMEM((4 * PIECES, gate_piece, width), F32), pltpu.SemaphoreType.DMA((4 * PIECES,))],
            0, 7 << 20, "place_gate", [SM] + [VM] * 6, HBM,
        )(now, *args)

    def small_call(run, shape, name):
        return lambda now, *args: call(run, shape, [], 1 << 16, 1 << 18, name, [SM] + [VM] * len(args))(now, *args)

    got = {}

    class Event:
        def branch_x():
            got["branch_x"] = mp(mark(event(branch)), 2)

        def branch_core():
            got["branch_core"] = mp(mark(event(branch)), 1)

        def branch_relay():
            got["branch_x"] = event(got["branch_x"])
            got["branch_relay"] = mp(mark(got["branch_x"]), 1)

        def ffn_back():
            got["cot_2"], got["own"], got["over"], got["core"], got["bias"] = kernel(ffn_back, back_3, branch, slope, *hidden_weights)

        def pre_x():
            got["over"] = mp(mark(event(got["over"])), 2)

        def pre_core():
            got["core"] = mp(mark(event(got["core"])), 1)

        def pre_relay():
            got["over"] = event(got["over"])
            got["relay"] = mp(mark(got["over"][1]), 1)

        def gate_over():
            near, far_got = event(gate_near, gate_got)
            got["gate"] = near, far_got, mp(mark(add(near[PIECES:], far_got[PIECES:])), 2)

        def down_weights():
            got["down"] = kernel(
                functools.partial(weight_product, "down_weights"), act_own, act_over, act_core, act_relay,
                branch, got["branch_x"], got["branch_core"], got["branch_relay"],
            )

        def up_weights():
            got["up"] = kernel(
                functools.partial(weight_product, "up_weights"), got["own"], got["over"], got["core"], got["relay"],
                low_2, low_x, low_core, low_relay,
            )

        def self_back():
            got["self"] = kernel(
                attend_back, True, got["cot_2"], (), norm_2, inv_2, 1, (self_q, self_k, self_v, self_log), self_near, self_far
            )

        def self_halo():
            left, right = event(got["self"][1], got["self"][2])
            got["halos"] = to_next(mark(right)), to_previous(left)

        def self_weights():
            low, dq, dk, dv = got["self"][5:9]
            got["self_grads"] = kernel(attend_weights, self_o, low, dq, dk, dv, low_1, left_1, low_1, right_1)

        def self_core():
            self_sum.core(*got["self_grads"])

        def cross_back():
            got["cross"] = kernel(
                attend_back, False, got["self"][0], got["halos"], norm_1, inv_1, 0,
                (cross_q, cross_k, cross_v, cross_log), cross_near, cross_far,
            )

        def cross_halo():
            left, right = event(got["cross"][1], got["cross"][2])
            got["cross_halos"] = to_next(mark(right)), to_previous(left)

        def cross_weights():
            low, dq, dk, dv = got["cross"][5:9]
            got["cross_grads"] = kernel(attend_weights, cross_o, low, dq, dk, dv, own, partner_left, partner, partner_right)

        def cross_core():
            cross_sum.core(*got["cross_grads"])

        def small_core():
            got["small"] = kernel(
                small_call(pack_small, small_shape, "pack_small"), got["bias"],
                got["cross"][3], got["self"][3], gain_3, got["cross"][4], got["self"][4], shift_3, down_bias_part, gate_bias_part,
            )
            got["small_got"] = mp(got["small"], 1)

        def small_over():
            got["small"] = kernel(small_call(add_small, small_shape, "add_small"), got["small"], got["small_got"])
            got["small_got"] = mp(got["small"], 2)

        def self_first():
            rows_all = struct((PIECES, shard + 16, width), BF)
            self_sum.first(kernel(
                small_call(spread_small, rows_all, "spread_small"), self_sum.fold(), got["small"], got["small_got"]
            ))

        def partner():
            left, right, mine_cot = event(*got["cross_halos"], got["cross"][9])
            cot = mine_cot + jnp.concatenate([left, right], axis=0).astype(F32)
            got["partner"] = dp(mark(cot.astype(BF)), half_axis)

        def partner_end():
            mine_cot, theirs = event(got["cross"][0], got["partner"])
            got["stream"] = mark(mine_cot + theirs.astype(F32))[None]

        def down_first():
            down_sum.first(got["down"])

        def up_first():
            near, far_got, over, parts = event(*got["gate"], got["up"])
            gate = near[:PIECES].astype(F32) + far_got[:PIECES].astype(F32) + over.astype(F32)
            up_sum.first(jnp.concatenate([parts, gate.astype(BF)], axis=1))

        def cross_first():
            cross_sum.first(cross_sum.fold())

        def up_fourth():
            up_sum.fourth(shared=True)

        def gate_x():
            pieces = event(*(source for source in up_sum.sources()))
            got["gate_near"] = mark(jnp.stack([piece[2 * piece_rows :] for piece in pieces]))
            got["gate_x"] = mp(got["gate_near"], 2)

        def gate_core():
            got["gate_x"] = event(got["gate_x"])
            got["gate_core"] = mp(mark(jnp.concatenate([got["gate_near"], got["gate_x"]], axis=0)), 1)

        def gate_place():
            got["gate_grad"] = kernel(place_gate_call, *up_sum.sources(), got["gate_x"], got["gate_core"])

        def up_place():
            got["up_grad"] = kernel(place_hidden, *up_sum.sources())

        def down_place():
            got["down_grad"] = kernel(place_hidden, *down_sum.sources())

        def self_place():
            got["attn"] = kernel(place_layer, 1, self_sum.sources(), got.get("attn", ()))

        def cross_place():
            got["attn"] = kernel(place_layer, 0, cross_sum.sources(), got.get("attn", ()))

    groups = {"down": down_sum, "up": up_sum, "self": self_sum, "cross": cross_sum}
    for name in ORDER:
        if hasattr(Event, name):
            getattr(Event, name)()
        else:
            group, stage = name.split("_")
            getattr(groups[group], stage)()
    united_out = group_exchange(event(united).reshape(half_axis, slice_rows, width)).astype(F32)

    mine_small = self_sum.piece[shard : shard + 9].astype(F32)
    other_small = self_sum.other[shard : shard + 9].astype(F32)
    is_text = modality == 0
    pair = jnp.stack([jnp.where(is_text, mine_small, other_small), jnp.where(is_text, other_small, mine_small)])
    attn_in_grad, attn_out_grad = got["attn"]
    return (
        united_out[:, None],
        got["stream"],
        attn_in_grad,
        attn_out_grad,
        got["up_grad"].reshape(2, PIECES * piece_rows, width),
        pair[:, 8],
        got["down_grad"].reshape(2, PIECES * piece_rows, width),
        pair[:, 6],
        pair[:, 0:3],
        pair[:, 3:6],
        got["gate_grad"].reshape(2, width, width),
        mine_small[7] + other_small[7],
    )


def solution(mesh):
    placed = (
        P("dp", "mp", None),
        P(),
        P(None, None, None, "mp", None),
        P(None, None, "mp", None),
        P(None, "mp", None),
        P(None, "mp"),
        P(None, "mp", None),
        P(),
        P(),
        P(),
        P(),
        P(),
        P(None, "mp", "dp", None),
    )
    return jax.shard_map(
        body,
        mesh=mesh,
        in_specs=placed,
        out_specs=(
            P(None, "mp", "dp", None),
            P("dp", "mp", None),
            P(None, None, None, "mp", None),
            P(None, None, "mp", None),
            P(None, "mp", None),
            P(None, "mp"),
            P(None, "mp", None),
            P(),
            P(),
            P(),
            P(),
            P(),
        ),
        check_vma=False,
    )
```

```python
import functools

import jax
import jax.numpy as jnp
from jax import lax
from jax.experimental import pallas as pl
from jax.experimental.pallas import tpu as pltpu
from jax.sharding import PartitionSpec as P

DH = 64
L = 1024
PAGES = 16
EPS = 1e-05
SCALE = 0.125
LOG2E = 1.4426950408889634
MASKED = -1e30
HALO = 128
PIECES = 4
BF = jnp.bfloat16
F32 = jnp.float32
VMEM_LIMIT = 16 * 1024 * 1024
SMALL_LIMIT = 4 * 1024 * 1024

VM = pl.BlockSpec(memory_space=pltpu.VMEM)
SM = pl.BlockSpec(memory_space=pltpu.SMEM)
ANY = pl.BlockSpec(memory_space=pl.ANY)


def nn(a, b):
    return lax.dot_general(a, b, (((1,), (0,)), ((), ())), preferred_element_type=F32)


def nt(a, b):
    return lax.dot_general(a, b, (((1,), (1,)), ((), ())), preferred_element_type=F32)


def tn(a, b):
    return lax.dot_general(a, b, (((0,), (0,)), ((), ())), preferred_element_type=F32)


def call(body, outs, scratch=(), flops=0, traffic=0, name=None, specs=None, out_specs=None, aliases=None, limit=VMEM_LIMIT):
    def run(*args):
        return pl.pallas_call(
            body,
            out_shape=outs,
            in_specs=specs if specs is not None else [SM] + [VM] * (len(args) - 1),
            out_specs=out_specs if out_specs is not None else jax.tree.map(lambda _: VM, outs),
            scratch_shapes=list(scratch),
            input_output_aliases=aliases or {},
            compiler_params=pltpu.CompilerParams(vmem_limit_bytes=limit),
            cost_estimate=pl.CostEstimate(flops=flops, bytes_accessed=traffic, transcendentals=0),
            name=name,
        )(*args)

    return run


def struct(shape, dtype):
    return jax.ShapeDtypeStruct(shape, dtype)


def after(value, *deps):
    return lax.optimization_barrier((value,) + deps)[0]


class Where:
    def __init__(self, scal, half_axis):
        self.modality = scal[0] // half_axis
        self.sequence = scal[0] % half_axis
        self.turn = scal[0] % PIECES
        self.place = scal[1]


def page_ends(pages, sequence):
    ends = []
    used = jnp.int32(0)
    running = jnp.int32(0)
    for page in range(PAGES):
        running = running + pages[sequence, page]
        fits = running <= L
        ends.append(jnp.where(fits, running, 2 * L))
        used = jnp.where(fits, running, used)
    return ends, used


def segment_of(position, ends):
    segment = jnp.zeros_like(position)
    for end in ends:
        segment = segment + (end <= position).astype(jnp.int32)
    return segment


def block_bias(ends, base, block, keys):
    query = base + block * HALO + lax.broadcasted_iota(jnp.int32, (HALO, 1), 0)
    key = base + (block - 1) * HALO + lax.broadcasted_iota(jnp.int32, (1, keys), 1)
    query_seg = segment_of(query, ends)
    key_seg = segment_of(key, ends)
    key_seg = jnp.where((key >= 0) & (key < L), key_seg, -1)
    return jnp.where(query_seg == key_seg, 0.0, MASKED)


def normalise(residual, gain, shift):
    center = residual - jnp.mean(residual, axis=-1, keepdims=True)
    inverse = lax.rsqrt(jnp.mean(center * center, axis=-1, keepdims=True) + EPS)
    normed = center * inverse
    return normed * gain + shift, normed, inverse


def norm_back(cot, gain, normed, inverse):
    grad = cot * gain
    back = inverse * (
        grad
        - jnp.mean(grad, axis=-1, keepdims=True)
        - normed * jnp.mean(grad * normed, axis=-1, keepdims=True)
    )
    return back, jnp.sum(cot * normed, axis=0, keepdims=True), jnp.sum(cot, axis=0, keepdims=True)


def attention_matrices(layer, turn, mine, far, near_pieces, far_pieces, pieces):
    for relative in range(PIECES):
        pieces[0, relative ^ turn] = near_pieces[relative][...]
        pieces[1, relative ^ turn] = far_pieces[relative][...]

    def matrix(which):
        return jnp.concatenate([mine[layer, which], pieces[0, which], far[layer, which], pieces[1, which]], axis=0)

    return matrix


def stack_heads(pair, first):
    zero = jnp.zeros_like(pair)
    return jnp.concatenate([jnp.where(first, pair, zero), jnp.where(first, zero, pair)], axis=0)


def extend(left, own, right, extended):
    rows = own.shape[0]
    extended[0:HALO, :] = left[...]
    extended[HALO : HALO + rows, :] = own[...]
    extended[HALO + rows : 2 * HALO + rows, :] = right[...]


def attention_forward(half_axis, layer, *refs):
    scal, pages, query_in, left, own, right, resid, params = refs[:8]
    mine, far, near_pieces, far_pieces = refs[8], refs[9], refs[10:14], refs[14:18]
    q_out, k_out, v_out, o_out, log_out, norm_out, inv_out, full_out, low_out, head_out, tail_out = refs[18:29]
    extended, pieces = refs[29:]
    where = Where(scal, half_axis)
    rows, width = query_in.shape
    window = 3 * HALO
    matrix = attention_matrices(layer, where.turn, mine, far, near_pieces, far_pieces, pieces)
    extend(left, own, right, extended)
    ends, _ = page_ends(pages, where.sequence)
    base = where.place * rows
    q_out[...] = nt(query_in[...], matrix(0)).astype(BF)
    k_out[...] = nt(extended[...], matrix(1)).astype(BF)
    v_out[...] = nt(extended[...], matrix(2)).astype(BF)
    lane = lax.broadcasted_iota(jnp.int32, (1, 2 * DH), 1)
    first = lane < DH
    for block in range(rows // HALO):
        bias = block_bias(ends, base, block, window)
        bias = jnp.concatenate([bias, bias], axis=0)
        row = slice(block * HALO, (block + 1) * HALO)
        span = slice(block * HALO, block * HALO + window)
        logs = jnp.zeros((HALO, 2 * DH), F32)
        for pair in range(width // (2 * DH)):
            cols = slice(pair * 2 * DH, (pair + 1) * 2 * DH)
            scores = nt(stack_heads(q_out[row, cols], first), k_out[span, cols])
            scores = scores * (SCALE * LOG2E) + bias
            top = jnp.max(scores, axis=-1, keepdims=True)
            expo = jnp.exp2(scores - top)
            total = jnp.sum(expo, axis=-1, keepdims=True)
            mixed = nn(expo.astype(BF), v_out[span, cols]) / total
            log = top + jnp.log2(total)
            logs = jnp.where(lane == 2 * pair, log[:HALO], jnp.where(lane == 2 * pair + 1, log[HALO:], logs))
            o_out[row, cols] = jnp.where(first, mixed[:HALO], mixed[HALO:]).astype(BF)
        log_out[row, :] = logs
    residual = resid[...].astype(F32) + nn(o_out[...], matrix(3))
    full, normed, inverse = normalise(residual, params[layer : layer + 1, :], params[3 + layer : 4 + layer, :])
    norm_out[...] = normed
    inv_out[...] = inverse
    full_out[...] = full
    low = full.astype(BF)
    low_out[...] = low
    head_out[...] = low[:HALO]
    tail_out[...] = low[rows - HALO :]


def attention_backward(half_axis, layer, same_input, *refs):
    scal, pages, cot_in, normed, inverse, params = refs[:6]
    q_in, k_in, v_in, log_in = refs[6:10]
    refs = refs[10:]
    halos = ()
    if not same_input:
        halos, refs = refs[:2], refs[2:]
    mine, far, near_pieces, far_pieces = refs[0], refs[1], refs[2:6], refs[6:10]
    refs = refs[10:]
    query_cot, to_left, to_right, gain_out, shift_out, low, dq, dkl, dvl = refs[:9]
    refs = refs[9:]
    if not same_input:
        key_cot, refs = refs[0], refs[1:]
    pieces, o_cot, dk, dv = refs
    where = Where(scal, half_axis)
    rows, width = cot_in.shape
    keys = rows + 2 * HALO
    window = 3 * HALO
    matrix = attention_matrices(layer, where.turn, mine, far, near_pieces, far_pieces, pieces)
    cot = cot_in[...]
    if halos:
        cot = cot + jnp.concatenate([halos[0][...], halos[1][...]], axis=0).astype(F32)
    back, gain_grad, shift_grad = norm_back(cot, params[layer : layer + 1, :], normed[...], inverse[...])
    gain_out[...] = gain_grad
    shift_out[...] = shift_grad
    query_cot[...] = back
    low[...] = back.astype(BF)
    o_cot[...] = nt(low[...], matrix(3)).astype(BF)
    ends, _ = page_ends(pages, where.sequence)
    base = where.place * rows
    lane = lax.broadcasted_iota(jnp.int32, (1, 2 * DH), 1)
    first = lane < DH
    dk[...] = jnp.zeros_like(dk)
    dv[...] = jnp.zeros_like(dv)
    for block in range(rows // HALO):
        bias = block_bias(ends, base, block, window)
        bias = jnp.concatenate([bias, bias], axis=0)
        row = slice(block * HALO, (block + 1) * HALO)
        span = slice(block * HALO, block * HALO + window)
        logs = log_in[row, :]
        for pair in range(width // (2 * DH)):
            cols = slice(pair * 2 * DH, (pair + 1) * 2 * DH)
            queries = stack_heads(q_in[row, cols], first)
            cots = stack_heads(o_cot[row, cols], first)
            key_pair = k_in[span, cols]
            log = jnp.concatenate([logs[:, 2 * pair : 2 * pair + 1], logs[:, 2 * pair + 1 : 2 * pair + 2]], axis=0)
            weights = jnp.exp2(nt(queries, key_pair) * (SCALE * LOG2E) + bias - log)
            weight_cot = nt(cots, v_in[span, cols])
            inner = jnp.sum(weights * weight_cot, axis=-1, keepdims=True)
            score_cot = (weights * (weight_cot - inner)).astype(BF)
            grads = nn(score_cot, key_pair)
            dq[row, cols] = (jnp.where(first, grads[:HALO], grads[HALO:]) * SCALE).astype(BF)
            dk[span, cols] += tn(score_cot, queries)
            dv[span, cols] += tn(weights.astype(BF), cots)
    dkl[...] = (dk[...] * SCALE).astype(BF)
    dvl[...] = dv[...].astype(BF)
    back = nn(dkl[...], matrix(1)) + nn(dvl[...], matrix(2))
    to_left[...] = back[0:HALO, :].astype(BF)
    to_right[...] = back[HALO + rows : keys, :].astype(BF)
    middle = back[HALO : HALO + rows, :]
    direct = nn(dq[...], matrix(0))
    if same_input:
        query_cot[...] += direct + middle
    else:
        query_cot[...] += direct
        key_cot[...] = middle


def attention_weights(half_axis, scal, o_in, low, dq, dk, dv, query_in, left, own, right, near_out, far_out, extended):
    turn = Where(scal, half_axis).turn
    extend(left, own, right, extended)
    piece = near_out.shape[1]
    jobs = ((0, dq, query_in), (1, dk, extended), (2, dv, extended), (3, o_in, low))
    for which, cots, inputs in jobs:
        value = tn(cots[...], inputs[...]).astype(BF)
        for place, (target, start) in enumerate(((near_out, 0), (near_out, PIECES), (far_out, 0), (far_out, PIECES))):
            target[start + (which ^ turn)] = value[place * piece : (place + 1) * piece]


def gelu_parts(value):
    root = 0.7978845608028654
    square = value * value
    inner = jnp.tanh(root * (value + 0.044715 * value * square))
    half = 0.5 * (1.0 + inner)
    slope = half + 0.5 * value * (1.0 - inner * inner) * (root * (1.0 + 3.0 * 0.044715 * square))
    return value * half, slope


def hidden_matrices(turn, refs):
    whole, pieces = (refs[0], refs[1]), (refs[2:7], refs[7:12])

    def matrix(kind, place):
        if place % 2 == 0:
            parts = [whole[place // 2][kind, relative ^ turn] for relative in range(PIECES)]
        else:
            x, y, z, *last = pieces[place // 2]
            parts = [x[kind], y[kind], z[kind], last[kind][...]]
        return jnp.concatenate(parts, axis=0)

    return matrix


def ffn_forward(half_axis, *refs):
    scal, low, full, bias_own, bias_x, bias_far, params = refs[:7]
    act_own, act_over, act_core, slope_out, norm_out, inv_out, keep_out, send_out = refs[19:27]
    where = Where(scal, half_axis)
    matrix = hidden_matrices(where.turn, refs[7:19])
    rows, width = low.shape
    total = full[...] + params[6:7, :]
    biases = (bias_own[...], bias_x[...], bias_far[0:1, :], bias_far[1:2, :])
    for place in range(4):
        cols = slice(place * width, (place + 1) * width)
        pre = nt(low[...], matrix(0, place)) + biases[place]
        value, slope = gelu_parts(pre)
        value = value.astype(BF)
        if place % 2 == 0:
            (act_own, act_core)[place // 2][...] = value
        else:
            act_over[place // 2] = value
        slope_out[:, cols] = slope
        total = total + nn(value, matrix(1, place))
    out, normed, inverse = normalise(total, params[2:3, :], params[5:6, :])
    norm_out[...] = normed
    inv_out[...] = inverse
    out = out.astype(BF)
    half = rows // 2
    is_text = where.modality == 0
    keep_out[...] = jnp.where(is_text, out[:half], out[half:])
    send_out[...] = jnp.where(is_text, out[half:], out[:half])


def last_norm_backward(half_axis, scal, keep, got, normed, inverse, params, back_out, branch_out, gain_out, shift_out, bias_out):
    where = Where(scal, half_axis)
    is_text = where.modality == 0
    kept, other = keep[...], got[...]
    cot = jnp.concatenate([jnp.where(is_text, kept, other), jnp.where(is_text, other, kept)], axis=0).astype(F32)
    back, gain_grad, shift_grad = norm_back(cot, params[2:3, :], normed[...], inverse[...])
    back_out[...] = back
    branch_out[...] = back.astype(BF)
    gain_out[...] = gain_grad
    shift_out[...] = shift_grad
    bias_out[...] = jnp.sum(back, axis=0, keepdims=True)


def ffn_backward(half_axis, *refs):
    scal, back, branch, slope = refs[:4]
    cot_out, pre_own, pre_over, pre_core, bias_out = refs[16:21]
    where = Where(scal, half_axis)
    matrix = hidden_matrices(where.turn, refs[4:16])
    rows, width = branch.shape
    total = back[...]
    for place in range(4):
        cols = slice(place * width, (place + 1) * width)
        act_cot = nt(branch[...], matrix(1, place))
        pre_cot = (act_cot * slope[:, cols]).astype(BF)
        if place % 2 == 0:
            (pre_own, pre_core)[place // 2][...] = pre_cot
        else:
            pre_over[place // 2] = pre_cot
        bias_out[:, cols] = jnp.sum(pre_cot.astype(F32), axis=0, keepdims=True)
        total = total + nn(pre_cot, matrix(0, place))
    cot_out[...] = total


def split_piece(order, relative):
    return (relative % 2, relative // 2) if order == "yz" else (relative // 2, relative % 2)


def rows_product(half_axis, order, scal, left_own, left_over, left_core, left_relay, *refs):
    rights, (keep, send, parts) = refs[:4], refs[4:]
    total = tn(left_own[...], rights[0][...])
    for left, right in ((left_over[0], rights[1]), (left_core[...], rights[2]), (left_relay[1], rights[3])):
        total = total + tn(left, right[...])
    rows = parts.shape[1]
    for piece in range(PIECES):
        parts[piece] = total[piece * rows : (piece + 1) * rows].astype(BF)
    for relative in range(PIECES):
        side, index = split_piece(order, relative)
        target = (keep, send)[side]
        target[index, 0:rows, :] = parts[relative]


def sum_sent(scal, near, got, *outs):
    start = PIECES
    for out in outs:
        stop = start + out.shape[0]
        out[...] = (near[start:stop].astype(F32) + got[start:stop].astype(F32)).astype(BF)
        start = stop


def canonical(row, turn, piece):
    row = jnp.broadcast_to(row, (8, row.shape[1]))
    lane = lax.broadcasted_iota(jnp.int32, row.shape, 1)
    width = row.shape[1]
    swapped = jnp.where((lane // piece) % 2 == 0, pltpu.roll(row, width - piece, 1), pltpu.roll(row, piece, 1))
    row = jnp.where(turn % 2 == 1, swapped, row)
    return jnp.where(turn // 2 == 1, pltpu.roll(row, 2 * piece, 1), row)[0:1]


def sum_fold(order, scal, near, got, over_a, over_b, *refs):
    keep, send = refs[-2:]
    rows = near.shape[1]
    small = None
    if len(refs) > 2:
        mine, other = refs[:2]
        total = mine[4:12, :] + other[4:12, :]
        bias = canonical(mine[0:1, :] + other[1:2, :], scal[0] % PIECES, rows)
        small = jnp.concatenate([total, bias, jnp.zeros((7, total.shape[1]), F32)], axis=0).astype(BF)
    for relative in range(PIECES):
        side, index = split_piece(order, relative)
        target = (keep, send)[side]
        over = (over_a, over_b)[relative // 2][relative % 2]
        summed = near[relative].astype(F32) + got[relative].astype(F32) + over.astype(F32)
        target[index, 0:rows, :] = summed.astype(BF)
        if small is not None:
            target[index, rows : rows + 16, :] = small


def gate_fold(order, scal, near, got, over, keep, send):
    for relative in range(PIECES):
        side, index = split_piece(order, relative)
        summed = near[relative].astype(F32) + got[relative].astype(F32) + over[relative].astype(F32)
        (keep, send)[side][index] = summed.astype(BF)


def sum_second(scal, keep, got, kept, send):
    kept[...] = keep[0].astype(F32) + got[0].astype(F32)
    send[...] = (keep[1].astype(F32) + got[1].astype(F32)).astype(BF)


def sum_third(scal, kept, got, piece):
    piece[...] = (kept[...] + got[...].astype(F32)).astype(BF)


def join_pair(rows, scal, piece, other, pair):
    if rows:
        pair[0:rows, :] = piece[0:rows, :]
        pair[rows : 2 * rows, :] = other[0:rows, :]
    else:
        pair[...] = (piece[...].astype(F32) + other[...].astype(F32)).astype(BF)


def take_gate(start, scal, *refs):
    for piece, source in enumerate(refs[:PIECES]):
        refs[PIECES][piece] = source[start:, :]


def take_half(kind, scal, source, out):
    out[...] = source[kind]


def add_halos(scal, middle, left, right, out):
    out[0:HALO, :] = (middle[0:HALO, :] + left[...].astype(F32)).astype(BF)
    out[HALO:, :] = (middle[HALO:, :] + right[...].astype(F32)).astype(BF)


def add_rows(scal, left, right, out):
    out[...] = left[...] + right[...].astype(F32)


def gate_kernel(
    half_axis, scal, pages, keep, got, weight, params, cot_in,
    united, keep_out, send_out, near_out, far_out, bias_out, grads,
):
    where = Where(scal, half_axis)
    is_text = where.modality == 0
    kept, other = keep[...], got[...]
    text_low = jnp.where(is_text, kept, other)
    vision_low = jnp.where(is_text, other, kept)
    half, width = kept.shape
    _, used = page_ends(pages, where.sequence)
    position = where.place * (2 * half) + where.modality * half + lax.broadcasted_iota(jnp.int32, (half, 1), 0)
    mask = (position < used).astype(F32)
    gate = jax.nn.sigmoid(nt(text_low, weight[0]) + nt(vision_low, weight[1]) + params[7:8, :])
    text_full = text_low.astype(F32)
    vision_full = vision_low.astype(F32)
    united[...] = (mask * (gate * text_full + (1.0 - gate) * vision_full)).astype(BF)
    cot = cot_in[...].astype(F32) * mask
    gate_cot = (cot * (text_full - vision_full) * gate * (1.0 - gate)).astype(BF)
    text_cot = (cot * gate + nn(gate_cot, weight[0])).astype(BF)
    vision_cot = (cot * (1.0 - gate) + nn(gate_cot, weight[1])).astype(BF)
    keep_out[...] = jnp.where(is_text, text_cot, vision_cot)
    send_out[...] = jnp.where(is_text, vision_cot, text_cot)
    bias_out[...] = jnp.sum(gate_cot.astype(F32), axis=0, keepdims=True)
    grads[0:width, :] = tn(gate_cot, text_low)
    grads[width : 2 * width, :] = tn(gate_cot, vision_low)
    rows = near_out.shape[1]
    for spot, (target, start) in enumerate(((near_out, 0), (near_out, PIECES), (far_out, 0), (far_out, PIECES))):
        shard = where.place ^ (0, 2, 1, 3)[spot]
        for piece in range(PIECES):
            at = pl.multiple_of((shard * PIECES + (piece ^ where.turn)) * rows, rows)
            target[start + piece] = grads[pl.ds(at, rows), :].astype(BF)


def place_gate(half_axis, start, scal, *refs):
    near, over, far, far_over, out, wide, sems = refs[:4], *refs[4:]
    where = Where(scal, half_axis)
    rows = over.shape[1]
    copies = []
    for spot in range(4):
        shard = where.place ^ (0, 2, 1, 3)[spot]
        for piece in range(PIECES):
            if spot == 0:
                source = near[piece][start : start + rows, :]
            else:
                source = (over[piece], far[piece], far_over[piece])[spot - 1]
            slot = spot * PIECES + piece
            wide[slot] = source.astype(F32)
            copy = pltpu.make_async_copy(wide.at[slot], out.at[shard * PIECES + (piece ^ where.turn)], sems.at[slot])
            copy.start()
            copies.append(copy)
    for copy in copies:
        copy.wait()


def place_pieces(half_axis, layer, scal, *refs):
    wide, sems = refs[-2:]
    where = Where(scal, half_axis)
    sources, outs = refs[:4], refs[-3:-2] if layer is None else refs[-4:-2]
    rows = wide.shape[1]
    for relative, source in enumerate(sources):
        piece = relative ^ where.turn
        for kind in range(2):
            slot = relative * 2 + kind
            target = kind ^ where.modality
            wide[slot] = source[kind * rows : (kind + 1) * rows, :].astype(F32)

            def send(place, slot=slot):
                pltpu.make_async_copy(wide.at[slot], place, sems.at[slot]).start()

            if layer is None:
                send(outs[0].at[target, piece])
            else:
                pl.when(piece < 3)(lambda: send(outs[0].at[target, layer, piece]))
                pl.when(piece == 3)(lambda: send(outs[1].at[target, layer]))
    for slot in range(8):
        landing = outs[0].at[0, 0] if layer is None else outs[1].at[0, layer]
        pltpu.make_async_copy(wide.at[slot], landing, sems.at[slot]).wait()


def pack_small(scal, bias, *refs):
    out = refs[-1]
    width = out.shape[1]
    out[...] = jnp.zeros_like(out)
    for shard in range(4):
        out[shard : shard + 1, :] = bias[:, shard * width : (shard + 1) * width]
    for row, ref in enumerate(refs[:-1]):
        out[4 + row : 5 + row, :] = ref[...]


def add_small(scal, mine, got, out):
    out[...] = jnp.zeros_like(out)
    out[0:2, :] = mine[0:2, :] + got[2:4, :]
    out[4:12, :] = mine[4:12, :] + got[4:12, :]


SELF_ORDER = ("zy", "z")
CROSS_ORDER = ("zy", "y")
ORDER = (
    "branch_x", "branch_core", "ffn_back", "+branch_core", "+branch_x", "+gate", "branch_relay", "pre_x",
    "pre_core", "gate_first", "+branch_relay", "down_weights", "down_first", "self_back", "+core", "+down.got",
    "+gate.got", "+over", "self_halo", "pre_relay", "down_second", "gate_second", "self_weights", "+halos",
    "+relay", "self_core", "up_weights", "+self.got", "+down.got", "+gate.got", "self_over", "down_third",
    "up_first", "gate_third", "cross_back", "+self.from_x", "+gate.other", "+up.got", "+down.other", "up_second",
    "down_fourth", "self_rest_over", "small_core", "cross_weights", "+small_got", "cross_core", "+up.got",
    "small_over", "+cross.got", "up_third", "+down.z", "cross_over", "+self.rest_x", "down_fifth", "self_first",
    "+down.y", "cross_rest_over", "+cross.from_x", "up_fourth", "self_second", "cross_first", "+down.far",
    "+up.y", "cross_halo", "up_fifth", "self_third", "cross_second", "+cross_halos", "gate_fourth", "cross_third",
    "+up.far", "self_fourth", "gate_fifth", "+gate.y", "cross_fourth", "self_fifth", "gate_x", "+self.z",
    "gate_core", "+gate_core", "partner", "cross_fifth", "partner_end", "down_place", "gate_place", "up_place",
    "self_place", "cross_place",
)


def body(
    streams, page_lengths, attn_in, attn_out, ffn_in, ffn_bias, ffn_out, out_bias,
    norm_gain, norm_bias, gate_weight, gate_bias, united_grad,
):
    devices = lax.axis_size("dp")
    half_axis = devices // 2
    group_bits = half_axis.bit_length() - 1
    data_index = lax.axis_index("dp")
    place = lax.axis_index("mp")
    modality = data_index // half_axis
    sequence = data_index % half_axis
    turn = data_index % PIECES
    own = streams[0]
    rows, width = own.shape
    keys = rows + 2 * HALO
    shard = attn_in.shape[3]

    def swap(value, axis, mask):
        pairs = [(source, source ^ mask) for source in range(lax.axis_size(axis))]
        return lax.ppermute(value, axis, pairs)

    def mp(value, mask):
        return swap(value, "mp", mask)

    def dp(value, mask):
        return swap(value, "dp", mask)

    count = lax.axis_size("mp")

    def to_next(value):
        return lax.ppermute(value, "mp", [(index, index + 1) for index in range(count - 1)])

    def to_previous(value):
        return lax.ppermute(value, "mp", [(index + 1, index) for index in range(count - 1)])

    def pick(stacked, index):
        return lax.dynamic_index_in_dim(stacked, index, 0, keepdims=False)

    scal = jnp.stack([data_index, place]).astype(jnp.int32)
    clock = [scal]

    def event(*values):
        fenced = lax.optimization_barrier(values + (clock[0],))[:-1]
        return fenced if len(fenced) > 1 else fenced[0]

    def mark(value):
        clock[0] = value
        return value

    def kernel(run, *args, due=()):
        now = after(scal, clock[0], *due)
        results = run(now, *args)
        mark(results[-1] if isinstance(results, (list, tuple)) else results)
        return results

    def add(left, right):
        return (left.astype(F32) + right.astype(F32)).astype(BF)

    def glue(run, outs, *args, due=()):
        def launch(now, *operands):
            return call(
                run, outs, [], 1 << 16, 1 << 18, getattr(run, "func", run).__name__, [SM] + [VM] * len(operands), limit=SMALL_LIMIT
            )(now, *operands)

        return kernel(launch, *args, due=due)

    piece_rows = ffn_in.shape[1] // PIECES
    half_rows = rows // 2
    slice_rows = united_grad.shape[2]

    def attention_piece(layer, index):
        inner = lax.dynamic_slice(
            attn_in, (index, layer, jnp.minimum(turn, 2), 0, 0), (1, 1, 1, shard, width)
        ).reshape(shard, width)
        outer = lax.dynamic_slice(attn_out, (index, layer, 0, 0), (1, 1, shard, width)).reshape(shard, width)
        return jnp.where(turn < 3, inner, outer)

    def group_exchange(blocks):
        moved = jnp.stack([pick(blocks, index ^ sequence) for index in range(half_axis)])
        shape = moved.shape
        for bit in range(group_bits):
            view = moved.reshape((half_axis >> (bit + 1), 2, 1 << bit) + shape[1:])
            got = dp(view[:, 1], 1 << bit)
            moved = jnp.stack([view[:, 0], got], axis=1).reshape(shape)
        return jnp.stack([pick(moved, index ^ sequence) for index in range(half_axis)])

    cross_x = mp(mark(attention_piece(0, modality)), 2)
    partner = dp(own, half_axis)
    self_x = mp(mark(attention_piece(1, event(modality))), 2)
    index = event(modality)
    hidden_part = jnp.stack([
        lax.dynamic_slice(weight, (index, turn * piece_rows, 0), (1, piece_rows, width))[0] for weight in (ffn_in, ffn_out)
    ])
    cross_x, hidden_part = event(cross_x, hidden_part)
    cross_y, cross_z = dp(mark(cross_x), 1), dp(cross_x, 2)
    hidden_x = mp(hidden_part, 2)
    index = event(modality)
    mine = mark(jnp.concatenate([pick(attn_in, index), pick(attn_out, index)[:, None]], axis=1))
    partner, cross_y = event(partner, cross_y)
    partner_left = to_next(partner[rows - HALO :])
    partner_right = to_previous(mark(partner[:HALO]))
    cross_yz = dp(cross_y, 2)
    self_x = mark(event(self_x))
    self_y, self_z = dp(self_x, 1), dp(self_x, 2)
    far = mp(event(mine), 1)
    cross_near = (cross_x, cross_y, cross_z, cross_yz)
    cross_far = tuple(mp(mark(event(piece)), 1) for piece in cross_near)
    index = event(modality)
    hidden_mine = mark(jnp.stack([pick(ffn_in, index), pick(ffn_out, index)]).reshape(2, PIECES, piece_rows, width))
    bias_own = jnp.concatenate([
        lax.dynamic_slice(ffn_bias, (index, (relative ^ turn) * piece_rows), (1, piece_rows)) for relative in range(PIECES)
    ], axis=1)
    params = jnp.concatenate(
        [pick(norm_gain, index), pick(norm_bias, index), pick(out_bias, index)[None], gate_bias[None]], axis=0
    )
    bias_x = mp(mark(bias_own), 2)
    gate_cot_in = mark(group_exchange(event(united_grad[:, 0])).reshape(half_rows, width))
    bias_x = event(bias_x)
    bias_far = mp(mark(jnp.concatenate([bias_own, bias_x], axis=0)), 1)
    hidden_x, self_y, self_z = event(hidden_x, self_y, self_z)
    hidden_y, hidden_z = dp(mark(hidden_x), 1), dp(hidden_x, 2)
    self_yz = dp(self_z, 1)
    self_near_three = tuple(mp(event(piece), 1) for piece in (self_x, self_y, self_z))

    rows_f = struct((rows, width), F32)
    rows_b = struct((rows, width), BF)
    keys_b = struct((keys, width), BF)
    row_f = struct((1, width), F32)
    column_f = struct((rows, 1), F32)
    halo_b = struct((HALO, width), BF)
    half_b = struct((half_rows, width), BF)
    attn_flops = 2 * width * width * (2 * rows + 2 * keys)
    matrix_scratch = [pltpu.VMEM((2, PIECES, shard, width), BF)]

    def attend(now, query_in, left, own_rows, right, resid, layer, near, far_pieces):
        return call(
            functools.partial(attention_forward, half_axis, layer),
            [rows_b, keys_b, keys_b, rows_b, struct((rows, 2 * DH), F32), rows_f, column_f, rows_f, rows_b, halo_b, halo_b],
            [pltpu.VMEM((keys, width), BF)] + matrix_scratch,
            attn_flops, 12 << 20, "attend", [SM, SM] + [VM] * 16,
        )(now, page_lengths, query_in, left, own_rows, right, resid, params, mine, far, *near, *far_pieces)

    cross_q, cross_k, cross_v, cross_o, cross_log, norm_1, inv_1, full_1, low_1, head_1, tail_1 = kernel(
        attend, own, partner_left, partner, partner_right, own, 0, cross_near, cross_far
    )
    left_1 = to_next(tail_1)
    right_1 = to_previous(head_1)
    self_yz = mark(event(self_yz))
    self_near = (self_x, self_y, self_z, self_yz)
    self_far = self_near_three + (mp(self_yz, 1),)
    piece_shape = struct((piece_rows, width), BF)
    up_yz = dp(glue(functools.partial(take_half, 0), piece_shape, hidden_y), 2)
    down_yz = dp(glue(functools.partial(take_half, 1), piece_shape, hidden_z), 1)
    hidden_far_mine = mp(event(hidden_mine), 1)
    self_q, self_k, self_v, self_o, self_log, norm_2, inv_2, full_2, low_2, _, _ = kernel(
        attend, low_1, left_1, low_1, right_1, full_1, 1, self_near, self_far
    )
    hidden_far = tuple(mp(mark(event(piece)), 1) for piece in (hidden_x, hidden_y, hidden_z, up_yz, down_yz))

    hidden = 4 * PIECES * piece_rows
    hidden_weights = (
        hidden_mine, hidden_far_mine, hidden_x, hidden_y, hidden_z, up_yz, down_yz, *hidden_far
    )
    over_b = struct((2, rows, width), BF)

    def feed_forward(now, *args):
        return call(
            functools.partial(ffn_forward, half_axis),
            [rows_b, over_b, rows_b, struct((rows, hidden), F32), rows_f, column_f, half_b, half_b],
            [], 4 * rows * hidden * width, 18 << 20, "feed_forward", [SM] + [VM] * 18,
        )(now, *args)

    low_x, low_core = mp(low_2, 2), mp(low_2, 1)
    act_own, act_over, act_core, slope, norm_3, inv_3, keep_3, send_3 = kernel(
        feed_forward, low_2, full_2, bias_own, bias_x, bias_far, params, *hidden_weights
    )

    got_3 = dp(send_3, half_axis)
    low_x, low_core = event(low_x, low_core)
    act_core, act_over = event(act_core, act_over)
    act_over = mp(act_over, 2)
    act_core = mp(act_core, 1)
    low_relay = mp(mark(low_x), 1)
    gate_piece = 2 * width // (4 * PIECES)
    gate_half = struct((2 * PIECES, gate_piece, width), BF)

    def gate_call(now, *args):
        return call(
            functools.partial(gate_kernel, half_axis),
            [half_b, half_b, half_b, gate_half, gate_half, row_f],
            [pltpu.VMEM((2 * width, width), F32)],
            12 * half_rows * width * width, 8 << 20, "gate", [SM, SM] + [VM] * 5,
        )(now, *args)

    united, keep_cot, send_cot, gate_near, gate_far, gate_bias_part = kernel(
        gate_call, page_lengths, keep_3, got_3, gate_weight, params, gate_cot_in, due=(act_core, low_relay)
    )
    got_cot = dp(send_cot, half_axis)
    gate_got = mp(gate_far, 1)
    act_over = event(act_over)
    act_relay = mp(mark(act_over), 1)
    gate_sent = glue(sum_sent, struct((PIECES, gate_piece, width), BF), gate_near, gate_got)
    gate_over = mp(gate_sent, 2)

    def last_norm(now, *args):
        return call(
            functools.partial(last_norm_backward, half_axis),
            [rows_f, rows_b, row_f, row_f, row_f], [], 1 << 20, 3 << 20, "last_norm_back", [SM] + [VM] * 5,
        )(now, *args)

    back_3, branch, gain_3, shift_3, down_bias_part = kernel(last_norm, keep_cot, got_cot, norm_3, inv_3, params)

    class Sum:
        def __init__(self, order, last, extra=0, main=piece_rows):
            self.order, self.last, self.main = order, last, main
            self.rows = main + extra
            self.halves = [struct((2, self.rows, width), BF)] * 2

        def core(self, near, far):
            self.near = near
            self.got = mp(mark(event(far)), 1)

        def over(self):
            half = struct((2, piece_rows, width), BF)
            first, self.rest = glue(sum_sent, [half, half], self.near, self.got)
            self.from_x = mp(first, 2)

        def rest_over(self):
            self.rest_x = mp(mark(event(self.rest)), 2)

        def fold(self, *small):
            self.begin(*glue(
                functools.partial(sum_fold, self.order), self.halves, self.near, self.got, self.from_x, self.rest_x, *small
            ))

        def begin(self, keep, send):
            self.keep = keep
            self.got = dp(send, 1 if self.order == "yz" else 2)

        def second(self):
            self.kept, send = glue(
                sum_second, [struct((self.rows, width), F32), struct((self.rows, width), BF)], self.keep, self.got
            )
            self.got = dp(send, 2 if self.order == "yz" else 1)

        def third(self):
            piece = glue(sum_third, struct((self.rows, width), BF), self.kept, self.got)
            for bit in range(2, group_bits):
                piece = add(piece, dp(piece, 1 << bit))
            self.piece = mark(piece)
            self.other = dp(piece, half_axis)

        def fourth(self):
            self.pair = glue(
                functools.partial(join_pair, self.main), struct((2 * self.main or self.rows, width), BF), self.piece, self.other
            )
            self.y, self.z = dp(self.pair, 1), dp(self.pair, 2)

        def fifth(self):
            if self.last == "y":
                self.z = event(self.z)
                self.far = dp(mark(self.z), 1)
            else:
                self.y = event(self.y)
                self.far = dp(mark(self.y), 2)

        def sources(self):
            return self.pair, self.y, self.z, self.far

    down_sum, up_sum, self_sum, cross_sum = Sum("yz", "y"), Sum("zy", "y"), Sum(*SELF_ORDER, 16), Sum(*CROSS_ORDER)
    gate_sum = Sum("zy", "y", gate_piece, 0)
    attn_half = struct((2 * PIECES, shard, width), BF)
    small_shape = struct((16, width), F32)
    wide = [pltpu.VMEM((8, piece_rows, width), F32), pltpu.SemaphoreType.DMA((8,))]

    def ffn_back(now, *args):
        return call(
            functools.partial(ffn_backward, half_axis),
            [rows_f, rows_b, over_b, rows_b, struct((1, hidden), F32)],
            [], 4 * rows * hidden * width, 16 << 20, "feed_forward_back", [SM] + [VM] * 15,
        )(now, *args)

    def weight_product(name, group, now, *args):
        return call(
            functools.partial(rows_product, half_axis, group.order), group.halves,
            [pltpu.VMEM((PIECES, piece_rows, width), BF)], 8 * rows * width * width, 5 << 20, name, [SM] + [VM] * len(args),
        )(now, *args)

    def attend_back(now, same_input, cot_in, halos, normed, inverse, layer, saved, near, far_pieces):
        outs = [rows_f, halo_b, halo_b, row_f, row_f, rows_b, rows_b, keys_b, keys_b] + [rows_f] * (not same_input)
        return call(
            functools.partial(attention_backward, half_axis, layer, same_input),
            outs,
            [
                pltpu.VMEM((2, PIECES, shard, width), BF), pltpu.VMEM((rows, width), BF), pltpu.VMEM((keys, width), F32),
                pltpu.VMEM((keys, width), F32),
            ],
            attn_flops, 14 << 20, "attend_back", [SM, SM] + [VM] * (18 + len(halos)),
        )(now, page_lengths, cot_in, normed, inverse, params, *saved, *halos, mine, far, *near, *far_pieces)

    def attend_weights(now, *args):
        return call(
            functools.partial(attention_weights, half_axis),
            [attn_half, attn_half], [pltpu.VMEM((keys, width), BF)],
            attn_flops, 10 << 20, "attend_weights", [SM] + [VM] * 9,
        )(now, *args)

    def place_hidden(now, *sources):
        return call(
            functools.partial(place_pieces, half_axis, None), struct((2, PIECES, piece_rows, width), F32), wide,
            0, 7 << 20, "place_hidden", [SM] + [VM] * 4, ANY,
        )(now, *sources)

    attn_shapes = [struct((2, 2, 3, shard, width), F32), struct((2, 2, shard, width), F32)]

    def place_layer(now, layer, sources, previous):
        return call(
            functools.partial(place_pieces, half_axis, layer), attn_shapes, wide, 0, 7 << 20, "place_layer",
            [SM] + [VM] * 4 + [ANY] * len(previous), [ANY, ANY], {5: 0, 6: 1} if previous else None,
        )(now, *sources, *previous)

    def place_gate_call(now, *args):
        return call(
            functools.partial(place_gate, half_axis, 0), struct((4 * PIECES, gate_piece, width), F32),
            [pltpu.VMEM((4 * PIECES, gate_piece, width), F32), pltpu.SemaphoreType.DMA((4 * PIECES,))],
            0, 7 << 20, "place_gate", [SM] + [VM] * 7, ANY,
        )(now, *args)

    def small_call(run, shape, name):
        return lambda now, *args: call(
            run, shape, [], 1 << 16, 1 << 18, name, [SM] + [VM] * len(args), limit=SMALL_LIMIT
        )(now, *args)

    got = {"gate": gate_over}

    class Event:
        def branch_x():
            got["branch_x"] = mp(mark(event(branch)), 2)

        def branch_core():
            got["branch_core"] = mp(mark(event(branch)), 1)

        def branch_relay():
            got["branch_x"] = event(got["branch_x"])
            got["branch_relay"] = mp(mark(got["branch_x"]), 1)

        def ffn_back():
            got["cot_2"], got["own"], got["over"], got["core"], got["bias"] = kernel(ffn_back, back_3, branch, slope, *hidden_weights)

        def pre_x():
            got["over"] = mp(mark(event(got["over"])), 2)

        def pre_core():
            got["core"] = mp(mark(event(got["core"])), 1)

        def pre_relay():
            got["over"] = event(got["over"])
            got["relay"] = mp(mark(got["over"]), 1)

        def down_weights():
            got["down"] = kernel(
                functools.partial(weight_product, "down_weights", down_sum), act_own, act_over, act_core, act_relay,
                branch, got["branch_x"], got["branch_core"], got["branch_relay"],
            )

        def up_weights():
            got["up"] = kernel(
                functools.partial(weight_product, "up_weights", up_sum), got["own"], got["over"], got["core"], got["relay"],
                low_2, low_x, low_core, low_relay,
            )

        def self_back():
            got["self"] = kernel(
                attend_back, True, got["cot_2"], (), norm_2, inv_2, 1, (self_q, self_k, self_v, self_log), self_near, self_far
            )

        def self_halo():
            left, right = event(got["self"][1], got["self"][2])
            got["halos"] = to_next(mark(right)), to_previous(left)

        def self_weights():
            low, dq, dk, dv = got["self"][5:9]
            got["self_grads"] = kernel(attend_weights, self_o, low, dq, dk, dv, low_1, left_1, low_1, right_1)

        def self_core():
            self_sum.core(*got["self_grads"])

        def cross_back():
            got["cross"] = kernel(
                attend_back, False, got["self"][0], got["halos"], norm_1, inv_1, 0,
                (cross_q, cross_k, cross_v, cross_log), cross_near, cross_far,
            )

        def cross_halo():
            left, right = event(got["cross"][1], got["cross"][2])
            got["cross_halos"] = to_next(mark(right)), to_previous(left)

        def cross_weights():
            low, dq, dk, dv = got["cross"][5:9]
            got["cross_grads"] = kernel(attend_weights, cross_o, low, dq, dk, dv, own, partner_left, partner, partner_right)

        def cross_core():
            cross_sum.core(*got["cross_grads"])

        def small_core():
            got["small"] = kernel(
                small_call(pack_small, small_shape, "pack_small"), got["bias"],
                got["cross"][3], got["self"][3], gain_3, got["cross"][4], got["self"][4], shift_3, down_bias_part, gate_bias_part,
            )
            got["small_got"] = mp(got["small"], 1)

        def small_over():
            got["small"] = kernel(small_call(add_small, small_shape, "add_small"), got["small"], got["small_got"])
            got["small_got"] = mp(got["small"], 2)

        def self_first():
            self_sum.fold(got["small"], got["small_got"])

        def partner():
            cot = glue(add_halos, rows_b, got["cross"][9], *got["cross_halos"])
            got["partner"] = dp(cot, half_axis)

        def partner_end():
            got["stream"] = glue(add_rows, rows_f, got["cross"][0], got["partner"])[None]

        def down_first():
            down_sum.begin(*got["down"])

        def up_first():
            up_sum.begin(*got["up"])

        def cross_first():
            cross_sum.fold()

        def gate_first():
            gate_sum.begin(*glue(
                functools.partial(gate_fold, gate_sum.order), gate_sum.halves, gate_near, gate_got, got["gate"]
            ))

        def gate_x():
            near = glue(
                functools.partial(take_gate, 0), struct((PIECES, gate_piece, width), BF), *gate_sum.sources()
            )
            got["gate_near"], got["gate_x"] = near, mp(near, 2)

        def gate_core():
            got["gate_x"] = event(got["gate_x"])
            got["gate_core"] = mp(got["gate_near"], 1), mp(mark(got["gate_x"]), 1)

        def gate_place():
            got["gate_grad"] = kernel(place_gate_call, *gate_sum.sources(), got["gate_x"], *got["gate_core"])

        def up_place():
            got["up_grad"] = kernel(place_hidden, *up_sum.sources())

        def down_place():
            got["down_grad"] = kernel(place_hidden, *down_sum.sources())

        def self_place():
            got["attn"] = kernel(place_layer, 1, self_sum.sources(), got.get("attn", ()))

        def cross_place():
            got["attn"] = kernel(place_layer, 0, cross_sum.sources(), got.get("attn", ()))

    groups = {"gate": gate_sum, "down": down_sum, "up": up_sum, "self": self_sum, "cross": cross_sum}
    def arrived(key):
        owner, _, field = key.partition(".")
        holder = vars(groups[owner]) if field else got
        if (field or owner) not in holder:
            return
        value = holder[field or owner]
        if isinstance(value, tuple):
            holder[field or owner] = event(*value)
            mark(holder[field or owner][-1])
        else:
            holder[field or owner] = mark(event(value))

    for name in ORDER:
        if name.startswith("+"):
            arrived(name[1:])
        elif hasattr(Event, name):
            getattr(Event, name)()
        else:
            group, stage = name.split("_", 1)
            getattr(groups[group], stage)()
    united_out = group_exchange(event(united).reshape(half_axis, slice_rows, width)).astype(F32)

    mine_small = self_sum.piece[shard : shard + 9].astype(F32)
    other_small = self_sum.other[shard : shard + 9].astype(F32)
    is_text = modality == 0
    pair = jnp.stack([jnp.where(is_text, mine_small, other_small), jnp.where(is_text, other_small, mine_small)])
    attn_in_grad, attn_out_grad = got["attn"]
    return (
        united_out[:, None],
        got["stream"],
        attn_in_grad,
        attn_out_grad,
        got["up_grad"].reshape(2, PIECES * piece_rows, width),
        pair[:, 8],
        got["down_grad"].reshape(2, PIECES * piece_rows, width),
        pair[:, 6],
        pair[:, 0:3],
        pair[:, 3:6],
        got["gate_grad"].reshape(2, width, width),
        mine_small[7] + other_small[7],
    )


def solution(mesh):
    placed = (
        P("dp", "mp", None),
        P(),
        P(None, None, None, "mp", None),
        P(None, None, "mp", None),
        P(None, "mp", None),
        P(None, "mp"),
        P(None, "mp", None),
        P(),
        P(),
        P(),
        P(),
        P(),
        P(None, "mp", "dp", None),
    )
    return jax.shard_map(
        body,
        mesh=mesh,
        in_specs=placed,
        out_specs=(
            P(None, "mp", "dp", None),
            P("dp", "mp", None),
            P(None, None, None, "mp", None),
            P(None, None, "mp", None),
            P(None, "mp", None),
            P(None, "mp"),
            P(None, "mp", None),
            P(),
            P(),
            P(),
            P(),
            P(),
        ),
        check_vma=False,
    )
```

```python
import functools

import jax
import jax.numpy as jnp
from jax import lax
from jax.experimental import pallas as pl
from jax.experimental.pallas import tpu as pltpu
from jax.sharding import PartitionSpec as P

DH = 64
L = 1024
PAGES = 16
EPS = 1e-05
SCALE = 0.125
LOG2E = 1.4426950408889634
MASKED = -1e30
HALO = 128
PIECES = 4
BF = jnp.bfloat16
F32 = jnp.float32
VMEM_LIMIT = 16 * 1024 * 1024
SMALL_LIMIT = 4 * 1024 * 1024

VM = pl.BlockSpec(memory_space=pltpu.VMEM)
SM = pl.BlockSpec(memory_space=pltpu.SMEM)
ANY = pl.BlockSpec(memory_space=pl.ANY)


def nn(a, b):
    return lax.dot_general(a, b, (((1,), (0,)), ((), ())), preferred_element_type=F32)


def nt(a, b):
    return lax.dot_general(a, b, (((1,), (1,)), ((), ())), preferred_element_type=F32)


def tn(a, b):
    return lax.dot_general(a, b, (((0,), (0,)), ((), ())), preferred_element_type=F32)


def call(body, outs, scratch=(), flops=0, traffic=0, name=None, specs=None, out_specs=None, aliases=None, limit=VMEM_LIMIT):
    def run(*args):
        return pl.pallas_call(
            body,
            out_shape=outs,
            in_specs=specs if specs is not None else [SM] + [VM] * (len(args) - 1),
            out_specs=out_specs if out_specs is not None else jax.tree.map(lambda _: VM, outs),
            scratch_shapes=list(scratch),
            input_output_aliases=aliases or {},
            compiler_params=pltpu.CompilerParams(vmem_limit_bytes=limit),
            cost_estimate=pl.CostEstimate(flops=flops, bytes_accessed=traffic, transcendentals=0),
            name=name,
        )(*args)

    return run


def struct(shape, dtype):
    return jax.ShapeDtypeStruct(shape, dtype)


def after(value, *deps):
    return lax.optimization_barrier((value,) + deps)[0]


class Where:
    def __init__(self, scal, half_axis):
        self.modality = scal[0] // half_axis
        self.sequence = scal[0] % half_axis
        self.turn = scal[0] % PIECES
        self.place = scal[1]


def page_ends(pages, sequence):
    ends = []
    used = jnp.int32(0)
    running = jnp.int32(0)
    for page in range(PAGES):
        running = running + pages[sequence, page]
        fits = running <= L
        ends.append(jnp.where(fits, running, 2 * L))
        used = jnp.where(fits, running, used)
    return ends, used


def segment_of(position, ends):
    segment = jnp.zeros_like(position)
    for end in ends:
        segment = segment + (end <= position).astype(jnp.int32)
    return segment


def block_bias(ends, base, block, keys):
    query = base + block * HALO + lax.broadcasted_iota(jnp.int32, (HALO, 1), 0)
    key = base + (block - 1) * HALO + lax.broadcasted_iota(jnp.int32, (1, keys), 1)
    query_seg = segment_of(query, ends)
    key_seg = segment_of(key, ends)
    key_seg = jnp.where((key >= 0) & (key < L), key_seg, -1)
    return jnp.where(query_seg == key_seg, 0.0, MASKED)


def normalise(residual, gain, shift):
    center = residual - jnp.mean(residual, axis=-1, keepdims=True)
    inverse = lax.rsqrt(jnp.mean(center * center, axis=-1, keepdims=True) + EPS)
    normed = center * inverse
    return normed * gain + shift, normed, inverse


def norm_back(cot, gain, normed, inverse):
    grad = cot * gain
    back = inverse * (
        grad
        - jnp.mean(grad, axis=-1, keepdims=True)
        - normed * jnp.mean(grad * normed, axis=-1, keepdims=True)
    )
    return back, jnp.sum(cot * normed, axis=0, keepdims=True), jnp.sum(cot, axis=0, keepdims=True)


def attention_matrices(layer, turn, mine, far, near_pieces, far_pieces, pieces):
    for relative in range(PIECES):
        pieces[0, relative ^ turn] = near_pieces[relative][...]
        pieces[1, relative ^ turn] = far_pieces[relative][...]

    def matrix(which):
        return jnp.concatenate([mine[layer, which], pieces[0, which], far[layer, which], pieces[1, which]], axis=0)

    return matrix


def stack_heads(pair, first):
    zero = jnp.zeros_like(pair)
    return jnp.concatenate([jnp.where(first, pair, zero), jnp.where(first, zero, pair)], axis=0)


def extend(left, own, right, extended):
    rows = own.shape[0]
    extended[0:HALO, :] = left[...]
    extended[HALO : HALO + rows, :] = own[...]
    extended[HALO + rows : 2 * HALO + rows, :] = right[...]


def attention_forward(half_axis, layer, *refs):
    scal, pages, query_in, left, own, right, resid, params = refs[:8]
    mine, far, near_pieces, far_pieces = refs[8], refs[9], refs[10:14], refs[14:18]
    q_out, k_out, v_out, o_out, log_out, norm_out, inv_out, full_out, low_out, head_out, tail_out = refs[18:29]
    extended, pieces = refs[29:]
    where = Where(scal, half_axis)
    rows, width = query_in.shape
    window = 3 * HALO
    matrix = attention_matrices(layer, where.turn, mine, far, near_pieces, far_pieces, pieces)
    extend(left, own, right, extended)
    ends, _ = page_ends(pages, where.sequence)
    base = where.place * rows
    q_out[...] = nt(query_in[...], matrix(0)).astype(BF)
    k_out[...] = nt(extended[...], matrix(1)).astype(BF)
    v_out[...] = nt(extended[...], matrix(2)).astype(BF)
    lane = lax.broadcasted_iota(jnp.int32, (1, 2 * DH), 1)
    first = lane < DH
    for block in range(rows // HALO):
        bias = block_bias(ends, base, block, window)
        bias = jnp.concatenate([bias, bias], axis=0)
        row = slice(block * HALO, (block + 1) * HALO)
        span = slice(block * HALO, block * HALO + window)
        logs = jnp.zeros((HALO, 2 * DH), F32)
        for pair in range(width // (2 * DH)):
            cols = slice(pair * 2 * DH, (pair + 1) * 2 * DH)
            scores = nt(stack_heads(q_out[row, cols], first), k_out[span, cols])
            scores = scores * (SCALE * LOG2E) + bias
            top = jnp.max(scores, axis=-1, keepdims=True)
            expo = jnp.exp2(scores - top)
            total = jnp.sum(expo, axis=-1, keepdims=True)
            mixed = nn(expo.astype(BF), v_out[span, cols]) / total
            log = top + jnp.log2(total)
            logs = jnp.where(lane == 2 * pair, log[:HALO], jnp.where(lane == 2 * pair + 1, log[HALO:], logs))
            o_out[row, cols] = jnp.where(first, mixed[:HALO], mixed[HALO:]).astype(BF)
        log_out[row, :] = logs
    residual = resid[...].astype(F32) + nn(o_out[...], matrix(3))
    full, normed, inverse = normalise(residual, params[layer : layer + 1, :], params[3 + layer : 4 + layer, :])
    norm_out[...] = normed
    inv_out[...] = inverse
    full_out[...] = full
    low = full.astype(BF)
    low_out[...] = low
    head_out[...] = low[:HALO]
    tail_out[...] = low[rows - HALO :]


def attention_backward(half_axis, layer, same_input, *refs):
    scal, pages, cot_in, normed, inverse, params = refs[:6]
    q_in, k_in, v_in, log_in = refs[6:10]
    refs = refs[10:]
    halos = ()
    if not same_input:
        halos, refs = refs[:2], refs[2:]
    mine, far, near_pieces, far_pieces = refs[0], refs[1], refs[2:6], refs[6:10]
    refs = refs[10:]
    query_cot, to_left, to_right, gain_out, shift_out, low, dq, dkl, dvl = refs[:9]
    refs = refs[9:]
    if not same_input:
        key_cot, refs = refs[0], refs[1:]
    pieces, o_cot, dk, dv = refs
    where = Where(scal, half_axis)
    rows, width = cot_in.shape
    keys = rows + 2 * HALO
    window = 3 * HALO
    matrix = attention_matrices(layer, where.turn, mine, far, near_pieces, far_pieces, pieces)
    cot = cot_in[...]
    if halos:
        cot = cot + jnp.concatenate([halos[0][...], halos[1][...]], axis=0).astype(F32)
    back, gain_grad, shift_grad = norm_back(cot, params[layer : layer + 1, :], normed[...], inverse[...])
    gain_out[...] = gain_grad
    shift_out[...] = shift_grad
    query_cot[...] = back
    low[...] = back.astype(BF)
    o_cot[...] = nt(low[...], matrix(3)).astype(BF)
    ends, _ = page_ends(pages, where.sequence)
    base = where.place * rows
    lane = lax.broadcasted_iota(jnp.int32, (1, 2 * DH), 1)
    first = lane < DH
    dk[...] = jnp.zeros_like(dk)
    dv[...] = jnp.zeros_like(dv)
    for block in range(rows // HALO):
        bias = block_bias(ends, base, block, window)
        bias = jnp.concatenate([bias, bias], axis=0)
        row = slice(block * HALO, (block + 1) * HALO)
        span = slice(block * HALO, block * HALO + window)
        logs = log_in[row, :]
        for pair in range(width // (2 * DH)):
            cols = slice(pair * 2 * DH, (pair + 1) * 2 * DH)
            queries = stack_heads(q_in[row, cols], first)
            cots = stack_heads(o_cot[row, cols], first)
            key_pair = k_in[span, cols]
            log = jnp.concatenate([logs[:, 2 * pair : 2 * pair + 1], logs[:, 2 * pair + 1 : 2 * pair + 2]], axis=0)
            weights = jnp.exp2(nt(queries, key_pair) * (SCALE * LOG2E) + bias - log)
            weight_cot = nt(cots, v_in[span, cols])
            inner = jnp.sum(weights * weight_cot, axis=-1, keepdims=True)
            score_cot = (weights * (weight_cot - inner)).astype(BF)
            grads = nn(score_cot, key_pair)
            dq[row, cols] = (jnp.where(first, grads[:HALO], grads[HALO:]) * SCALE).astype(BF)
            dk[span, cols] += tn(score_cot, queries)
            dv[span, cols] += tn(weights.astype(BF), cots)
    dkl[...] = (dk[...] * SCALE).astype(BF)
    dvl[...] = dv[...].astype(BF)
    back = nn(dkl[...], matrix(1)) + nn(dvl[...], matrix(2))
    to_left[...] = back[0:HALO, :].astype(BF)
    to_right[...] = back[HALO + rows : keys, :].astype(BF)
    middle = back[HALO : HALO + rows, :]
    direct = nn(dq[...], matrix(0))
    if same_input:
        query_cot[...] += direct + middle
    else:
        query_cot[...] += direct
        key_cot[...] = middle


def attention_weights(half_axis, scal, o_in, low, dq, dk, dv, query_in, left, own, right, near_out, far_out, extended):
    turn = Where(scal, half_axis).turn
    extend(left, own, right, extended)
    piece = near_out.shape[1]
    jobs = ((0, dq, query_in), (1, dk, extended), (2, dv, extended), (3, o_in, low))
    for which, cots, inputs in jobs:
        value = tn(cots[...], inputs[...]).astype(BF)
        for place, (target, start) in enumerate(((near_out, 0), (near_out, PIECES), (far_out, 0), (far_out, PIECES))):
            target[start + (which ^ turn)] = value[place * piece : (place + 1) * piece]


def gelu_parts(value):
    root = 0.7978845608028654
    square = value * value
    inner = jnp.tanh(root * (value + 0.044715 * value * square))
    half = 0.5 * (1.0 + inner)
    slope = half + 0.5 * value * (1.0 - inner * inner) * (root * (1.0 + 3.0 * 0.044715 * square))
    return value * half, slope


def hidden_matrices(turn, refs):
    whole, pieces = (refs[0], refs[1]), (refs[2:7], refs[7:12])

    def matrix(kind, place):
        if place % 2 == 0:
            parts = [whole[place // 2][kind, relative ^ turn] for relative in range(PIECES)]
        else:
            x, y, z, *last = pieces[place // 2]
            parts = [x[kind], y[kind], z[kind], last[kind][...]]
        return jnp.concatenate(parts, axis=0)

    return matrix


def ffn_forward(half_axis, *refs):
    scal, low, full, bias_own, bias_x, bias_far, params = refs[:7]
    acts, (slope_out, norm_out, inv_out, keep_out, send_out) = refs[19:23], refs[23:28]
    where = Where(scal, half_axis)
    matrix = hidden_matrices(where.turn, refs[7:19])
    rows, width = low.shape
    total = full[...] + params[6:7, :]
    biases = (bias_own[...], bias_x[...], bias_far[0:1, :], bias_far[1:2, :])
    for place in range(4):
        cols = slice(place * width, (place + 1) * width)
        pre = nt(low[...], matrix(0, place)) + biases[place]
        value, slope = gelu_parts(pre)
        value = value.astype(BF)
        acts[place][...] = value
        slope_out[:, cols] = slope
        total = total + nn(value, matrix(1, place))
    out, normed, inverse = normalise(total, params[2:3, :], params[5:6, :])
    norm_out[...] = normed
    inv_out[...] = inverse
    out = out.astype(BF)
    half = rows // 2
    is_text = where.modality == 0
    keep_out[...] = jnp.where(is_text, out[:half], out[half:])
    send_out[...] = jnp.where(is_text, out[half:], out[:half])


def last_norm_backward(half_axis, scal, keep, got, normed, inverse, params, back_out, branch_out, gain_out, shift_out, bias_out):
    where = Where(scal, half_axis)
    is_text = where.modality == 0
    kept, other = keep[...], got[...]
    cot = jnp.concatenate([jnp.where(is_text, kept, other), jnp.where(is_text, other, kept)], axis=0).astype(F32)
    back, gain_grad, shift_grad = norm_back(cot, params[2:3, :], normed[...], inverse[...])
    back_out[...] = back
    branch_out[...] = back.astype(BF)
    gain_out[...] = gain_grad
    shift_out[...] = shift_grad
    bias_out[...] = jnp.sum(back, axis=0, keepdims=True)


def ffn_backward(half_axis, *refs):
    scal, back, branch, slope = refs[:4]
    cot_out, pre_own, pre_over, pre_core, bias_out = refs[16:21]
    where = Where(scal, half_axis)
    matrix = hidden_matrices(where.turn, refs[4:16])
    rows, width = branch.shape
    total = back[...]
    for place in range(4):
        cols = slice(place * width, (place + 1) * width)
        act_cot = nt(branch[...], matrix(1, place))
        pre_cot = (act_cot * slope[:, cols]).astype(BF)
        if place % 2 == 0:
            (pre_own, pre_core)[place // 2][...] = pre_cot
        else:
            pre_over[place // 2] = pre_cot
        bias_out[:, cols] = jnp.sum(pre_cot.astype(F32), axis=0, keepdims=True)
        total = total + nn(pre_cot, matrix(0, place))
    cot_out[...] = total


def split_piece(order, relative):
    return (relative % 2, relative // 2) if order == "yz" else (relative // 2, relative % 2)


def rows_product(half_axis, order, scal, left_own, left_over, left_core, left_relay, *refs):
    rights, (keep, send, parts) = refs[:4], refs[4:]
    total = tn(left_own[...], rights[0][...])
    if len(left_over.shape) == 3:
        left_over, left_relay = left_over.at[0], left_relay.at[1]
    for left, right in ((left_over[...], rights[1]), (left_core[...], rights[2]), (left_relay[...], rights[3])):
        total = total + tn(left, right[...])
    rows = parts.shape[1]
    for piece in range(PIECES):
        parts[piece] = total[piece * rows : (piece + 1) * rows].astype(BF)
    for relative in range(PIECES):
        side, index = split_piece(order, relative)
        target = (keep, send)[side]
        target[index, 0:rows, :] = parts[relative]


def sum_sent(scal, near, got, *outs):
    start = PIECES
    for out in outs:
        stop = start + out.shape[0]
        out[...] = (near[start:stop].astype(F32) + got[start:stop].astype(F32)).astype(BF)
        start = stop


def canonical(row, turn, piece):
    row = jnp.broadcast_to(row, (8, row.shape[1]))
    lane = lax.broadcasted_iota(jnp.int32, row.shape, 1)
    width = row.shape[1]
    swapped = jnp.where((lane // piece) % 2 == 0, pltpu.roll(row, width - piece, 1), pltpu.roll(row, piece, 1))
    row = jnp.where(turn % 2 == 1, swapped, row)
    return jnp.where(turn // 2 == 1, pltpu.roll(row, 2 * piece, 1), row)[0:1]


def sum_fold(order, scal, near, got, over_a, over_b, *refs):
    keep, send = refs[-2:]
    rows = near.shape[1]
    small = None
    if len(refs) > 2:
        mine, other = refs[:2]
        total = mine[4:12, :] + other[4:12, :]
        bias = canonical(mine[0:1, :] + other[1:2, :], scal[0] % PIECES, rows)
        small = jnp.concatenate([total, bias, jnp.zeros((7, total.shape[1]), F32)], axis=0).astype(BF)
    for relative in range(PIECES):
        side, index = split_piece(order, relative)
        target = (keep, send)[side]
        over = (over_a, over_b)[relative // 2][relative % 2]
        summed = near[relative].astype(F32) + got[relative].astype(F32) + over.astype(F32)
        target[index, 0:rows, :] = summed.astype(BF)
        if small is not None:
            target[index, rows : rows + 16, :] = small


def gate_fold(order, scal, near, got, over, keep, send):
    for relative in range(PIECES):
        side, index = split_piece(order, relative)
        summed = near[relative].astype(F32) + got[relative].astype(F32) + over[relative].astype(F32)
        (keep, send)[side][index] = summed.astype(BF)


def sum_second(scal, keep, got, kept, send):
    kept[...] = keep[0].astype(F32) + got[0].astype(F32)
    send[...] = (keep[1].astype(F32) + got[1].astype(F32)).astype(BF)


def sum_third(scal, kept, got, piece):
    piece[...] = (kept[...] + got[...].astype(F32)).astype(BF)


def join_pair(rows, scal, piece, other, pair):
    if rows:
        pair[0:rows, :] = piece[0:rows, :]
        pair[rows : 2 * rows, :] = other[0:rows, :]
    else:
        pair[...] = (piece[...].astype(F32) + other[...].astype(F32)).astype(BF)


def take_gate(start, scal, *refs):
    for piece, source in enumerate(refs[:PIECES]):
        refs[PIECES][piece] = source[start:, :]


def take_half(kind, scal, source, out):
    out[...] = source[kind]


def add_halos(scal, middle, left, right, out):
    out[0:HALO, :] = (middle[0:HALO, :] + left[...].astype(F32)).astype(BF)
    out[HALO:, :] = (middle[HALO:, :] + right[...].astype(F32)).astype(BF)


def add_rows(scal, left, right, out):
    out[...] = left[...] + right[...].astype(F32)


def gate_kernel(
    half_axis, scal, pages, keep, got, weight, params, cot_in,
    united, keep_out, send_out, near_out, far_out, bias_out, grads,
):
    where = Where(scal, half_axis)
    is_text = where.modality == 0
    kept, other = keep[...], got[...]
    text_low = jnp.where(is_text, kept, other)
    vision_low = jnp.where(is_text, other, kept)
    half, width = kept.shape
    _, used = page_ends(pages, where.sequence)
    position = where.place * (2 * half) + where.modality * half + lax.broadcasted_iota(jnp.int32, (half, 1), 0)
    mask = (position < used).astype(F32)
    gate = jax.nn.sigmoid(nt(text_low, weight[0]) + nt(vision_low, weight[1]) + params[7:8, :])
    text_full = text_low.astype(F32)
    vision_full = vision_low.astype(F32)
    united[...] = (mask * (gate * text_full + (1.0 - gate) * vision_full)).astype(BF)
    cot = cot_in[...].astype(F32) * mask
    gate_cot = (cot * (text_full - vision_full) * gate * (1.0 - gate)).astype(BF)
    text_cot = (cot * gate + nn(gate_cot, weight[0])).astype(BF)
    vision_cot = (cot * (1.0 - gate) + nn(gate_cot, weight[1])).astype(BF)
    keep_out[...] = jnp.where(is_text, text_cot, vision_cot)
    send_out[...] = jnp.where(is_text, vision_cot, text_cot)
    bias_out[...] = jnp.sum(gate_cot.astype(F32), axis=0, keepdims=True)
    grads[0:width, :] = tn(gate_cot, text_low)
    grads[width : 2 * width, :] = tn(gate_cot, vision_low)
    rows = near_out.shape[1]
    for spot, (target, start) in enumerate(((near_out, 0), (near_out, PIECES), (far_out, 0), (far_out, PIECES))):
        shard = where.place ^ (0, 2, 1, 3)[spot]
        for piece in range(PIECES):
            at = pl.multiple_of((shard * PIECES + (piece ^ where.turn)) * rows, rows)
            target[start + piece] = grads[pl.ds(at, rows), :].astype(BF)


def place_gate(half_axis, start, scal, *refs):
    near, over, far, far_over, out, wide, sems = refs[:4], *refs[4:]
    where = Where(scal, half_axis)
    rows = over.shape[1]
    copies = []
    for spot in range(4):
        shard = where.place ^ (0, 2, 1, 3)[spot]
        for piece in range(PIECES):
            if spot == 0:
                source = near[piece][start : start + rows, :]
            else:
                source = (over[piece], far[piece], far_over[piece])[spot - 1]
            slot = spot * PIECES + piece
            wide[slot] = source.astype(F32)
            copy = pltpu.make_async_copy(wide.at[slot], out.at[shard * PIECES + (piece ^ where.turn)], sems.at[slot])
            copy.start()
            copies.append(copy)
    for copy in copies:
        copy.wait()


def place_pieces(half_axis, layer, scal, *refs):
    wide, sems = refs[-2:]
    where = Where(scal, half_axis)
    sources, outs = refs[:4], refs[-3:-2] if layer is None else refs[-4:-2]
    rows = wide.shape[1]
    for relative, source in enumerate(sources):
        piece = relative ^ where.turn
        for kind in range(2):
            slot = relative * 2 + kind
            target = kind ^ where.modality
            wide[slot] = source[kind * rows : (kind + 1) * rows, :].astype(F32)

            def send(place, slot=slot):
                pltpu.make_async_copy(wide.at[slot], place, sems.at[slot]).start()

            if layer is None:
                send(outs[0].at[target, piece])
            else:
                pl.when(piece < 3)(lambda: send(outs[0].at[target, layer, piece]))
                pl.when(piece == 3)(lambda: send(outs[1].at[target, layer]))
    for slot in range(8):
        landing = outs[0].at[0, 0] if layer is None else outs[1].at[0, layer]
        pltpu.make_async_copy(wide.at[slot], landing, sems.at[slot]).wait()


def pack_small(scal, bias, *refs):
    out = refs[-1]
    width = out.shape[1]
    out[...] = jnp.zeros_like(out)
    for shard in range(4):
        out[shard : shard + 1, :] = bias[:, shard * width : (shard + 1) * width]
    for row, ref in enumerate(refs[:-1]):
        out[4 + row : 5 + row, :] = ref[...]


def add_small(scal, mine, got, out):
    out[...] = jnp.zeros_like(out)
    out[0:2, :] = mine[0:2, :] + got[2:4, :]
    out[4:12, :] = mine[4:12, :] + got[4:12, :]


SELF_ORDER = ("yz", "y")
CROSS_ORDER = ("zy", "y")
ORDER = (
    "branch_x", "branch_core", "act_relay", "ffn_back", "+branch_core", "+act_relay", "+branch_x", "branch_relay",
    "pre_x", "pre_core", "+branch_relay", "down_weights", "down_first", "self_back", "+core", "+down.got",
    "+over", "self_halo", "pre_relay", "down_second", "gate_over", "self_weights", "+halos", "+relay",
    "self_core", "up_weights", "+self.got", "up_first", "self_over", "cross_back", "+gate", "+self.from_x",
    "+down.got", "+up.got", "down_third", "up_second", "small_core", "gate_first", "small_over", "self_rest_over",
    "cross_weights", "+small_got", "cross_core", "up_third", "+gate.got", "down_fourth", "cross_over",
    "self_first", "+down.y", "up_fourth", "+down.z", "cross_rest_over", "self_second", "+cross.from_x",
    "gate_second", "up_fifth", "cross_first", "gate_third", "+self.got", "+up.y", "cross_halo", "self_third",
    "cross_second", "+cross_halos", "gate_fourth", "up_place", "cross_third", "gate_fifth", "self_fourth",
    "gate_x", "cross_fourth", "self_fifth", "+self.y", "down_fifth", "+gate_x", "partner", "cross_fifth",
    "+cross.y", "+gate_core", "gate_core", "self_place", "gate_place", "down_place", "partner_end", "cross_place",
)


def body(
    streams, page_lengths, attn_in, attn_out, ffn_in, ffn_bias, ffn_out, out_bias,
    norm_gain, norm_bias, gate_weight, gate_bias, united_grad,
):
    devices = lax.axis_size("dp")
    half_axis = devices // 2
    group_bits = half_axis.bit_length() - 1
    data_index = lax.axis_index("dp")
    place = lax.axis_index("mp")
    modality = data_index // half_axis
    sequence = data_index % half_axis
    turn = data_index % PIECES
    own = streams[0]
    rows, width = own.shape
    keys = rows + 2 * HALO
    shard = attn_in.shape[3]

    def swap(value, axis, mask):
        pairs = [(source, source ^ mask) for source in range(lax.axis_size(axis))]
        return lax.ppermute(value, axis, pairs)

    def mp(value, mask):
        return swap(value, "mp", mask)

    def dp(value, mask):
        return swap(value, "dp", mask)

    count = lax.axis_size("mp")

    def to_next(value):
        return lax.ppermute(value, "mp", [(index, index + 1) for index in range(count - 1)])

    def to_previous(value):
        return lax.ppermute(value, "mp", [(index + 1, index) for index in range(count - 1)])

    def pick(stacked, index):
        return lax.dynamic_index_in_dim(stacked, index, 0, keepdims=False)

    scal = jnp.stack([data_index, place]).astype(jnp.int32)
    clock = [scal]

    def event(*values):
        fenced = lax.optimization_barrier(values + (clock[0],))[:-1]
        return fenced if len(fenced) > 1 else fenced[0]

    def mark(value):
        clock[0] = value
        return value

    def kernel(run, *args, due=()):
        now = after(scal, clock[0], *due)
        results = run(now, *args)
        mark(results[-1] if isinstance(results, (list, tuple)) else results)
        return results

    def add(left, right):
        return (left.astype(F32) + right.astype(F32)).astype(BF)

    def glue(run, outs, *args, due=()):
        def launch(now, *operands):
            return call(
                run, outs, [], 1 << 16, 1 << 18, getattr(run, "func", run).__name__, [SM] + [VM] * len(operands), limit=SMALL_LIMIT
            )(now, *operands)

        return kernel(launch, *args, due=due)

    piece_rows = ffn_in.shape[1] // PIECES
    half_rows = rows // 2
    slice_rows = united_grad.shape[2]

    def attention_piece(layer, index):
        inner = lax.dynamic_slice(
            attn_in, (index, layer, jnp.minimum(turn, 2), 0, 0), (1, 1, 1, shard, width)
        ).reshape(shard, width)
        outer = lax.dynamic_slice(attn_out, (index, layer, 0, 0), (1, 1, shard, width)).reshape(shard, width)
        return jnp.where(turn < 3, inner, outer)

    def group_exchange(blocks):
        moved = jnp.stack([pick(blocks, index ^ sequence) for index in range(half_axis)])
        shape = moved.shape
        for bit in range(group_bits):
            view = moved.reshape((half_axis >> (bit + 1), 2, 1 << bit) + shape[1:])
            got = dp(view[:, 1], 1 << bit)
            moved = jnp.stack([view[:, 0], got], axis=1).reshape(shape)
        return jnp.stack([pick(moved, index ^ sequence) for index in range(half_axis)])

    cross_x = mp(mark(attention_piece(0, modality)), 2)
    partner = dp(own, half_axis)
    self_x = mp(mark(attention_piece(1, event(modality))), 2)
    index = event(modality)
    hidden_part = jnp.stack([
        lax.dynamic_slice(weight, (index, turn * piece_rows, 0), (1, piece_rows, width))[0] for weight in (ffn_in, ffn_out)
    ])
    cross_x, hidden_part = event(cross_x, hidden_part)
    cross_y, cross_z = dp(mark(cross_x), 1), dp(cross_x, 2)
    hidden_x = mp(hidden_part, 2)
    index = event(modality)
    mine = mark(jnp.concatenate([pick(attn_in, index), pick(attn_out, index)[:, None]], axis=1))
    partner, cross_y = event(partner, cross_y)
    partner_left = to_next(partner[rows - HALO :])
    partner_right = to_previous(mark(partner[:HALO]))
    cross_yz = dp(cross_y, 2)
    self_x = mark(event(self_x))
    self_y, self_z = dp(self_x, 1), dp(self_x, 2)
    far = mp(event(mine), 1)
    cross_near = (cross_x, cross_y, cross_z, cross_yz)
    cross_far = tuple(mp(mark(event(piece)), 1) for piece in cross_near)
    index = event(modality)
    hidden_mine = mark(jnp.stack([pick(ffn_in, index), pick(ffn_out, index)]).reshape(2, PIECES, piece_rows, width))
    bias_own = jnp.concatenate([
        lax.dynamic_slice(ffn_bias, (index, (relative ^ turn) * piece_rows), (1, piece_rows)) for relative in range(PIECES)
    ], axis=1)
    params = jnp.concatenate(
        [pick(norm_gain, index), pick(norm_bias, index), pick(out_bias, index)[None], gate_bias[None]], axis=0
    )
    bias_x = mp(mark(bias_own), 2)
    gate_cot_in = mark(group_exchange(event(united_grad[:, 0])).reshape(half_rows, width))
    bias_x = event(bias_x)
    bias_far = mp(mark(jnp.concatenate([bias_own, bias_x], axis=0)), 1)
    hidden_x, self_y, self_z = event(hidden_x, self_y, self_z)
    self_yz = dp(mark(self_z), 1)
    hidden_y, hidden_z = dp(mark(event(hidden_x)), 1), dp(hidden_x, 2)
    self_near_three = tuple(mp(event(piece), 1) for piece in (self_x, self_y, self_z))

    rows_f = struct((rows, width), F32)
    rows_b = struct((rows, width), BF)
    keys_b = struct((keys, width), BF)
    row_f = struct((1, width), F32)
    column_f = struct((rows, 1), F32)
    halo_b = struct((HALO, width), BF)
    half_b = struct((half_rows, width), BF)
    attn_flops = 2 * width * width * (2 * rows + 2 * keys)
    matrix_scratch = [pltpu.VMEM((2, PIECES, shard, width), BF)]

    def attend(now, query_in, left, own_rows, right, resid, layer, near, far_pieces):
        return call(
            functools.partial(attention_forward, half_axis, layer),
            [rows_b, keys_b, keys_b, rows_b, struct((rows, 2 * DH), F32), rows_f, column_f, rows_f, rows_b, halo_b, halo_b],
            [pltpu.VMEM((keys, width), BF)] + matrix_scratch,
            attn_flops, 12 << 20, "attend", [SM, SM] + [VM] * 16,
        )(now, page_lengths, query_in, left, own_rows, right, resid, params, mine, far, *near, *far_pieces)

    cross_q, cross_k, cross_v, cross_o, cross_log, norm_1, inv_1, full_1, low_1, head_1, tail_1 = kernel(
        attend, own, partner_left, partner, partner_right, own, 0, cross_near, cross_far
    )
    self_yz, tail_1, head_1 = event(self_yz, tail_1, head_1)
    left_1 = to_next(mark(tail_1))
    right_1 = to_previous(head_1)
    self_near = (self_x, self_y, self_z, self_yz)
    self_far = self_near_three + (mp(self_yz, 1),)
    left_1, right_1 = event(left_1, right_1)
    hidden_y, hidden_z, left_1 = event(hidden_y, hidden_z, left_1)
    mark(left_1)
    piece_shape = struct((piece_rows, width), BF)
    up_yz = dp(glue(functools.partial(take_half, 0), piece_shape, hidden_y), 2)
    down_yz = dp(glue(functools.partial(take_half, 1), piece_shape, hidden_z), 1)
    hidden_far_mine, hidden_far_x = mp(event(hidden_mine), 1), mp(hidden_x, 1)
    self_q, self_k, self_v, self_o, self_log, norm_2, inv_2, full_2, low_2, _, _ = kernel(
        attend, low_1, left_1, low_1, right_1, full_1, 1, self_near, self_far
    )
    up_yz, down_yz, hidden_far_mine, hidden_far_x = event(up_yz, down_yz, hidden_far_mine, hidden_far_x)
    mark(up_yz)
    hidden_far = (hidden_far_x, mp(hidden_y, 1), mp(hidden_z, 1), mp(up_yz, 1), mp(down_yz, 1))

    hidden = 4 * PIECES * piece_rows
    hidden_weights = (
        hidden_mine, hidden_far_mine, hidden_x, hidden_y, hidden_z, up_yz, down_yz, *hidden_far
    )
    over_b = struct((2, rows, width), BF)

    def feed_forward(now, *args):
        return call(
            functools.partial(ffn_forward, half_axis),
            [rows_b] * 4 + [struct((rows, hidden), F32), rows_f, column_f, half_b, half_b],
            [], 4 * rows * hidden * width, 18 << 20, "feed_forward", [SM] + [VM] * 18,
        )(now, *args)

    low_x, low_core = mp(low_2, 2), mp(low_2, 1)
    act_own, act_x, act_core, act_diagonal, slope, norm_3, inv_3, keep_3, send_3 = kernel(
        feed_forward, low_2, full_2, bias_own, bias_x, bias_far, params, *hidden_weights
    )

    got_3 = dp(send_3, half_axis)
    act_x = mp(event(act_x), 2)
    gate_piece = 2 * width // (4 * PIECES)
    gate_half = struct((2 * PIECES, gate_piece, width), BF)

    def gate_call(now, *args):
        return call(
            functools.partial(gate_kernel, half_axis),
            [half_b, half_b, half_b, gate_half, gate_half, row_f],
            [pltpu.VMEM((2 * width, width), F32)],
            12 * half_rows * width * width, 8 << 20, "gate", [SM, SM] + [VM] * 5,
        )(now, *args)

    united, keep_cot, send_cot, gate_near, gate_far, gate_bias_part = kernel(
        gate_call, page_lengths, keep_3, got_3, gate_weight, params, gate_cot_in, due=(low_core, low_x, act_x)
    )
    got_cot = dp(send_cot, half_axis)
    gate_got = mp(gate_far, 1)
    act_diagonal, act_core, low_sent = event(act_diagonal, act_core, low_x)
    act_diagonal = mp(act_diagonal, 2)
    act_core = mp(act_core, 1)
    low_relay = mp(low_sent, 1)
    gate_sent = glue(sum_sent, struct((PIECES, gate_piece, width), BF), gate_near, gate_got)

    def last_norm(now, *args):
        return call(
            functools.partial(last_norm_backward, half_axis),
            [rows_f, rows_b, row_f, row_f, row_f], [], 1 << 20, 3 << 20, "last_norm_back", [SM] + [VM] * 5,
        )(now, *args)

    back_3, branch, gain_3, shift_3, down_bias_part = kernel(last_norm, keep_cot, got_cot, norm_3, inv_3, params, due=(act_diagonal, act_core, low_relay))

    class Sum:
        def __init__(self, order, last, extra=0, main=piece_rows):
            self.order, self.last, self.main = order, last, main
            self.rows = main + extra
            self.halves = [struct((2, self.rows, width), BF)] * 2

        def core(self, near, far):
            self.near = near
            self.got = mp(mark(event(far)), 1)

        def over(self):
            half = struct((2, piece_rows, width), BF)
            first, self.rest = glue(sum_sent, [half, half], self.near, self.got)
            self.from_x = mp(first, 2)

        def rest_over(self):
            self.rest_x = mp(mark(event(self.rest)), 2)

        def fold(self, *small):
            self.begin(*glue(
                functools.partial(sum_fold, self.order), self.halves, self.near, self.got, self.from_x, self.rest_x, *small
            ))

        def begin(self, keep, send):
            self.keep = keep
            self.got = dp(send, 1 if self.order == "yz" else 2)

        def second(self):
            self.kept, send = glue(
                sum_second, [struct((self.rows, width), F32), struct((self.rows, width), BF)], self.keep, self.got
            )
            self.got = dp(send, 2 if self.order == "yz" else 1)

        def third(self):
            piece = glue(sum_third, struct((self.rows, width), BF), self.kept, self.got)
            for bit in range(2, group_bits):
                piece = add(piece, dp(piece, 1 << bit))
            self.piece = mark(piece)
            self.other = dp(piece, half_axis)

        def fourth(self):
            self.pair = glue(
                functools.partial(join_pair, self.main), struct((2 * self.main or self.rows, width), BF), self.piece, self.other
            )
            self.y, self.z = dp(self.pair, 1), dp(self.pair, 2)

        def fifth(self):
            if self.last == "y":
                self.z = event(self.z)
                self.far = dp(mark(self.z), 1)
            else:
                self.y = event(self.y)
                self.far = dp(mark(self.y), 2)

        def sources(self):
            return self.pair, self.y, self.z, self.far

    down_sum, up_sum, self_sum, cross_sum = Sum("yz", "y"), Sum("zy", "y"), Sum(*SELF_ORDER, 16), Sum(*CROSS_ORDER)
    gate_sum = Sum("zy", "y", gate_piece, 0)
    attn_half = struct((2 * PIECES, shard, width), BF)
    small_shape = struct((16, width), F32)
    wide = [pltpu.VMEM((8, piece_rows, width), F32), pltpu.SemaphoreType.DMA((8,))]

    def ffn_back(now, *args):
        return call(
            functools.partial(ffn_backward, half_axis),
            [rows_f, rows_b, over_b, rows_b, struct((1, hidden), F32)],
            [], 4 * rows * hidden * width, 16 << 20, "feed_forward_back", [SM] + [VM] * 15,
        )(now, *args)

    def weight_product(name, group, now, *args):
        return call(
            functools.partial(rows_product, half_axis, group.order), group.halves,
            [pltpu.VMEM((PIECES, piece_rows, width), BF)], 8 * rows * width * width, 5 << 20, name, [SM] + [VM] * len(args),
        )(now, *args)

    def attend_back(now, same_input, cot_in, halos, normed, inverse, layer, saved, near, far_pieces):
        outs = [rows_f, halo_b, halo_b, row_f, row_f, rows_b, rows_b, keys_b, keys_b] + [rows_f] * (not same_input)
        return call(
            functools.partial(attention_backward, half_axis, layer, same_input),
            outs,
            [
                pltpu.VMEM((2, PIECES, shard, width), BF), pltpu.VMEM((rows, width), BF), pltpu.VMEM((keys, width), F32),
                pltpu.VMEM((keys, width), F32),
            ],
            attn_flops, 14 << 20, "attend_back", [SM, SM] + [VM] * (18 + len(halos)),
        )(now, page_lengths, cot_in, normed, inverse, params, *saved, *halos, mine, far, *near, *far_pieces)

    def attend_weights(now, *args):
        return call(
            functools.partial(attention_weights, half_axis),
            [attn_half, attn_half], [pltpu.VMEM((keys, width), BF)],
            attn_flops, 10 << 20, "attend_weights", [SM] + [VM] * 9,
        )(now, *args)

    def place_hidden(now, *sources):
        return call(
            functools.partial(place_pieces, half_axis, None), struct((2, PIECES, piece_rows, width), F32), wide,
            0, 7 << 20, "place_hidden", [SM] + [VM] * 4, ANY,
        )(now, *sources)

    attn_shapes = [struct((2, 2, 3, shard, width), F32), struct((2, 2, shard, width), F32)]

    def place_layer(now, layer, sources, previous):
        return call(
            functools.partial(place_pieces, half_axis, layer), attn_shapes, wide, 0, 7 << 20, "place_layer",
            [SM] + [VM] * 4 + [ANY] * len(previous), [ANY, ANY], {5: 0, 6: 1} if previous else None,
        )(now, *sources, *previous)

    def place_gate_call(now, *args):
        return call(
            functools.partial(place_gate, half_axis, 0), struct((4 * PIECES, gate_piece, width), F32),
            [pltpu.VMEM((4 * PIECES, gate_piece, width), F32), pltpu.SemaphoreType.DMA((4 * PIECES,))],
            0, 7 << 20, "place_gate", [SM] + [VM] * 7, ANY,
        )(now, *args)

    def small_call(run, shape, name):
        return lambda now, *args: call(
            run, shape, [], 1 << 16, 1 << 18, name, [SM] + [VM] * len(args), limit=SMALL_LIMIT
        )(now, *args)

    got = {"act_diagonal": act_diagonal}

    class Event:
        def act_relay():
            got["act_relay"] = mp(mark(event(got["act_diagonal"])), 1)

        def gate_over():
            got["gate"] = mp(mark(event(gate_sent)), 2)

        def branch_x():
            got["branch_x"] = mp(mark(event(branch)), 2)

        def branch_core():
            got["branch_core"] = mp(mark(event(branch)), 1)

        def branch_relay():
            got["branch_x"] = event(got["branch_x"])
            got["branch_relay"] = mp(mark(got["branch_x"]), 1)

        def ffn_back():
            got["cot_2"], got["own"], got["over"], got["core"], got["bias"] = kernel(ffn_back, back_3, branch, slope, *hidden_weights)

        def pre_x():
            got["over"] = mp(mark(event(got["over"])), 2)

        def pre_core():
            got["core"] = mp(mark(event(got["core"])), 1)

        def pre_relay():
            got["over"] = event(got["over"])
            got["relay"] = mp(mark(got["over"]), 1)

        def down_weights():
            got["down"] = kernel(
                functools.partial(weight_product, "down_weights", down_sum), act_own, act_x, act_core, got["act_relay"],
                branch, got["branch_x"], got["branch_core"], got["branch_relay"],
            )

        def up_weights():
            got["up"] = kernel(
                functools.partial(weight_product, "up_weights", up_sum), got["own"], got["over"], got["core"], got["relay"],
                low_2, low_x, low_core, low_relay,
            )

        def self_back():
            got["self"] = kernel(
                attend_back, True, got["cot_2"], (), norm_2, inv_2, 1, (self_q, self_k, self_v, self_log), self_near, self_far
            )

        def self_halo():
            left, right = event(got["self"][1], got["self"][2])
            got["halos"] = to_next(mark(right)), to_previous(left)

        def self_weights():
            low, dq, dk, dv = got["self"][5:9]
            got["self_grads"] = kernel(attend_weights, self_o, low, dq, dk, dv, low_1, left_1, low_1, right_1)

        def self_core():
            self_sum.core(*got["self_grads"])

        def cross_back():
            got["cross"] = kernel(
                attend_back, False, got["self"][0], got["halos"], norm_1, inv_1, 0,
                (cross_q, cross_k, cross_v, cross_log), cross_near, cross_far,
            )

        def cross_halo():
            left, right = event(got["cross"][1], got["cross"][2])
            got["cross_halos"] = to_next(mark(right)), to_previous(left)

        def cross_weights():
            low, dq, dk, dv = got["cross"][5:9]
            got["cross_grads"] = kernel(attend_weights, cross_o, low, dq, dk, dv, own, partner_left, partner, partner_right)

        def cross_core():
            cross_sum.core(*got["cross_grads"])

        def small_core():
            got["small"] = kernel(
                small_call(pack_small, small_shape, "pack_small"), got["bias"],
                got["cross"][3], got["self"][3], gain_3, got["cross"][4], got["self"][4], shift_3, down_bias_part, gate_bias_part,
            )
            got["small_got"] = mp(got["small"], 1)

        def small_over():
            got["small"] = kernel(small_call(add_small, small_shape, "add_small"), got["small"], got["small_got"])
            got["small_got"] = mp(got["small"], 2)

        def self_first():
            self_sum.fold(got["small"], got["small_got"])

        def partner():
            cot = glue(add_halos, rows_b, got["cross"][9], *got["cross_halos"])
            got["partner"] = dp(cot, half_axis)

        def partner_end():
            got["stream"] = glue(add_rows, rows_f, got["cross"][0], got["partner"])[None]

        def down_first():
            down_sum.begin(*got["down"])

        def up_first():
            up_sum.begin(*got["up"])

        def cross_first():
            cross_sum.fold()

        def gate_first():
            gate_sum.begin(*glue(
                functools.partial(gate_fold, gate_sum.order), gate_sum.halves, gate_near, gate_got, got["gate"]
            ))

        def gate_x():
            near = glue(
                functools.partial(take_gate, 0), struct((PIECES, gate_piece, width), BF), *gate_sum.sources()
            )
            got["gate_near"], got["gate_x"] = near, mp(near, 2)

        def gate_core():
            got["gate_x"] = event(got["gate_x"])
            got["gate_core"] = mp(got["gate_near"], 1), mp(mark(got["gate_x"]), 1)

        def gate_place():
            got["gate_grad"] = kernel(place_gate_call, *gate_sum.sources(), got["gate_x"], *got["gate_core"])

        def up_place():
            got["up_grad"] = kernel(place_hidden, *up_sum.sources())

        def down_place():
            got["down_grad"] = kernel(place_hidden, *down_sum.sources())

        def self_place():
            got["attn"] = kernel(place_layer, 1, self_sum.sources(), got.get("attn", ()))

        def cross_place():
            got["attn"] = kernel(place_layer, 0, cross_sum.sources(), got.get("attn", ()))

    groups = {"gate": gate_sum, "down": down_sum, "up": up_sum, "self": self_sum, "cross": cross_sum}
    def arrived(key):
        owner, _, field = key.partition(".")
        holder = vars(groups[owner]) if field else got
        if (field or owner) not in holder:
            return
        value = holder[field or owner]
        if isinstance(value, tuple):
            holder[field or owner] = event(*value)
            mark(holder[field or owner][-1])
        else:
            holder[field or owner] = mark(event(value))

    for name in ORDER:
        if name.startswith("+"):
            arrived(name[1:])
        elif hasattr(Event, name):
            getattr(Event, name)()
        else:
            group, stage = name.split("_", 1)
            getattr(groups[group], stage)()
    united_out = group_exchange(event(united).reshape(half_axis, slice_rows, width)).astype(F32)

    mine_small = self_sum.piece[shard : shard + 9].astype(F32)
    other_small = self_sum.other[shard : shard + 9].astype(F32)
    is_text = modality == 0
    pair = jnp.stack([jnp.where(is_text, mine_small, other_small), jnp.where(is_text, other_small, mine_small)])
    attn_in_grad, attn_out_grad = got["attn"]
    return (
        united_out[:, None],
        got["stream"],
        attn_in_grad,
        attn_out_grad,
        got["up_grad"].reshape(2, PIECES * piece_rows, width),
        pair[:, 8],
        got["down_grad"].reshape(2, PIECES * piece_rows, width),
        pair[:, 6],
        pair[:, 0:3],
        pair[:, 3:6],
        got["gate_grad"].reshape(2, width, width),
        mine_small[7] + other_small[7],
    )


def solution(mesh):
    placed = (
        P("dp", "mp", None),
        P(),
        P(None, None, None, "mp", None),
        P(None, None, "mp", None),
        P(None, "mp", None),
        P(None, "mp"),
        P(None, "mp", None),
        P(),
        P(),
        P(),
        P(),
        P(),
        P(None, "mp", "dp", None),
    )
    return jax.shard_map(
        body,
        mesh=mesh,
        in_specs=placed,
        out_specs=(
            P(None, "mp", "dp", None),
            P("dp", "mp", None),
            P(None, None, None, "mp", None),
            P(None, None, "mp", None),
            P(None, "mp", None),
            P(None, "mp"),
            P(None, "mp", None),
            P(),
            P(),
            P(),
            P(),
            P(),
        ),
        check_vma=False,
    )
```

```python
import functools

import jax
import jax.numpy as jnp
from jax import lax
from jax.experimental import pallas as pl
from jax.experimental.pallas import tpu as pltpu
from jax.sharding import PartitionSpec as P

DH = 64
L = 1024
PAGES = 16
EPS = 1e-05
SCALE = 0.125
LOG2E = 1.4426950408889634
MASKED = -1e30
HALO = 128
PIECES = 4
BF = jnp.bfloat16
F32 = jnp.float32
VMEM_LIMIT = 16 * 1024 * 1024
SMALL_LIMIT = 4 * 1024 * 1024

VM = pl.BlockSpec(memory_space=pltpu.VMEM)
SM = pl.BlockSpec(memory_space=pltpu.SMEM)
ANY = pl.BlockSpec(memory_space=pl.ANY)


def nn(a, b):
    return lax.dot_general(a, b, (((1,), (0,)), ((), ())), preferred_element_type=F32)


def nt(a, b):
    return lax.dot_general(a, b, (((1,), (1,)), ((), ())), preferred_element_type=F32)


def tn(a, b):
    return lax.dot_general(a, b, (((0,), (0,)), ((), ())), preferred_element_type=F32)


def call(body, outs, scratch=(), flops=0, traffic=0, name=None, specs=None, out_specs=None, aliases=None, limit=VMEM_LIMIT):
    def run(*args):
        return pl.pallas_call(
            body,
            out_shape=outs,
            in_specs=specs if specs is not None else [SM] + [VM] * (len(args) - 1),
            out_specs=out_specs if out_specs is not None else jax.tree.map(lambda _: VM, outs),
            scratch_shapes=list(scratch),
            input_output_aliases=aliases or {},
            compiler_params=pltpu.CompilerParams(vmem_limit_bytes=limit),
            cost_estimate=pl.CostEstimate(flops=flops, bytes_accessed=traffic, transcendentals=0),
            name=name,
        )(*args)

    return run


def struct(shape, dtype):
    return jax.ShapeDtypeStruct(shape, dtype)


def after(value, *deps):
    return lax.optimization_barrier((value,) + deps)[0]


class Where:
    def __init__(self, scal, half_axis):
        self.modality = scal[0] // half_axis
        self.sequence = scal[0] % half_axis
        self.turn = scal[0] % PIECES
        self.place = scal[1]


def page_ends(pages, sequence):
    ends = []
    used = jnp.int32(0)
    running = jnp.int32(0)
    for page in range(PAGES):
        running = running + pages[sequence, page]
        fits = running <= L
        ends.append(jnp.where(fits, running, 2 * L))
        used = jnp.where(fits, running, used)
    return ends, used


def segment_of(position, ends):
    segment = jnp.zeros_like(position)
    for end in ends:
        segment = segment + (end <= position).astype(jnp.int32)
    return segment


def block_bias(ends, base, block, keys):
    query = base + block * HALO + lax.broadcasted_iota(jnp.int32, (HALO, 1), 0)
    key = base + (block - 1) * HALO + lax.broadcasted_iota(jnp.int32, (1, keys), 1)
    query_seg = segment_of(query, ends)
    key_seg = segment_of(key, ends)
    key_seg = jnp.where((key >= 0) & (key < L), key_seg, -1)
    return jnp.where(query_seg == key_seg, 0.0, MASKED)


def normalise(residual, gain, shift):
    center = residual - jnp.mean(residual, axis=-1, keepdims=True)
    inverse = lax.rsqrt(jnp.mean(center * center, axis=-1, keepdims=True) + EPS)
    normed = center * inverse
    return normed * gain + shift, normed, inverse


def norm_back(cot, gain, normed, inverse):
    grad = cot * gain
    back = inverse * (
        grad
        - jnp.mean(grad, axis=-1, keepdims=True)
        - normed * jnp.mean(grad * normed, axis=-1, keepdims=True)
    )
    return back, jnp.sum(cot * normed, axis=0, keepdims=True), jnp.sum(cot, axis=0, keepdims=True)


def attention_matrices(layer, turn, mine, far, near_pieces, far_pieces, pieces):
    for relative in range(PIECES):
        pieces[0, relative ^ turn] = near_pieces[relative][...]
        pieces[1, relative ^ turn] = far_pieces[relative][...]

    def matrix(which):
        return jnp.concatenate([mine[layer, which], pieces[0, which], far[layer, which], pieces[1, which]], axis=0)

    return matrix


def stack_heads(pair, first):
    zero = jnp.zeros_like(pair)
    return jnp.concatenate([jnp.where(first, pair, zero), jnp.where(first, zero, pair)], axis=0)


def extend(left, own, right, extended):
    rows = own.shape[0]
    extended[0:HALO, :] = left[...]
    extended[HALO : HALO + rows, :] = own[...]
    extended[HALO + rows : 2 * HALO + rows, :] = right[...]


def attention_forward(half_axis, layer, *refs):
    scal, pages, query_in, left, own, right, resid, params = refs[:8]
    mine, far, near_pieces, far_pieces = refs[8], refs[9], refs[10:14], refs[14:18]
    q_out, k_out, v_out, o_out, log_out, norm_out, inv_out, full_out, low_out, head_out, tail_out = refs[18:29]
    extended, pieces = refs[29:]
    where = Where(scal, half_axis)
    rows, width = query_in.shape
    window = 3 * HALO
    matrix = attention_matrices(layer, where.turn, mine, far, near_pieces, far_pieces, pieces)
    extend(left, own, right, extended)
    ends, _ = page_ends(pages, where.sequence)
    base = where.place * rows
    q_out[...] = nt(query_in[...], matrix(0)).astype(BF)
    k_out[...] = nt(extended[...], matrix(1)).astype(BF)
    v_out[...] = nt(extended[...], matrix(2)).astype(BF)
    lane = lax.broadcasted_iota(jnp.int32, (1, 2 * DH), 1)
    first = lane < DH
    for block in range(rows // HALO):
        bias = block_bias(ends, base, block, window)
        bias = jnp.concatenate([bias, bias], axis=0)
        row = slice(block * HALO, (block + 1) * HALO)
        span = slice(block * HALO, block * HALO + window)
        logs = jnp.zeros((HALO, 2 * DH), F32)
        for pair in range(width // (2 * DH)):
            cols = slice(pair * 2 * DH, (pair + 1) * 2 * DH)
            scores = nt(stack_heads(q_out[row, cols], first), k_out[span, cols])
            scores = scores * (SCALE * LOG2E) + bias
            top = jnp.max(scores, axis=-1, keepdims=True)
            expo = jnp.exp2(scores - top)
            total = jnp.sum(expo, axis=-1, keepdims=True)
            mixed = nn(expo.astype(BF), v_out[span, cols]) / total
            log = top + jnp.log2(total)
            logs = jnp.where(lane == 2 * pair, log[:HALO], jnp.where(lane == 2 * pair + 1, log[HALO:], logs))
            o_out[row, cols] = jnp.where(first, mixed[:HALO], mixed[HALO:]).astype(BF)
        log_out[row, :] = logs
    residual = resid[...].astype(F32) + nn(o_out[...], matrix(3))
    full, normed, inverse = normalise(residual, params[layer : layer + 1, :], params[3 + layer : 4 + layer, :])
    norm_out[...] = normed
    inv_out[...] = inverse
    full_out[...] = full
    low = full.astype(BF)
    low_out[...] = low
    head_out[...] = low[:HALO]
    tail_out[...] = low[rows - HALO :]


def attention_backward(half_axis, layer, same_input, *refs):
    scal, pages, cot_in, normed, inverse, params = refs[:6]
    q_in, k_in, v_in, log_in = refs[6:10]
    refs = refs[10:]
    halos = ()
    if not same_input:
        halos, refs = refs[:2], refs[2:]
    mine, far, near_pieces, far_pieces = refs[0], refs[1], refs[2:6], refs[6:10]
    refs = refs[10:]
    query_cot, to_left, to_right, gain_out, shift_out, low, dq, dkl, dvl = refs[:9]
    refs = refs[9:]
    if not same_input:
        key_cot, refs = refs[0], refs[1:]
    pieces, o_cot, dk, dv = refs
    where = Where(scal, half_axis)
    rows, width = cot_in.shape
    keys = rows + 2 * HALO
    window = 3 * HALO
    matrix = attention_matrices(layer, where.turn, mine, far, near_pieces, far_pieces, pieces)
    cot = cot_in[...]
    if halos:
        cot = cot + jnp.concatenate([halos[0][...], halos[1][...]], axis=0).astype(F32)
    back, gain_grad, shift_grad = norm_back(cot, params[layer : layer + 1, :], normed[...], inverse[...])
    gain_out[...] = gain_grad
    shift_out[...] = shift_grad
    query_cot[...] = back
    low[...] = back.astype(BF)
    o_cot[...] = nt(low[...], matrix(3)).astype(BF)
    ends, _ = page_ends(pages, where.sequence)
    base = where.place * rows
    lane = lax.broadcasted_iota(jnp.int32, (1, 2 * DH), 1)
    first = lane < DH
    dk[...] = jnp.zeros_like(dk)
    dv[...] = jnp.zeros_like(dv)
    for block in range(rows // HALO):
        bias = block_bias(ends, base, block, window)
        bias = jnp.concatenate([bias, bias], axis=0)
        row = slice(block * HALO, (block + 1) * HALO)
        span = slice(block * HALO, block * HALO + window)
        logs = log_in[row, :]
        for pair in range(width // (2 * DH)):
            cols = slice(pair * 2 * DH, (pair + 1) * 2 * DH)
            queries = stack_heads(q_in[row, cols], first)
            cots = stack_heads(o_cot[row, cols], first)
            key_pair = k_in[span, cols]
            log = jnp.concatenate([logs[:, 2 * pair : 2 * pair + 1], logs[:, 2 * pair + 1 : 2 * pair + 2]], axis=0)
            weights = jnp.exp2(nt(queries, key_pair) * (SCALE * LOG2E) + bias - log)
            weight_cot = nt(cots, v_in[span, cols])
            inner = jnp.sum(weights * weight_cot, axis=-1, keepdims=True)
            score_cot = (weights * (weight_cot - inner)).astype(BF)
            grads = nn(score_cot, key_pair)
            dq[row, cols] = (jnp.where(first, grads[:HALO], grads[HALO:]) * SCALE).astype(BF)
            dk[span, cols] += tn(score_cot, queries)
            dv[span, cols] += tn(weights.astype(BF), cots)
    dkl[...] = (dk[...] * SCALE).astype(BF)
    dvl[...] = dv[...].astype(BF)
    back = nn(dkl[...], matrix(1)) + nn(dvl[...], matrix(2))
    to_left[...] = back[0:HALO, :].astype(BF)
    to_right[...] = back[HALO + rows : keys, :].astype(BF)
    middle = back[HALO : HALO + rows, :]
    direct = nn(dq[...], matrix(0))
    if same_input:
        query_cot[...] += direct + middle
    else:
        query_cot[...] += direct
        key_cot[...] = middle


def attention_weights(half_axis, scal, o_in, low, dq, dk, dv, query_in, left, own, right, near_out, far_out, extended):
    turn = Where(scal, half_axis).turn
    extend(left, own, right, extended)
    piece = near_out.shape[1]
    jobs = ((0, dq, query_in), (1, dk, extended), (2, dv, extended), (3, o_in, low))
    for which, cots, inputs in jobs:
        value = tn(cots[...], inputs[...]).astype(BF)
        for place, (target, start) in enumerate(((near_out, 0), (near_out, PIECES), (far_out, 0), (far_out, PIECES))):
            target[start + (which ^ turn)] = value[place * piece : (place + 1) * piece]


def gelu_parts(value):
    root = 0.7978845608028654
    square = value * value
    inner = jnp.tanh(root * (value + 0.044715 * value * square))
    half = 0.5 * (1.0 + inner)
    slope = half + 0.5 * value * (1.0 - inner * inner) * (root * (1.0 + 3.0 * 0.044715 * square))
    return value * half, slope


def hidden_matrices(turn, refs):
    whole, pieces = (refs[0], refs[1]), (refs[2:7], refs[7:12])

    def matrix(kind, place):
        if place % 2 == 0:
            parts = [whole[place // 2][kind, relative ^ turn] for relative in range(PIECES)]
        else:
            x, y, z, *last = pieces[place // 2]
            parts = [x[kind], y[kind], z[kind], last[kind][...]]
        return jnp.concatenate(parts, axis=0)

    return matrix


def ffn_forward(half_axis, *refs):
    scal, low, full, bias_own, bias_x, bias_far, params = refs[:7]
    acts, (slope_out, norm_out, inv_out, keep_out, send_out) = refs[19:23], refs[23:28]
    where = Where(scal, half_axis)
    matrix = hidden_matrices(where.turn, refs[7:19])
    rows, width = low.shape
    total = full[...] + params[6:7, :]
    biases = (bias_own[...], bias_x[...], bias_far[0:1, :], bias_far[1:2, :])
    for place in range(4):
        cols = slice(place * width, (place + 1) * width)
        pre = nt(low[...], matrix(0, place)) + biases[place]
        value, slope = gelu_parts(pre)
        value = value.astype(BF)
        acts[place][...] = value
        slope_out[:, cols] = slope
        total = total + nn(value, matrix(1, place))
    out, normed, inverse = normalise(total, params[2:3, :], params[5:6, :])
    norm_out[...] = normed
    inv_out[...] = inverse
    out = out.astype(BF)
    half = rows // 2
    is_text = where.modality == 0
    keep_out[...] = jnp.where(is_text, out[:half], out[half:])
    send_out[...] = jnp.where(is_text, out[half:], out[:half])


def last_norm_backward(half_axis, scal, keep, got, normed, inverse, params, back_out, branch_out, gain_out, shift_out, bias_out):
    where = Where(scal, half_axis)
    is_text = where.modality == 0
    kept, other = keep[...], got[...]
    cot = jnp.concatenate([jnp.where(is_text, kept, other), jnp.where(is_text, other, kept)], axis=0).astype(F32)
    back, gain_grad, shift_grad = norm_back(cot, params[2:3, :], normed[...], inverse[...])
    back_out[...] = back
    branch_out[...] = back.astype(BF)
    gain_out[...] = gain_grad
    shift_out[...] = shift_grad
    bias_out[...] = jnp.sum(back, axis=0, keepdims=True)


def ffn_backward(half_axis, *refs):
    scal, back, branch, slope = refs[:4]
    cot_out, pre_own, pre_over, pre_core, bias_out = refs[16:21]
    where = Where(scal, half_axis)
    matrix = hidden_matrices(where.turn, refs[4:16])
    rows, width = branch.shape
    total = back[...]
    for place in range(4):
        cols = slice(place * width, (place + 1) * width)
        act_cot = nt(branch[...], matrix(1, place))
        pre_cot = (act_cot * slope[:, cols]).astype(BF)
        if place % 2 == 0:
            (pre_own, pre_core)[place // 2][...] = pre_cot
        else:
            pre_over[place // 2] = pre_cot
        bias_out[:, cols] = jnp.sum(pre_cot.astype(F32), axis=0, keepdims=True)
        total = total + nn(pre_cot, matrix(0, place))
    cot_out[...] = total


def split_piece(order, relative):
    return (relative % 2, relative // 2) if order == "yz" else (relative // 2, relative % 2)


def rows_product(half_axis, order, scal, left_own, left_over, left_core, left_relay, *refs):
    rights, (keep, send, parts) = refs[:4], refs[4:]
    total = tn(left_own[...], rights[0][...])
    if len(left_over.shape) == 3:
        left_over, left_relay = left_over.at[0], left_relay.at[1]
    for left, right in ((left_over[...], rights[1]), (left_core[...], rights[2]), (left_relay[...], rights[3])):
        total = total + tn(left, right[...])
    rows = parts.shape[1]
    for piece in range(PIECES):
        parts[piece] = total[piece * rows : (piece + 1) * rows].astype(BF)
    for relative in range(PIECES):
        side, index = split_piece(order, relative)
        target = (keep, send)[side]
        target[index, 0:rows, :] = parts[relative]


def sum_sent(scal, near, got, *outs):
    start = PIECES
    for out in outs:
        stop = start + out.shape[0]
        out[...] = (near[start:stop].astype(F32) + got[start:stop].astype(F32)).astype(BF)
        start = stop


def canonical(row, turn, piece):
    row = jnp.broadcast_to(row, (8, row.shape[1]))
    lane = lax.broadcasted_iota(jnp.int32, row.shape, 1)
    width = row.shape[1]
    swapped = jnp.where((lane // piece) % 2 == 0, pltpu.roll(row, width - piece, 1), pltpu.roll(row, piece, 1))
    row = jnp.where(turn % 2 == 1, swapped, row)
    return jnp.where(turn // 2 == 1, pltpu.roll(row, 2 * piece, 1), row)[0:1]


def sum_fold(order, scal, near, got, over_a, over_b, *refs):
    keep, send = refs[-2:]
    rows = near.shape[1]
    small = None
    if len(refs) > 2:
        mine, other = refs[:2]
        total = mine[4:12, :] + other[4:12, :]
        bias = canonical(mine[0:1, :] + other[1:2, :], scal[0] % PIECES, rows)
        small = jnp.concatenate([total, bias, jnp.zeros((7, total.shape[1]), F32)], axis=0).astype(BF)
    for relative in range(PIECES):
        side, index = split_piece(order, relative)
        target = (keep, send)[side]
        over = (over_a, over_b)[relative // 2][relative % 2]
        summed = near[relative].astype(F32) + got[relative].astype(F32) + over.astype(F32)
        target[index, 0:rows, :] = summed.astype(BF)
        if small is not None:
            target[index, rows : rows + 16, :] = small


def gate_fold(order, scal, near, got, over, keep, send):
    for relative in range(PIECES):
        side, index = split_piece(order, relative)
        summed = near[relative].astype(F32) + got[relative].astype(F32) + over[relative].astype(F32)
        (keep, send)[side][index] = summed.astype(BF)


def sum_second(scal, keep, got, kept, send):
    kept[...] = keep[0].astype(F32) + got[0].astype(F32)
    send[...] = (keep[1].astype(F32) + got[1].astype(F32)).astype(BF)


def sum_third(scal, kept, got, piece):
    piece[...] = (kept[...] + got[...].astype(F32)).astype(BF)


def join_pair(rows, scal, piece, other, pair):
    if rows:
        pair[0:rows, :] = piece[0:rows, :]
        pair[rows : 2 * rows, :] = other[0:rows, :]
    else:
        pair[...] = (piece[...].astype(F32) + other[...].astype(F32)).astype(BF)


def take_gate(start, scal, *refs):
    for piece, source in enumerate(refs[:PIECES]):
        refs[PIECES][piece] = source[start:, :]


def take_half(kind, scal, source, out):
    out[...] = source[kind]


def add_halos(scal, middle, left, right, out):
    out[0:HALO, :] = (middle[0:HALO, :] + left[...].astype(F32)).astype(BF)
    out[HALO:, :] = (middle[HALO:, :] + right[...].astype(F32)).astype(BF)


def add_rows(scal, left, right, out):
    out[...] = left[...] + right[...].astype(F32)


def gate_kernel(
    half_axis, scal, pages, keep, got, weight, params, cot_in,
    united, keep_out, send_out, near_out, far_out, bias_out, grads,
):
    where = Where(scal, half_axis)
    is_text = where.modality == 0
    kept, other = keep[...], got[...]
    text_low = jnp.where(is_text, kept, other)
    vision_low = jnp.where(is_text, other, kept)
    half, width = kept.shape
    _, used = page_ends(pages, where.sequence)
    position = where.place * (2 * half) + where.modality * half + lax.broadcasted_iota(jnp.int32, (half, 1), 0)
    mask = (position < used).astype(F32)
    gate = jax.nn.sigmoid(nt(text_low, weight[0]) + nt(vision_low, weight[1]) + params[7:8, :])
    text_full = text_low.astype(F32)
    vision_full = vision_low.astype(F32)
    united[...] = (mask * (gate * text_full + (1.0 - gate) * vision_full)).astype(BF)
    cot = cot_in[...].astype(F32) * mask
    gate_cot = (cot * (text_full - vision_full) * gate * (1.0 - gate)).astype(BF)
    text_cot = (cot * gate + nn(gate_cot, weight[0])).astype(BF)
    vision_cot = (cot * (1.0 - gate) + nn(gate_cot, weight[1])).astype(BF)
    keep_out[...] = jnp.where(is_text, text_cot, vision_cot)
    send_out[...] = jnp.where(is_text, vision_cot, text_cot)
    bias_out[...] = jnp.sum(gate_cot.astype(F32), axis=0, keepdims=True)
    grads[0:width, :] = tn(gate_cot, text_low)
    grads[width : 2 * width, :] = tn(gate_cot, vision_low)
    rows = near_out.shape[1]
    for spot, (target, start) in enumerate(((near_out, 0), (near_out, PIECES), (far_out, 0), (far_out, PIECES))):
        shard = where.place ^ (0, 2, 1, 3)[spot]
        for piece in range(PIECES):
            at = pl.multiple_of((shard * PIECES + (piece ^ where.turn)) * rows, rows)
            target[start + piece] = grads[pl.ds(at, rows), :].astype(BF)


def place_gate(half_axis, start, scal, *refs):
    near, over, far, far_over, out, wide, sems = refs[:4], *refs[4:]
    where = Where(scal, half_axis)
    rows = over.shape[1]
    copies = []
    for spot in range(4):
        shard = where.place ^ (0, 2, 1, 3)[spot]
        for piece in range(PIECES):
            if spot == 0:
                source = near[piece][start : start + rows, :]
            else:
                source = (over[piece], far[piece], far_over[piece])[spot - 1]
            slot = spot * PIECES + piece
            wide[slot] = source.astype(F32)
            copy = pltpu.make_async_copy(wide.at[slot], out.at[shard * PIECES + (piece ^ where.turn)], sems.at[slot])
            copy.start()
            copies.append(copy)
    for copy in copies:
        copy.wait()


def place_pieces(half_axis, layer, scal, *refs):
    wide, sems = refs[-2:]
    where = Where(scal, half_axis)
    sources, outs = refs[:4], refs[-3:-2] if layer is None else refs[-4:-2]
    rows = wide.shape[1]
    for relative, source in enumerate(sources):
        piece = relative ^ where.turn
        for kind in range(2):
            slot = relative * 2 + kind
            target = kind ^ where.modality
            wide[slot] = source[kind * rows : (kind + 1) * rows, :].astype(F32)

            def send(place, slot=slot):
                pltpu.make_async_copy(wide.at[slot], place, sems.at[slot]).start()

            if layer is None:
                send(outs[0].at[target, piece])
            else:
                pl.when(piece < 3)(lambda: send(outs[0].at[target, layer, piece]))
                pl.when(piece == 3)(lambda: send(outs[1].at[target, layer]))
    for slot in range(8):
        landing = outs[0].at[0, 0] if layer is None else outs[1].at[0, layer]
        pltpu.make_async_copy(wide.at[slot], landing, sems.at[slot]).wait()


def pack_small(scal, bias, *refs):
    out = refs[-1]
    width = out.shape[1]
    out[...] = jnp.zeros_like(out)
    for shard in range(4):
        out[shard : shard + 1, :] = bias[:, shard * width : (shard + 1) * width]
    for row, ref in enumerate(refs[:-1]):
        out[4 + row : 5 + row, :] = ref[...]


def add_small(scal, mine, got, out):
    out[...] = jnp.zeros_like(out)
    out[0:2, :] = mine[0:2, :] + got[2:4, :]
    out[4:12, :] = mine[4:12, :] + got[4:12, :]


SELF_ORDER = ("yz", "z")
CROSS_ORDER = ("zy", "y")
ORDER = (
    "branch_x", "branch_core", "act_relay", "ffn_back", "+branch_core", "+act_relay", "+branch_x", "branch_relay",
    "pre_x", "pre_core", "+branch_relay", "down_weights", "down_first", "self_back", "+core", "+down.got",
    "+over", "self_halo", "pre_relay", "down_second", "gate_over", "self_weights", "+halos", "+relay",
    "self_core", "up_weights", "+self.got", "up_first", "self_over", "cross_back", "+gate", "+self.from_x",
    "+down.got", "+up.got", "down_third", "up_second", "small_core", "gate_first", "cross_weights", "up_third",
    "self_rest_over", "+small_got", "united_first", "cross_core", "gate_second", "+cross.got", "down_fourth",
    "+gate.got", "small_over", "+up.other", "cross_over", "self_first", "+down.y", "up_fourth", "+down.z",
    "cross_rest_over", "+cross.from_x", "gate_third", "self_second", "+up.z", "down_fifth", "cross_first",
    "+self.got", "gate_fourth", "+up.y", "cross_halo", "+cross_halos", "united_rest", "self_third",
    "cross_second", "gate_fifth", "+down.far", "up_fifth", "cross_third", "+gate.y", "self_fourth", "+gate.far",
    "cross_fourth", "down_place", "+up.far", "gate_x", "self_fifth", "+self.z", "partner", "cross_fifth",
    "+cross.y", "gate_core", "up_place", "gate_place", "self_place", "cross_place", "partner_end",
)


def body(
    streams, page_lengths, attn_in, attn_out, ffn_in, ffn_bias, ffn_out, out_bias,
    norm_gain, norm_bias, gate_weight, gate_bias, united_grad,
):
    devices = lax.axis_size("dp")
    half_axis = devices // 2
    group_bits = half_axis.bit_length() - 1
    data_index = lax.axis_index("dp")
    place = lax.axis_index("mp")
    modality = data_index // half_axis
    sequence = data_index % half_axis
    turn = data_index % PIECES
    own = streams[0]
    rows, width = own.shape
    keys = rows + 2 * HALO
    shard = attn_in.shape[3]

    def swap(value, axis, mask):
        pairs = [(source, source ^ mask) for source in range(lax.axis_size(axis))]
        return lax.ppermute(value, axis, pairs)

    def mp(value, mask):
        return swap(value, "mp", mask)

    def dp(value, mask):
        return swap(value, "dp", mask)

    count = lax.axis_size("mp")

    def to_next(value):
        return lax.ppermute(value, "mp", [(index, index + 1) for index in range(count - 1)])

    def to_previous(value):
        return lax.ppermute(value, "mp", [(index + 1, index) for index in range(count - 1)])

    def pick(stacked, index):
        return lax.dynamic_index_in_dim(stacked, index, 0, keepdims=False)

    scal = jnp.stack([data_index, place]).astype(jnp.int32)
    clock = [scal]

    def event(*values):
        fenced = lax.optimization_barrier(values + (clock[0],))[:-1]
        return fenced if len(fenced) > 1 else fenced[0]

    def mark(value):
        clock[0] = value
        return value

    def kernel(run, *args, due=()):
        now = after(scal, clock[0], *due)
        results = run(now, *args)
        mark(results[-1] if isinstance(results, (list, tuple)) else results)
        return results

    def add(left, right):
        return (left.astype(F32) + right.astype(F32)).astype(BF)

    def glue(run, outs, *args, due=()):
        def launch(now, *operands):
            return call(
                run, outs, [], 1 << 16, 1 << 18, getattr(run, "func", run).__name__, [SM] + [VM] * len(operands), limit=SMALL_LIMIT
            )(now, *operands)

        return kernel(launch, *args, due=due)

    piece_rows = ffn_in.shape[1] // PIECES
    half_rows = rows // 2
    slice_rows = united_grad.shape[2]

    def attention_piece(layer, index):
        inner = lax.dynamic_slice(
            attn_in, (index, layer, jnp.minimum(turn, 2), 0, 0), (1, 1, 1, shard, width)
        ).reshape(shard, width)
        outer = lax.dynamic_slice(attn_out, (index, layer, 0, 0), (1, 1, shard, width)).reshape(shard, width)
        return jnp.where(turn < 3, inner, outer)

    def group_exchange(blocks):
        moved = jnp.stack([pick(blocks, index ^ sequence) for index in range(half_axis)])
        shape = moved.shape
        for bit in range(group_bits):
            view = moved.reshape((half_axis >> (bit + 1), 2, 1 << bit) + shape[1:])
            got = dp(view[:, 1], 1 << bit)
            moved = jnp.stack([view[:, 0], got], axis=1).reshape(shape)
        return jnp.stack([pick(moved, index ^ sequence) for index in range(half_axis)])

    cross_x = mp(mark(attention_piece(0, modality)), 2)
    partner = dp(own, half_axis)
    self_x = mp(mark(attention_piece(1, event(modality))), 2)
    index = event(modality)
    hidden_part = jnp.stack([
        lax.dynamic_slice(weight, (index, turn * piece_rows, 0), (1, piece_rows, width))[0] for weight in (ffn_in, ffn_out)
    ])
    cross_x, hidden_part = event(cross_x, hidden_part)
    cross_y, cross_z = dp(mark(cross_x), 1), dp(cross_x, 2)
    hidden_x = mp(hidden_part, 2)
    index = event(modality)
    mine = mark(jnp.concatenate([pick(attn_in, index), pick(attn_out, index)[:, None]], axis=1))
    partner, cross_y = event(partner, cross_y)
    partner_left = to_next(partner[rows - HALO :])
    partner_right = to_previous(mark(partner[:HALO]))
    cross_yz = dp(cross_y, 2)
    self_x = mark(event(self_x))
    self_y, self_z = dp(self_x, 1), dp(self_x, 2)
    far = mp(event(mine), 1)
    cross_near = (cross_x, cross_y, cross_z, cross_yz)
    cross_far = tuple(mp(mark(event(piece)), 1) for piece in cross_near)
    index = event(modality)
    hidden_mine = mark(jnp.stack([pick(ffn_in, index), pick(ffn_out, index)]).reshape(2, PIECES, piece_rows, width))
    bias_own = jnp.concatenate([
        lax.dynamic_slice(ffn_bias, (index, (relative ^ turn) * piece_rows), (1, piece_rows)) for relative in range(PIECES)
    ], axis=1)
    params = jnp.concatenate(
        [pick(norm_gain, index), pick(norm_bias, index), pick(out_bias, index)[None], gate_bias[None]], axis=0
    )
    bias_x = mp(mark(bias_own), 2)
    gate_cot_in = mark(group_exchange(event(united_grad[:, 0])).reshape(half_rows, width))
    bias_x = event(bias_x)
    bias_far = mp(mark(jnp.concatenate([bias_own, bias_x], axis=0)), 1)
    hidden_x, self_y, self_z = event(hidden_x, self_y, self_z)
    self_yz = dp(mark(self_z), 1)
    hidden_y, hidden_z = dp(mark(event(hidden_x)), 1), dp(hidden_x, 2)
    self_near_three = tuple(mp(event(piece), 1) for piece in (self_x, self_y, self_z))

    rows_f = struct((rows, width), F32)
    rows_b = struct((rows, width), BF)
    keys_b = struct((keys, width), BF)
    row_f = struct((1, width), F32)
    column_f = struct((rows, 1), F32)
    halo_b = struct((HALO, width), BF)
    half_b = struct((half_rows, width), BF)
    attn_flops = 2 * width * width * (2 * rows + 2 * keys)
    matrix_scratch = [pltpu.VMEM((2, PIECES, shard, width), BF)]

    def attend(now, query_in, left, own_rows, right, resid, layer, near, far_pieces):
        return call(
            functools.partial(attention_forward, half_axis, layer),
            [rows_b, keys_b, keys_b, rows_b, struct((rows, 2 * DH), F32), rows_f, column_f, rows_f, rows_b, halo_b, halo_b],
            [pltpu.VMEM((keys, width), BF)] + matrix_scratch,
            attn_flops, 12 << 20, "attend", [SM, SM] + [VM] * 16,
        )(now, page_lengths, query_in, left, own_rows, right, resid, params, mine, far, *near, *far_pieces)

    cross_q, cross_k, cross_v, cross_o, cross_log, norm_1, inv_1, full_1, low_1, head_1, tail_1 = kernel(
        attend, own, partner_left, partner, partner_right, own, 0, cross_near, cross_far
    )
    self_yz, tail_1, head_1 = event(self_yz, tail_1, head_1)
    left_1 = to_next(mark(tail_1))
    right_1 = to_previous(head_1)
    self_near = (self_x, self_y, self_z, self_yz)
    self_far = self_near_three + (mp(self_yz, 1),)
    left_1, right_1 = event(left_1, right_1)
    hidden_y, hidden_z, left_1 = event(hidden_y, hidden_z, left_1)
    mark(left_1)
    piece_shape = struct((piece_rows, width), BF)
    up_yz = dp(glue(functools.partial(take_half, 0), piece_shape, hidden_y), 2)
    down_yz = dp(glue(functools.partial(take_half, 1), piece_shape, hidden_z), 1)
    hidden_far_mine, hidden_far_x = mp(event(hidden_mine), 1), mp(hidden_x, 1)
    self_q, self_k, self_v, self_o, self_log, norm_2, inv_2, full_2, low_2, _, _ = kernel(
        attend, low_1, left_1, low_1, right_1, full_1, 1, self_near, self_far
    )
    up_yz, down_yz, hidden_far_mine, hidden_far_x = event(up_yz, down_yz, hidden_far_mine, hidden_far_x)
    mark(up_yz)
    hidden_far = (hidden_far_x, mp(hidden_y, 1), mp(hidden_z, 1), mp(up_yz, 1), mp(down_yz, 1))

    hidden = 4 * PIECES * piece_rows
    hidden_weights = (
        hidden_mine, hidden_far_mine, hidden_x, hidden_y, hidden_z, up_yz, down_yz, *hidden_far
    )
    over_b = struct((2, rows, width), BF)

    def feed_forward(now, *args):
        return call(
            functools.partial(ffn_forward, half_axis),
            [rows_b] * 4 + [struct((rows, hidden), F32), rows_f, column_f, half_b, half_b],
            [], 4 * rows * hidden * width, 18 << 20, "feed_forward", [SM] + [VM] * 18,
        )(now, *args)

    low_x, low_core = mp(low_2, 2), mp(low_2, 1)
    act_own, act_x, act_core, act_diagonal, slope, norm_3, inv_3, keep_3, send_3 = kernel(
        feed_forward, low_2, full_2, bias_own, bias_x, bias_far, params, *hidden_weights
    )

    got_3 = dp(send_3, half_axis)
    act_x = mp(event(act_x), 2)
    gate_piece = 2 * width // (4 * PIECES)
    gate_half = struct((2 * PIECES, gate_piece, width), BF)

    def gate_call(now, *args):
        return call(
            functools.partial(gate_kernel, half_axis),
            [half_b, half_b, half_b, gate_half, gate_half, row_f],
            [pltpu.VMEM((2 * width, width), F32)],
            12 * half_rows * width * width, 8 << 20, "gate", [SM, SM] + [VM] * 5,
        )(now, *args)

    united, keep_cot, send_cot, gate_near, gate_far, gate_bias_part = kernel(
        gate_call, page_lengths, keep_3, got_3, gate_weight, params, gate_cot_in, due=(low_core, low_x, act_x)
    )
    got_cot = dp(send_cot, half_axis)
    gate_got = mp(gate_far, 1)
    act_diagonal, act_core, low_sent = event(act_diagonal, act_core, low_x)
    act_diagonal = mp(act_diagonal, 2)
    act_core = mp(act_core, 1)
    low_relay = mp(low_sent, 1)
    gate_sent = glue(sum_sent, struct((PIECES, gate_piece, width), BF), gate_near, gate_got)

    def last_norm(now, *args):
        return call(
            functools.partial(last_norm_backward, half_axis),
            [rows_f, rows_b, row_f, row_f, row_f], [], 1 << 20, 3 << 20, "last_norm_back", [SM] + [VM] * 5,
        )(now, *args)

    back_3, branch, gain_3, shift_3, down_bias_part = kernel(last_norm, keep_cot, got_cot, norm_3, inv_3, params, due=(act_diagonal, act_core, low_relay))

    class Sum:
        def __init__(self, order, last, extra=0, main=piece_rows):
            self.order, self.last, self.main = order, last, main
            self.rows = main + extra
            self.halves = [struct((2, self.rows, width), BF)] * 2

        def core(self, near, far):
            self.near = near
            self.got = mp(mark(event(far)), 1)

        def over(self):
            half = struct((2, piece_rows, width), BF)
            first, self.rest = glue(sum_sent, [half, half], self.near, self.got)
            self.from_x = mp(first, 2)

        def rest_over(self):
            self.rest_x = mp(mark(event(self.rest)), 2)

        def fold(self, *small):
            self.begin(*glue(
                functools.partial(sum_fold, self.order), self.halves, self.near, self.got, self.from_x, self.rest_x, *small
            ))

        def begin(self, keep, send):
            self.keep = keep
            self.got = dp(send, 1 if self.order == "yz" else 2)

        def second(self):
            self.kept, send = glue(
                sum_second, [struct((self.rows, width), F32), struct((self.rows, width), BF)], self.keep, self.got
            )
            self.got = dp(send, 2 if self.order == "yz" else 1)

        def third(self):
            piece = glue(sum_third, struct((self.rows, width), BF), self.kept, self.got)
            for bit in range(2, group_bits):
                piece = add(piece, dp(piece, 1 << bit))
            self.piece = mark(piece)
            self.other = dp(piece, half_axis)

        def fourth(self):
            self.pair = glue(
                functools.partial(join_pair, self.main), struct((2 * self.main or self.rows, width), BF), self.piece, self.other
            )
            self.y, self.z = dp(self.pair, 1), dp(self.pair, 2)

        def fifth(self):
            if self.last == "y":
                self.z = event(self.z)
                self.far = dp(mark(self.z), 1)
            else:
                self.y = event(self.y)
                self.far = dp(mark(self.y), 2)

        def sources(self):
            return self.pair, self.y, self.z, self.far

    down_sum, up_sum, self_sum, cross_sum = Sum("yz", "y"), Sum("zy", "y"), Sum(*SELF_ORDER, 16), Sum(*CROSS_ORDER)
    gate_sum = Sum("zy", "y", gate_piece, 0)
    attn_half = struct((2 * PIECES, shard, width), BF)
    small_shape = struct((16, width), F32)
    wide = [pltpu.VMEM((8, piece_rows, width), F32), pltpu.SemaphoreType.DMA((8,))]

    def ffn_back(now, *args):
        return call(
            functools.partial(ffn_backward, half_axis),
            [rows_f, rows_b, over_b, rows_b, struct((1, hidden), F32)],
            [], 4 * rows * hidden * width, 16 << 20, "feed_forward_back", [SM] + [VM] * 15,
        )(now, *args)

    def weight_product(name, group, now, *args):
        return call(
            functools.partial(rows_product, half_axis, group.order), group.halves,
            [pltpu.VMEM((PIECES, piece_rows, width), BF)], 8 * rows * width * width, 5 << 20, name, [SM] + [VM] * len(args),
        )(now, *args)

    def attend_back(now, same_input, cot_in, halos, normed, inverse, layer, saved, near, far_pieces):
        outs = [rows_f, halo_b, halo_b, row_f, row_f, rows_b, rows_b, keys_b, keys_b] + [rows_f] * (not same_input)
        return call(
            functools.partial(attention_backward, half_axis, layer, same_input),
            outs,
            [
                pltpu.VMEM((2, PIECES, shard, width), BF), pltpu.VMEM((rows, width), BF), pltpu.VMEM((keys, width), F32),
                pltpu.VMEM((keys, width), F32),
            ],
            attn_flops, 14 << 20, "attend_back", [SM, SM] + [VM] * (18 + len(halos)),
        )(now, page_lengths, cot_in, normed, inverse, params, *saved, *halos, mine, far, *near, *far_pieces)

    def attend_weights(now, *args):
        return call(
            functools.partial(attention_weights, half_axis),
            [attn_half, attn_half], [pltpu.VMEM((keys, width), BF)],
            attn_flops, 10 << 20, "attend_weights", [SM] + [VM] * 9,
        )(now, *args)

    def place_hidden(now, *sources):
        return call(
            functools.partial(place_pieces, half_axis, None), struct((2, PIECES, piece_rows, width), F32), wide,
            0, 7 << 20, "place_hidden", [SM] + [VM] * 4, ANY,
        )(now, *sources)

    attn_shapes = [struct((2, 2, 3, shard, width), F32), struct((2, 2, shard, width), F32)]

    def place_layer(now, layer, sources, previous):
        return call(
            functools.partial(place_pieces, half_axis, layer), attn_shapes, wide, 0, 7 << 20, "place_layer",
            [SM] + [VM] * 4 + [ANY] * len(previous), [ANY, ANY], {5: 0, 6: 1} if previous else None,
        )(now, *sources, *previous)

    def place_gate_call(now, *args):
        return call(
            functools.partial(place_gate, half_axis, 0), struct((4 * PIECES, gate_piece, width), F32),
            [pltpu.VMEM((4 * PIECES, gate_piece, width), F32), pltpu.SemaphoreType.DMA((4 * PIECES,))],
            0, 7 << 20, "place_gate", [SM] + [VM] * 7, ANY,
        )(now, *args)

    def small_call(run, shape, name):
        return lambda now, *args: call(
            run, shape, [], 1 << 16, 1 << 18, name, [SM] + [VM] * len(args), limit=SMALL_LIMIT
        )(now, *args)

    got = {"act_diagonal": act_diagonal}

    class Event:
        def act_relay():
            got["act_relay"] = mp(mark(event(got["act_diagonal"])), 1)

        def united_first():
            blocks = united.reshape(half_axis, slice_rows, width)
            moved = jnp.stack([pick(event(blocks), index ^ sequence) for index in range(half_axis)])
            view = moved.reshape((half_axis // 2, 2) + moved.shape[1:])
            got["united"] = view[:, 0], dp(mark(view[:, 1]), 1)

        def united_rest():
            kept, other = event(*got["united"])
            moved = jnp.stack([kept, other], axis=1).reshape(half_axis, slice_rows, width)
            for bit in range(1, group_bits):
                view = moved.reshape((half_axis >> (bit + 1), 2, 1 << bit) + moved.shape[1:])
                moved = jnp.stack([view[:, 0], dp(mark(view[:, 1]), 1 << bit)], axis=1).reshape(moved.shape)
            got["united"] = moved

        def gate_over():
            got["gate"] = mp(mark(event(gate_sent)), 2)

        def branch_x():
            got["branch_x"] = mp(mark(event(branch)), 2)

        def branch_core():
            got["branch_core"] = mp(mark(event(branch)), 1)

        def branch_relay():
            got["branch_x"] = event(got["branch_x"])
            got["branch_relay"] = mp(mark(got["branch_x"]), 1)

        def ffn_back():
            got["cot_2"], got["own"], got["over"], got["core"], got["bias"] = kernel(ffn_back, back_3, branch, slope, *hidden_weights)

        def pre_x():
            got["over"] = mp(mark(event(got["over"])), 2)

        def pre_core():
            got["core"] = mp(mark(event(got["core"])), 1)

        def pre_relay():
            got["over"] = event(got["over"])
            got["relay"] = mp(mark(got["over"]), 1)

        def down_weights():
            got["down"] = kernel(
                functools.partial(weight_product, "down_weights", down_sum), act_own, act_x, act_core, got["act_relay"],
                branch, got["branch_x"], got["branch_core"], got["branch_relay"],
            )

        def up_weights():
            got["up"] = kernel(
                functools.partial(weight_product, "up_weights", up_sum), got["own"], got["over"], got["core"], got["relay"],
                low_2, low_x, low_core, low_relay,
            )

        def self_back():
            got["self"] = kernel(
                attend_back, True, got["cot_2"], (), norm_2, inv_2, 1, (self_q, self_k, self_v, self_log), self_near, self_far
            )

        def self_halo():
            left, right = event(got["self"][1], got["self"][2])
            got["halos"] = to_next(mark(right)), to_previous(left)

        def self_weights():
            low, dq, dk, dv = got["self"][5:9]
            got["self_grads"] = kernel(attend_weights, self_o, low, dq, dk, dv, low_1, left_1, low_1, right_1)

        def self_core():
            self_sum.core(*got["self_grads"])

        def cross_back():
            got["cross"] = kernel(
                attend_back, False, got["self"][0], got["halos"], norm_1, inv_1, 0,
                (cross_q, cross_k, cross_v, cross_log), cross_near, cross_far,
            )

        def cross_halo():
            left, right = event(got["cross"][1], got["cross"][2])
            got["cross_halos"] = to_next(mark(right)), to_previous(left)

        def cross_weights():
            low, dq, dk, dv = got["cross"][5:9]
            got["cross_grads"] = kernel(attend_weights, cross_o, low, dq, dk, dv, own, partner_left, partner, partner_right)

        def cross_core():
            cross_sum.core(*got["cross_grads"])

        def small_core():
            got["small"] = kernel(
                small_call(pack_small, small_shape, "pack_small"), got["bias"],
                got["cross"][3], got["self"][3], gain_3, got["cross"][4], got["self"][4], shift_3, down_bias_part, gate_bias_part,
            )
            got["small_got"] = mp(got["small"], 1)

        def small_over():
            got["small"] = kernel(small_call(add_small, small_shape, "add_small"), got["small"], got["small_got"])
            got["small_got"] = mp(got["small"], 2)

        def self_first():
            self_sum.fold(got["small"], got["small_got"])

        def partner():
            cot = glue(add_halos, rows_b, got["cross"][9], *got["cross_halos"])
            got["partner"] = dp(cot, half_axis)

        def partner_end():
            got["stream"] = glue(add_rows, rows_f, got["cross"][0], got["partner"])[None]

        def down_first():
            down_sum.begin(*got["down"])

        def up_first():
            up_sum.begin(*got["up"])

        def cross_first():
            cross_sum.fold()

        def gate_first():
            gate_sum.begin(*glue(
                functools.partial(gate_fold, gate_sum.order), gate_sum.halves, gate_near, gate_got, got["gate"]
            ))

        def gate_x():
            near = glue(
                functools.partial(take_gate, 0), struct((PIECES, gate_piece, width), BF), *gate_sum.sources()
            )
            got["gate_near"], got["gate_x"] = near, mp(near, 2)

        def gate_core():
            got["gate_x"] = event(got["gate_x"])
            got["gate_core"] = mp(got["gate_near"], 1), mp(mark(got["gate_x"]), 1)

        def gate_place():
            got["gate_grad"] = kernel(place_gate_call, *gate_sum.sources(), got["gate_x"], *got["gate_core"])

        def up_place():
            got["up_grad"] = kernel(place_hidden, *up_sum.sources())

        def down_place():
            got["down_grad"] = kernel(place_hidden, *down_sum.sources())

        def self_place():
            got["attn"] = kernel(place_layer, 1, self_sum.sources(), got.get("attn", ()))

        def cross_place():
            got["attn"] = kernel(place_layer, 0, cross_sum.sources(), got.get("attn", ()))

    groups = {"gate": gate_sum, "down": down_sum, "up": up_sum, "self": self_sum, "cross": cross_sum}
    def arrived(key):
        owner, _, field = key.partition(".")
        holder = vars(groups[owner]) if field else got
        if (field or owner) not in holder:
            return
        value = holder[field or owner]
        if isinstance(value, tuple):
            holder[field or owner] = event(*value)
            mark(holder[field or owner][-1])
        else:
            holder[field or owner] = mark(event(value))

    for name in ORDER:
        if name.startswith("+"):
            arrived(name[1:])
        elif hasattr(Event, name):
            getattr(Event, name)()
        else:
            group, stage = name.split("_", 1)
            getattr(groups[group], stage)()
    united_out = jnp.stack([pick(got["united"], index ^ sequence) for index in range(half_axis)]).astype(F32)

    mine_small = self_sum.piece[shard : shard + 9].astype(F32)
    other_small = self_sum.other[shard : shard + 9].astype(F32)
    is_text = modality == 0
    pair = jnp.stack([jnp.where(is_text, mine_small, other_small), jnp.where(is_text, other_small, mine_small)])
    attn_in_grad, attn_out_grad = got["attn"]
    return (
        united_out[:, None],
        got["stream"],
        attn_in_grad,
        attn_out_grad,
        got["up_grad"].reshape(2, PIECES * piece_rows, width),
        pair[:, 8],
        got["down_grad"].reshape(2, PIECES * piece_rows, width),
        pair[:, 6],
        pair[:, 0:3],
        pair[:, 3:6],
        got["gate_grad"].reshape(2, width, width),
        mine_small[7] + other_small[7],
    )


def solution(mesh):
    placed = (
        P("dp", "mp", None),
        P(),
        P(None, None, None, "mp", None),
        P(None, None, "mp", None),
        P(None, "mp", None),
        P(None, "mp"),
        P(None, "mp", None),
        P(),
        P(),
        P(),
        P(),
        P(),
        P(None, "mp", "dp", None),
    )
    return jax.shard_map(
        body,
        mesh=mesh,
        in_specs=placed,
        out_specs=(
            P(None, "mp", "dp", None),
            P("dp", "mp", None),
            P(None, None, None, "mp", None),
            P(None, None, "mp", None),
            P(None, "mp", None),
            P(None, "mp"),
            P(None, "mp", None),
            P(),
            P(),
            P(),
            P(),
            P(),
        ),
        check_vma=False,
    )
```

```python
import functools

import jax
import jax.numpy as jnp
from jax import lax
from jax.experimental import pallas as pl
from jax.experimental.pallas import tpu as pltpu
from jax.sharding import PartitionSpec as P

DH = 64
L = 1024
PAGES = 16
EPS = 1e-05
SCALE = 0.125
LOG2E = 1.4426950408889634
MASKED = -1e30
HALO = 128
PIECES = 4
BF = jnp.bfloat16
F32 = jnp.float32
VMEM_LIMIT = 16 * 1024 * 1024
SMALL_LIMIT = 4 * 1024 * 1024

VM = pl.BlockSpec(memory_space=pltpu.VMEM)
SM = pl.BlockSpec(memory_space=pltpu.SMEM)
ANY = pl.BlockSpec(memory_space=pl.ANY)


def nn(a, b):
    return lax.dot_general(a, b, (((1,), (0,)), ((), ())), preferred_element_type=F32)


def nt(a, b):
    return lax.dot_general(a, b, (((1,), (1,)), ((), ())), preferred_element_type=F32)


def tn(a, b):
    return lax.dot_general(a, b, (((0,), (0,)), ((), ())), preferred_element_type=F32)


def call(body, outs, scratch=(), flops=0, traffic=0, name=None, specs=None, out_specs=None, aliases=None, limit=VMEM_LIMIT):
    def run(*args):
        return pl.pallas_call(
            body,
            out_shape=outs,
            in_specs=specs if specs is not None else [SM] + [VM] * (len(args) - 1),
            out_specs=out_specs if out_specs is not None else jax.tree.map(lambda _: VM, outs),
            scratch_shapes=list(scratch),
            input_output_aliases=aliases or {},
            compiler_params=pltpu.CompilerParams(vmem_limit_bytes=limit),
            cost_estimate=pl.CostEstimate(flops=flops, bytes_accessed=traffic, transcendentals=0),
            name=name,
        )(*args)

    return run


def struct(shape, dtype):
    return jax.ShapeDtypeStruct(shape, dtype)


def after(value, *deps):
    return lax.optimization_barrier((value,) + deps)[0]


class Where:
    def __init__(self, scal, half_axis):
        self.modality = scal[0] // half_axis
        self.sequence = scal[0] % half_axis
        self.turn = scal[0] % PIECES
        self.place = scal[1]


def page_ends(pages, sequence):
    ends = []
    used = jnp.int32(0)
    running = jnp.int32(0)
    for page in range(PAGES):
        running = running + pages[sequence, page]
        fits = running <= L
        ends.append(jnp.where(fits, running, 2 * L))
        used = jnp.where(fits, running, used)
    return ends, used


def segment_of(position, ends):
    segment = jnp.zeros_like(position)
    for end in ends:
        segment = segment + (end <= position).astype(jnp.int32)
    return segment


def block_bias(ends, base, block, keys):
    query = base + block * HALO + lax.broadcasted_iota(jnp.int32, (HALO, 1), 0)
    key = base + (block - 1) * HALO + lax.broadcasted_iota(jnp.int32, (1, keys), 1)
    query_seg = segment_of(query, ends)
    key_seg = segment_of(key, ends)
    key_seg = jnp.where((key >= 0) & (key < L), key_seg, -1)
    return jnp.where(query_seg == key_seg, 0.0, MASKED)


def normalise(residual, gain, shift):
    center = residual - jnp.mean(residual, axis=-1, keepdims=True)
    inverse = lax.rsqrt(jnp.mean(center * center, axis=-1, keepdims=True) + EPS)
    normed = center * inverse
    return normed * gain + shift, normed, inverse


def norm_back(cot, gain, normed, inverse):
    grad = cot * gain
    back = inverse * (
        grad
        - jnp.mean(grad, axis=-1, keepdims=True)
        - normed * jnp.mean(grad * normed, axis=-1, keepdims=True)
    )
    return back, jnp.sum(cot * normed, axis=0, keepdims=True), jnp.sum(cot, axis=0, keepdims=True)


def attention_matrices(layer, turn, mine, far, near_pieces, far_pieces, pieces):
    for relative in range(PIECES):
        pieces[0, relative ^ turn] = near_pieces[relative][...]
        pieces[1, relative ^ turn] = far_pieces[relative][...]

    def matrix(which):
        return jnp.concatenate([mine[layer, which], pieces[0, which], far[layer, which], pieces[1, which]], axis=0)

    return matrix


def stack_heads(pair, first):
    zero = jnp.zeros_like(pair)
    return jnp.concatenate([jnp.where(first, pair, zero), jnp.where(first, zero, pair)], axis=0)


def extend(left, own, right, extended):
    rows = own.shape[0]
    extended[0:HALO, :] = left[...]
    extended[HALO : HALO + rows, :] = own[...]
    extended[HALO + rows : 2 * HALO + rows, :] = right[...]


def attention_forward(half_axis, layer, *refs):
    scal, pages, query_in, left, own, right, resid, params = refs[:8]
    mine, far, near_pieces, far_pieces = refs[8], refs[9], refs[10:14], refs[14:18]
    q_out, k_out, v_out, o_out, log_out, norm_out, inv_out, full_out, low_out, head_out, tail_out = refs[18:29]
    extended, pieces = refs[29:]
    where = Where(scal, half_axis)
    rows, width = query_in.shape
    window = 3 * HALO
    matrix = attention_matrices(layer, where.turn, mine, far, near_pieces, far_pieces, pieces)
    extend(left, own, right, extended)
    ends, _ = page_ends(pages, where.sequence)
    base = where.place * rows
    q_out[...] = nt(query_in[...], matrix(0)).astype(BF)
    k_out[...] = nt(extended[...], matrix(1)).astype(BF)
    v_out[...] = nt(extended[...], matrix(2)).astype(BF)
    lane = lax.broadcasted_iota(jnp.int32, (1, 2 * DH), 1)
    first = lane < DH
    for block in range(rows // HALO):
        bias = block_bias(ends, base, block, window)
        bias = jnp.concatenate([bias, bias], axis=0)
        row = slice(block * HALO, (block + 1) * HALO)
        span = slice(block * HALO, block * HALO + window)
        logs = jnp.zeros((HALO, 2 * DH), F32)
        for pair in range(width // (2 * DH)):
            cols = slice(pair * 2 * DH, (pair + 1) * 2 * DH)
            scores = nt(stack_heads(q_out[row, cols], first), k_out[span, cols])
            scores = scores * (SCALE * LOG2E) + bias
            top = jnp.max(scores, axis=-1, keepdims=True)
            expo = jnp.exp2(scores - top)
            total = jnp.sum(expo, axis=-1, keepdims=True)
            mixed = nn(expo.astype(BF), v_out[span, cols]) / total
            log = top + jnp.log2(total)
            logs = jnp.where(lane == 2 * pair, log[:HALO], jnp.where(lane == 2 * pair + 1, log[HALO:], logs))
            o_out[row, cols] = jnp.where(first, mixed[:HALO], mixed[HALO:]).astype(BF)
        log_out[row, :] = logs
    residual = resid[...].astype(F32) + nn(o_out[...], matrix(3))
    full, normed, inverse = normalise(residual, params[layer : layer + 1, :], params[3 + layer : 4 + layer, :])
    norm_out[...] = normed
    inv_out[...] = inverse
    full_out[...] = full
    low = full.astype(BF)
    low_out[...] = low
    head_out[...] = low[:HALO]
    tail_out[...] = low[rows - HALO :]


def attention_backward(half_axis, layer, same_input, *refs):
    scal, pages, cot_in, normed, inverse, params = refs[:6]
    q_in, k_in, v_in, log_in = refs[6:10]
    refs = refs[10:]
    halos = ()
    if not same_input:
        halos, refs = refs[:2], refs[2:]
    mine, far, near_pieces, far_pieces = refs[0], refs[1], refs[2:6], refs[6:10]
    refs = refs[10:]
    query_cot, to_left, to_right, gain_out, shift_out, low, dq, dkl, dvl = refs[:9]
    refs = refs[9:]
    if not same_input:
        key_cot, refs = refs[0], refs[1:]
    pieces, o_cot, dk, dv = refs
    where = Where(scal, half_axis)
    rows, width = cot_in.shape
    keys = rows + 2 * HALO
    window = 3 * HALO
    matrix = attention_matrices(layer, where.turn, mine, far, near_pieces, far_pieces, pieces)
    cot = cot_in[...]
    if halos:
        cot = cot + jnp.concatenate([halos[0][...], halos[1][...]], axis=0).astype(F32)
    back, gain_grad, shift_grad = norm_back(cot, params[layer : layer + 1, :], normed[...], inverse[...])
    gain_out[...] = gain_grad
    shift_out[...] = shift_grad
    query_cot[...] = back
    low[...] = back.astype(BF)
    o_cot[...] = nt(low[...], matrix(3)).astype(BF)
    ends, _ = page_ends(pages, where.sequence)
    base = where.place * rows
    lane = lax.broadcasted_iota(jnp.int32, (1, 2 * DH), 1)
    first = lane < DH
    dk[...] = jnp.zeros_like(dk)
    dv[...] = jnp.zeros_like(dv)
    for block in range(rows // HALO):
        bias = block_bias(ends, base, block, window)
        bias = jnp.concatenate([bias, bias], axis=0)
        row = slice(block * HALO, (block + 1) * HALO)
        span = slice(block * HALO, block * HALO + window)
        logs = log_in[row, :]
        for pair in range(width // (2 * DH)):
            cols = slice(pair * 2 * DH, (pair + 1) * 2 * DH)
            queries = stack_heads(q_in[row, cols], first)
            cots = stack_heads(o_cot[row, cols], first)
            key_pair = k_in[span, cols]
            log = jnp.concatenate([logs[:, 2 * pair : 2 * pair + 1], logs[:, 2 * pair + 1 : 2 * pair + 2]], axis=0)
            weights = jnp.exp2(nt(queries, key_pair) * (SCALE * LOG2E) + bias - log)
            weight_cot = nt(cots, v_in[span, cols])
            inner = jnp.sum(weights * weight_cot, axis=-1, keepdims=True)
            score_cot = (weights * (weight_cot - inner)).astype(BF)
            grads = nn(score_cot, key_pair)
            dq[row, cols] = (jnp.where(first, grads[:HALO], grads[HALO:]) * SCALE).astype(BF)
            dk[span, cols] += tn(score_cot, queries)
            dv[span, cols] += tn(weights.astype(BF), cots)
    dkl[...] = (dk[...] * SCALE).astype(BF)
    dvl[...] = dv[...].astype(BF)
    back = nn(dkl[...], matrix(1)) + nn(dvl[...], matrix(2))
    to_left[...] = back[0:HALO, :].astype(BF)
    to_right[...] = back[HALO + rows : keys, :].astype(BF)
    middle = back[HALO : HALO + rows, :]
    direct = nn(dq[...], matrix(0))
    if same_input:
        query_cot[...] += direct + middle
    else:
        query_cot[...] += direct
        key_cot[...] = middle


def attention_weights(half_axis, scal, o_in, low, dq, dk, dv, query_in, left, own, right, near_out, far_out, extended):
    turn = Where(scal, half_axis).turn
    extend(left, own, right, extended)
    piece = near_out.shape[1]
    jobs = ((0, dq, query_in), (1, dk, extended), (2, dv, extended), (3, o_in, low))
    for which, cots, inputs in jobs:
        value = tn(cots[...], inputs[...]).astype(BF)
        for place, (target, start) in enumerate(((near_out, 0), (near_out, PIECES), (far_out, 0), (far_out, PIECES))):
            target[start + (which ^ turn)] = value[place * piece : (place + 1) * piece]


def gelu_parts(value):
    root = 0.7978845608028654
    square = value * value
    inner = jnp.tanh(root * (value + 0.044715 * value * square))
    half = 0.5 * (1.0 + inner)
    slope = half + 0.5 * value * (1.0 - inner * inner) * (root * (1.0 + 3.0 * 0.044715 * square))
    return value * half, slope


def hidden_matrices(turn, refs):
    whole, pieces = (refs[0], refs[1]), (refs[2:7], refs[7:12])

    def matrix(kind, place):
        if place % 2 == 0:
            parts = [whole[place // 2][kind, relative ^ turn] for relative in range(PIECES)]
        else:
            x, y, z, *last = pieces[place // 2]
            parts = [x[kind], y[kind], z[kind], last[kind][...]]
        return jnp.concatenate(parts, axis=0)

    return matrix


def ffn_forward(half_axis, *refs):
    scal, low, full, bias_own, bias_x, bias_far, params = refs[:7]
    acts, (slope_out, norm_out, inv_out, keep_out, send_out) = refs[19:23], refs[23:28]
    where = Where(scal, half_axis)
    matrix = hidden_matrices(where.turn, refs[7:19])
    rows, width = low.shape
    total = full[...] + params[6:7, :]
    biases = (bias_own[...], bias_x[...], bias_far[0:1, :], bias_far[1:2, :])
    for place in range(4):
        cols = slice(place * width, (place + 1) * width)
        pre = nt(low[...], matrix(0, place)) + biases[place]
        value, slope = gelu_parts(pre)
        value = value.astype(BF)
        acts[place][...] = value
        slope_out[:, cols] = slope
        total = total + nn(value, matrix(1, place))
    out, normed, inverse = normalise(total, params[2:3, :], params[5:6, :])
    norm_out[...] = normed
    inv_out[...] = inverse
    out = out.astype(BF)
    half = rows // 2
    is_text = where.modality == 0
    keep_out[...] = jnp.where(is_text, out[:half], out[half:])
    send_out[...] = jnp.where(is_text, out[half:], out[:half])


def last_norm_backward(half_axis, scal, keep, got, normed, inverse, params, back_out, branch_out, gain_out, shift_out, bias_out):
    where = Where(scal, half_axis)
    is_text = where.modality == 0
    kept, other = keep[...], got[...]
    cot = jnp.concatenate([jnp.where(is_text, kept, other), jnp.where(is_text, other, kept)], axis=0).astype(F32)
    back, gain_grad, shift_grad = norm_back(cot, params[2:3, :], normed[...], inverse[...])
    back_out[...] = back
    branch_out[...] = back.astype(BF)
    gain_out[...] = gain_grad
    shift_out[...] = shift_grad
    bias_out[...] = jnp.sum(back, axis=0, keepdims=True)


def ffn_backward(half_axis, *refs):
    scal, back, branch, slope = refs[:4]
    cot_out, pre_own, pre_over, pre_core, bias_out = refs[16:21]
    where = Where(scal, half_axis)
    matrix = hidden_matrices(where.turn, refs[4:16])
    rows, width = branch.shape
    total = back[...]
    for place in range(4):
        cols = slice(place * width, (place + 1) * width)
        act_cot = nt(branch[...], matrix(1, place))
        pre_cot = (act_cot * slope[:, cols]).astype(BF)
        if place % 2 == 0:
            (pre_own, pre_core)[place // 2][...] = pre_cot
        else:
            pre_over[place // 2] = pre_cot
        bias_out[:, cols] = jnp.sum(pre_cot.astype(F32), axis=0, keepdims=True)
        total = total + nn(pre_cot, matrix(0, place))
    cot_out[...] = total


def split_piece(order, relative):
    return (relative % 2, relative // 2) if order == "yz" else (relative // 2, relative % 2)


def rows_product(half_axis, order, scal, left_own, left_over, left_core, left_relay, *refs):
    rights, (keep, send, parts) = refs[:4], refs[4:]
    total = tn(left_own[...], rights[0][...])
    if len(left_over.shape) == 3:
        left_over, left_relay = left_over.at[0], left_relay.at[1]
    for left, right in ((left_over[...], rights[1]), (left_core[...], rights[2]), (left_relay[...], rights[3])):
        total = total + tn(left, right[...])
    rows = parts.shape[1]
    for piece in range(PIECES):
        parts[piece] = total[piece * rows : (piece + 1) * rows].astype(BF)
    for relative in range(PIECES):
        side, index = split_piece(order, relative)
        target = (keep, send)[side]
        target[index, 0:rows, :] = parts[relative]


def sum_sent(scal, near, got, *outs):
    start = PIECES
    for out in outs:
        stop = start + out.shape[0]
        out[...] = (near[start:stop].astype(F32) + got[start:stop].astype(F32)).astype(BF)
        start = stop


def canonical(row, turn, piece):
    row = jnp.broadcast_to(row, (8, row.shape[1]))
    lane = lax.broadcasted_iota(jnp.int32, row.shape, 1)
    width = row.shape[1]
    swapped = jnp.where((lane // piece) % 2 == 0, pltpu.roll(row, width - piece, 1), pltpu.roll(row, piece, 1))
    row = jnp.where(turn % 2 == 1, swapped, row)
    return jnp.where(turn // 2 == 1, pltpu.roll(row, 2 * piece, 1), row)[0:1]


def sum_fold(order, scal, near, got, over_a, over_b, *refs):
    keep, send = refs[-2:]
    rows = near.shape[1]
    small = None
    if len(refs) > 2:
        mine, other = refs[:2]
        total = mine[4:12, :] + other[4:12, :]
        bias = canonical(mine[0:1, :] + other[1:2, :], scal[0] % PIECES, rows)
        small = jnp.concatenate([total, bias, jnp.zeros((7, total.shape[1]), F32)], axis=0).astype(BF)
    for relative in range(PIECES):
        side, index = split_piece(order, relative)
        target = (keep, send)[side]
        over = (over_a, over_b)[relative // 2][relative % 2]
        summed = near[relative].astype(F32) + got[relative].astype(F32) + over.astype(F32)
        target[index, 0:rows, :] = summed.astype(BF)
        if small is not None:
            target[index, rows : rows + 16, :] = small


def gate_fold(order, scal, near, got, over, keep, send):
    for relative in range(PIECES):
        side, index = split_piece(order, relative)
        summed = near[relative].astype(F32) + got[relative].astype(F32) + over[relative].astype(F32)
        (keep, send)[side][index] = summed.astype(BF)


def sum_second(scal, keep, got, kept, send):
    kept[...] = keep[0].astype(F32) + got[0].astype(F32)
    send[...] = (keep[1].astype(F32) + got[1].astype(F32)).astype(BF)


def sum_third(scal, kept, got, piece):
    piece[...] = (kept[...] + got[...].astype(F32)).astype(BF)


def join_pair(rows, scal, piece, other, pair):
    if rows:
        pair[0:rows, :] = piece[0:rows, :]
        pair[rows : 2 * rows, :] = other[0:rows, :]
    else:
        pair[...] = (piece[...].astype(F32) + other[...].astype(F32)).astype(BF)


def take_gate(start, scal, *refs):
    for piece, source in enumerate(refs[:PIECES]):
        refs[PIECES][piece] = source[start:, :]


def take_half(kind, scal, source, out):
    out[...] = source[kind]


def add_halos(scal, middle, left, right, out):
    out[0:HALO, :] = (middle[0:HALO, :] + left[...].astype(F32)).astype(BF)
    out[HALO:, :] = (middle[HALO:, :] + right[...].astype(F32)).astype(BF)


def add_rows(scal, left, right, out):
    out[...] = left[...] + right[...].astype(F32)


def gate_kernel(
    half_axis, scal, pages, keep, got, weight, params, cot_in,
    united, keep_out, send_out, near_out, far_out, bias_out, grads,
):
    where = Where(scal, half_axis)
    is_text = where.modality == 0
    kept, other = keep[...], got[...]
    text_low = jnp.where(is_text, kept, other)
    vision_low = jnp.where(is_text, other, kept)
    half, width = kept.shape
    _, used = page_ends(pages, where.sequence)
    position = where.place * (2 * half) + where.modality * half + lax.broadcasted_iota(jnp.int32, (half, 1), 0)
    mask = (position < used).astype(F32)
    gate = jax.nn.sigmoid(nt(text_low, weight[0]) + nt(vision_low, weight[1]) + params[7:8, :])
    text_full = text_low.astype(F32)
    vision_full = vision_low.astype(F32)
    united[...] = (mask * (gate * text_full + (1.0 - gate) * vision_full)).astype(BF)
    cot = cot_in[...].astype(F32) * mask
    gate_cot = (cot * (text_full - vision_full) * gate * (1.0 - gate)).astype(BF)
    text_cot = (cot * gate + nn(gate_cot, weight[0])).astype(BF)
    vision_cot = (cot * (1.0 - gate) + nn(gate_cot, weight[1])).astype(BF)
    keep_out[...] = jnp.where(is_text, text_cot, vision_cot)
    send_out[...] = jnp.where(is_text, vision_cot, text_cot)
    bias_out[...] = jnp.sum(gate_cot.astype(F32), axis=0, keepdims=True)
    grads[0:width, :] = tn(gate_cot, text_low)
    grads[width : 2 * width, :] = tn(gate_cot, vision_low)
    rows = near_out.shape[1]
    for spot, (target, start) in enumerate(((near_out, 0), (near_out, PIECES), (far_out, 0), (far_out, PIECES))):
        shard = where.place ^ (0, 2, 1, 3)[spot]
        for piece in range(PIECES):
            at = pl.multiple_of((shard * PIECES + (piece ^ where.turn)) * rows, rows)
            target[start + piece] = grads[pl.ds(at, rows), :].astype(BF)


def place_gate(half_axis, start, scal, *refs):
    near, over, far, far_over, out, wide, sems = refs[:4], *refs[4:]
    where = Where(scal, half_axis)
    rows = over.shape[1]
    copies = []
    for spot in range(4):
        shard = where.place ^ (0, 2, 1, 3)[spot]
        for piece in range(PIECES):
            if spot == 0:
                source = near[piece][start : start + rows, :]
            else:
                source = (over[piece], far[piece], far_over[piece])[spot - 1]
            slot = spot * PIECES + piece
            wide[slot] = source.astype(F32)
            copy = pltpu.make_async_copy(wide.at[slot], out.at[shard * PIECES + (piece ^ where.turn)], sems.at[slot])
            copy.start()
            copies.append(copy)
    for copy in copies:
        copy.wait()


def place_pieces(half_axis, layer, scal, *refs):
    wide, sems = refs[-2:]
    where = Where(scal, half_axis)
    sources, outs = refs[:4], refs[-3:-2] if layer is None else refs[-4:-2]
    rows = wide.shape[1]
    for relative, source in enumerate(sources):
        piece = relative ^ where.turn
        for kind in range(2):
            slot = relative * 2 + kind
            target = kind ^ where.modality
            wide[slot] = source[kind * rows : (kind + 1) * rows, :].astype(F32)

            def send(place, slot=slot):
                pltpu.make_async_copy(wide.at[slot], place, sems.at[slot]).start()

            if layer is None:
                send(outs[0].at[target, piece])
            else:
                pl.when(piece < 3)(lambda: send(outs[0].at[target, layer, piece]))
                pl.when(piece == 3)(lambda: send(outs[1].at[target, layer]))
    for slot in range(8):
        landing = outs[0].at[0, 0] if layer is None else outs[1].at[0, layer]
        pltpu.make_async_copy(wide.at[slot], landing, sems.at[slot]).wait()


def pack_small(scal, bias, *refs):
    out = refs[-1]
    width = out.shape[1]
    out[...] = jnp.zeros_like(out)
    for shard in range(4):
        out[shard : shard + 1, :] = bias[:, shard * width : (shard + 1) * width]
    for row, ref in enumerate(refs[:-1]):
        out[4 + row : 5 + row, :] = ref[...]


def add_small(scal, mine, got, out):
    out[...] = jnp.zeros_like(out)
    out[0:2, :] = mine[0:2, :] + got[2:4, :]
    out[4:12, :] = mine[4:12, :] + got[4:12, :]


SELF_ORDER = ("yz", "z")
CROSS_ORDER = ("zy", "y")
ORDER = (
    "branch_x", "branch_core", "act_relay", "ffn_back", "+branch_core", "+act_relay", "+branch_x", "branch_relay",
    "pre_x", "pre_core", "+branch_relay", "down_weights", "down_first", "self_back", "+core", "+down.got",
    "+over", "self_halo", "pre_relay", "down_second", "gate_over", "self_weights", "+halos", "+relay",
    "self_core", "up_weights", "+self.got", "up_first", "self_over", "cross_back", "+gate", "+self.from_x",
    "+down.got", "+up.got", "self_rest_over", "down_third", "up_second", "small_core", "gate_first", "small_over",
    "cross_weights", "up_third", "+small_got", "united_first", "cross_core", "gate_second", "+cross.got",
    "down_fourth", "+gate.got", "+up.other", "cross_over", "self_first", "+down.y", "up_fourth", "+down.z",
    "cross_rest_over", "+cross.from_x", "gate_third", "self_second", "+up.z", "down_fifth", "cross_first",
    "+self.got", "gate_fourth", "+up.y", "cross_halo", "+cross_halos", "united_rest", "self_third",
    "cross_second", "gate_fifth", "+down.far", "up_fifth", "cross_third", "+gate.y", "self_fourth", "+gate.far",
    "cross_fourth", "down_place", "+up.far", "gate_x", "self_fifth", "+self.z", "partner", "cross_fifth",
    "+cross.y", "gate_core", "up_place", "gate_place", "self_place", "cross_place", "partner_end",
)


def body(
    streams, page_lengths, attn_in, attn_out, ffn_in, ffn_bias, ffn_out, out_bias,
    norm_gain, norm_bias, gate_weight, gate_bias, united_grad,
):
    devices = lax.axis_size("dp")
    half_axis = devices // 2
    group_bits = half_axis.bit_length() - 1
    data_index = lax.axis_index("dp")
    place = lax.axis_index("mp")
    modality = data_index // half_axis
    sequence = data_index % half_axis
    turn = data_index % PIECES
    own = streams[0]
    rows, width = own.shape
    keys = rows + 2 * HALO
    shard = attn_in.shape[3]

    def swap(value, axis, mask):
        pairs = [(source, source ^ mask) for source in range(lax.axis_size(axis))]
        return lax.ppermute(value, axis, pairs)

    def mp(value, mask):
        return swap(value, "mp", mask)

    def dp(value, mask):
        return swap(value, "dp", mask)

    count = lax.axis_size("mp")

    def to_next(value):
        return lax.ppermute(value, "mp", [(index, index + 1) for index in range(count - 1)])

    def to_previous(value):
        return lax.ppermute(value, "mp", [(index + 1, index) for index in range(count - 1)])

    def pick(stacked, index):
        return lax.dynamic_index_in_dim(stacked, index, 0, keepdims=False)

    scal = jnp.stack([data_index, place]).astype(jnp.int32)
    clock = [scal]

    def event(*values):
        fenced = lax.optimization_barrier(values + (clock[0],))[:-1]
        return fenced if len(fenced) > 1 else fenced[0]

    def mark(value):
        clock[0] = value
        return value

    def kernel(run, *args, due=()):
        now = after(scal, clock[0], *due)
        results = run(now, *args)
        mark(results[-1] if isinstance(results, (list, tuple)) else results)
        return results

    def add(left, right):
        return (left.astype(F32) + right.astype(F32)).astype(BF)

    def glue(run, outs, *args, due=()):
        def launch(now, *operands):
            return call(
                run, outs, [], 1 << 16, 1 << 18, getattr(run, "func", run).__name__, [SM] + [VM] * len(operands), limit=SMALL_LIMIT
            )(now, *operands)

        return kernel(launch, *args, due=due)

    piece_rows = ffn_in.shape[1] // PIECES
    half_rows = rows // 2
    slice_rows = united_grad.shape[2]

    def attention_piece(layer, index):
        inner = lax.dynamic_slice(
            attn_in, (index, layer, jnp.minimum(turn, 2), 0, 0), (1, 1, 1, shard, width)
        ).reshape(shard, width)
        outer = lax.dynamic_slice(attn_out, (index, layer, 0, 0), (1, 1, shard, width)).reshape(shard, width)
        return jnp.where(turn < 3, inner, outer)

    def group_exchange(blocks):
        moved = jnp.stack([pick(blocks, index ^ sequence) for index in range(half_axis)])
        shape = moved.shape
        for bit in range(group_bits):
            view = moved.reshape((half_axis >> (bit + 1), 2, 1 << bit) + shape[1:])
            got = dp(view[:, 1], 1 << bit)
            moved = jnp.stack([view[:, 0], got], axis=1).reshape(shape)
        return jnp.stack([pick(moved, index ^ sequence) for index in range(half_axis)])

    cross_x = mp(mark(attention_piece(0, modality)), 2)
    partner = dp(own, half_axis)
    self_x = mp(mark(attention_piece(1, event(modality))), 2)
    index = event(modality)
    hidden_part = jnp.stack([
        lax.dynamic_slice(weight, (index, turn * piece_rows, 0), (1, piece_rows, width))[0] for weight in (ffn_in, ffn_out)
    ])
    cross_x, hidden_part = event(cross_x, hidden_part)
    cross_y, cross_z = dp(mark(cross_x), 1), dp(cross_x, 2)
    hidden_x = mp(hidden_part, 2)
    index = event(modality)
    mine = mark(jnp.concatenate([pick(attn_in, index), pick(attn_out, index)[:, None]], axis=1))
    partner, cross_y = event(partner, cross_y)
    partner_left = to_next(partner[rows - HALO :])
    partner_right = to_previous(mark(partner[:HALO]))
    cross_yz = dp(cross_y, 2)
    self_x = mark(event(self_x))
    self_y, self_z = dp(self_x, 1), dp(self_x, 2)
    far = mp(event(mine), 1)
    cross_near = (cross_x, cross_y, cross_z, cross_yz)
    cross_far = tuple(mp(mark(event(piece)), 1) for piece in cross_near)
    index = event(modality)
    hidden_mine = mark(jnp.stack([pick(ffn_in, index), pick(ffn_out, index)]).reshape(2, PIECES, piece_rows, width))
    bias_own = jnp.concatenate([
        lax.dynamic_slice(ffn_bias, (index, (relative ^ turn) * piece_rows), (1, piece_rows)) for relative in range(PIECES)
    ], axis=1)
    params = jnp.concatenate(
        [pick(norm_gain, index), pick(norm_bias, index), pick(out_bias, index)[None], gate_bias[None]], axis=0
    )
    bias_x = mp(mark(bias_own), 2)
    gate_cot_in = mark(group_exchange(event(united_grad[:, 0])).reshape(half_rows, width))
    bias_x = event(bias_x)
    bias_far = mp(mark(jnp.concatenate([bias_own, bias_x], axis=0)), 1)
    hidden_x, self_y, self_z = event(hidden_x, self_y, self_z)
    self_yz = dp(mark(self_z), 1)
    hidden_y, hidden_z = dp(mark(event(hidden_x)), 1), dp(hidden_x, 2)
    self_near_three = tuple(mp(event(piece), 1) for piece in (self_x, self_y, self_z))

    rows_f = struct((rows, width), F32)
    rows_b = struct((rows, width), BF)
    keys_b = struct((keys, width), BF)
    row_f = struct((1, width), F32)
    column_f = struct((rows, 1), F32)
    halo_b = struct((HALO, width), BF)
    half_b = struct((half_rows, width), BF)
    attn_flops = 2 * width * width * (2 * rows + 2 * keys)
    matrix_scratch = [pltpu.VMEM((2, PIECES, shard, width), BF)]

    def attend(now, query_in, left, own_rows, right, resid, layer, near, far_pieces):
        return call(
            functools.partial(attention_forward, half_axis, layer),
            [rows_b, keys_b, keys_b, rows_b, struct((rows, 2 * DH), F32), rows_f, column_f, rows_f, rows_b, halo_b, halo_b],
            [pltpu.VMEM((keys, width), BF)] + matrix_scratch,
            attn_flops, 12 << 20, "attend", [SM, SM] + [VM] * 16,
        )(now, page_lengths, query_in, left, own_rows, right, resid, params, mine, far, *near, *far_pieces)

    cross_q, cross_k, cross_v, cross_o, cross_log, norm_1, inv_1, full_1, low_1, head_1, tail_1 = kernel(
        attend, own, partner_left, partner, partner_right, own, 0, cross_near, cross_far
    )
    self_yz, tail_1, head_1 = event(self_yz, tail_1, head_1)
    left_1 = to_next(mark(tail_1))
    right_1 = to_previous(head_1)
    self_near = (self_x, self_y, self_z, self_yz)
    self_far = self_near_three + (mp(self_yz, 1),)
    left_1, right_1 = event(left_1, right_1)
    hidden_y, hidden_z, left_1 = event(hidden_y, hidden_z, left_1)
    mark(left_1)
    piece_shape = struct((piece_rows, width), BF)
    up_yz = dp(glue(functools.partial(take_half, 0), piece_shape, hidden_y), 2)
    down_yz = dp(glue(functools.partial(take_half, 1), piece_shape, hidden_z), 1)
    hidden_far_mine, hidden_far_x = mp(event(hidden_mine), 1), mp(hidden_x, 1)
    self_q, self_k, self_v, self_o, self_log, norm_2, inv_2, full_2, low_2, _, _ = kernel(
        attend, low_1, left_1, low_1, right_1, full_1, 1, self_near, self_far
    )
    up_yz, down_yz, hidden_far_mine, hidden_far_x = event(up_yz, down_yz, hidden_far_mine, hidden_far_x)
    mark(up_yz)
    hidden_far = (hidden_far_x, mp(hidden_y, 1), mp(hidden_z, 1), mp(up_yz, 1), mp(down_yz, 1))

    hidden = 4 * PIECES * piece_rows
    hidden_weights = (
        hidden_mine, hidden_far_mine, hidden_x, hidden_y, hidden_z, up_yz, down_yz, *hidden_far
    )
    over_b = struct((2, rows, width), BF)

    def feed_forward(now, *args):
        return call(
            functools.partial(ffn_forward, half_axis),
            [rows_b] * 4 + [struct((rows, hidden), F32), rows_f, column_f, half_b, half_b],
            [], 4 * rows * hidden * width, 18 << 20, "feed_forward", [SM] + [VM] * 18,
        )(now, *args)

    low_x, low_core = mp(low_2, 2), mp(low_2, 1)
    act_own, act_x, act_core, act_diagonal, slope, norm_3, inv_3, keep_3, send_3 = kernel(
        feed_forward, low_2, full_2, bias_own, bias_x, bias_far, params, *hidden_weights
    )

    got_3 = dp(send_3, half_axis)
    act_x = mp(event(act_x), 2)
    gate_piece = 2 * width // (4 * PIECES)
    gate_half = struct((2 * PIECES, gate_piece, width), BF)

    def gate_call(now, *args):
        return call(
            functools.partial(gate_kernel, half_axis),
            [half_b, half_b, half_b, gate_half, gate_half, row_f],
            [pltpu.VMEM((2 * width, width), F32)],
            12 * half_rows * width * width, 8 << 20, "gate", [SM, SM] + [VM] * 5,
        )(now, *args)

    united, keep_cot, send_cot, gate_near, gate_far, gate_bias_part = kernel(
        gate_call, page_lengths, keep_3, got_3, gate_weight, params, gate_cot_in, due=(low_core, low_x, act_x)
    )
    got_cot = dp(send_cot, half_axis)
    gate_got = mp(gate_far, 1)
    act_diagonal, act_core, low_sent = event(act_diagonal, act_core, low_x)
    act_diagonal = mp(act_diagonal, 2)
    act_core = mp(act_core, 1)
    low_relay = mp(low_sent, 1)
    gate_sent = glue(sum_sent, struct((PIECES, gate_piece, width), BF), gate_near, gate_got)

    def last_norm(now, *args):
        return call(
            functools.partial(last_norm_backward, half_axis),
            [rows_f, rows_b, row_f, row_f, row_f], [], 1 << 20, 3 << 20, "last_norm_back", [SM] + [VM] * 5,
        )(now, *args)

    back_3, branch, gain_3, shift_3, down_bias_part = kernel(last_norm, keep_cot, got_cot, norm_3, inv_3, params, due=(act_diagonal, act_core, low_relay))

    class Sum:
        def __init__(self, order, last, extra=0, main=piece_rows):
            self.order, self.last, self.main = order, last, main
            self.rows = main + extra
            self.halves = [struct((2, self.rows, width), BF)] * 2

        def core(self, near, far):
            self.near = near
            self.got = mp(mark(event(far)), 1)

        def over(self):
            half = struct((2, piece_rows, width), BF)
            first, self.rest = glue(sum_sent, [half, half], self.near, self.got)
            self.from_x = mp(first, 2)

        def rest_over(self):
            self.rest_x = mp(mark(event(self.rest)), 2)

        def fold(self, *small):
            self.begin(*glue(
                functools.partial(sum_fold, self.order), self.halves, self.near, self.got, self.from_x, self.rest_x, *small
            ))

        def begin(self, keep, send):
            self.keep = keep
            self.got = dp(send, 1 if self.order == "yz" else 2)

        def second(self):
            self.kept, send = glue(
                sum_second, [struct((self.rows, width), F32), struct((self.rows, width), BF)], self.keep, self.got
            )
            self.got = dp(send, 2 if self.order == "yz" else 1)

        def third(self):
            piece = glue(sum_third, struct((self.rows, width), BF), self.kept, self.got)
            for bit in range(2, group_bits):
                piece = add(piece, dp(piece, 1 << bit))
            self.piece = mark(piece)
            self.other = dp(piece, half_axis)

        def fourth(self):
            self.pair = glue(
                functools.partial(join_pair, self.main), struct((2 * self.main or self.rows, width), BF), self.piece, self.other
            )
            self.y, self.z = dp(self.pair, 1), dp(self.pair, 2)

        def fifth(self):
            if self.last == "y":
                self.z = event(self.z)
                self.far = dp(mark(self.z), 1)
            else:
                self.y = event(self.y)
                self.far = dp(mark(self.y), 2)

        def sources(self):
            return self.pair, self.y, self.z, self.far

    down_sum, up_sum, self_sum, cross_sum = Sum("yz", "y"), Sum("zy", "y"), Sum(*SELF_ORDER, 16), Sum(*CROSS_ORDER)
    gate_sum = Sum("zy", "y", gate_piece, 0)
    attn_half = struct((2 * PIECES, shard, width), BF)
    small_shape = struct((16, width), F32)
    wide = [pltpu.VMEM((8, piece_rows, width), F32), pltpu.SemaphoreType.DMA((8,))]

    def ffn_back(now, *args):
        return call(
            functools.partial(ffn_backward, half_axis),
            [rows_f, rows_b, over_b, rows_b, struct((1, hidden), F32)],
            [], 4 * rows * hidden * width, 16 << 20, "feed_forward_back", [SM] + [VM] * 15,
        )(now, *args)

    def weight_product(name, group, now, *args):
        return call(
            functools.partial(rows_product, half_axis, group.order), group.halves,
            [pltpu.VMEM((PIECES, piece_rows, width), BF)], 8 * rows * width * width, 5 << 20, name, [SM] + [VM] * len(args),
        )(now, *args)

    def attend_back(now, same_input, cot_in, halos, normed, inverse, layer, saved, near, far_pieces):
        outs = [rows_f, halo_b, halo_b, row_f, row_f, rows_b, rows_b, keys_b, keys_b] + [rows_f] * (not same_input)
        return call(
            functools.partial(attention_backward, half_axis, layer, same_input),
            outs,
            [
                pltpu.VMEM((2, PIECES, shard, width), BF), pltpu.VMEM((rows, width), BF), pltpu.VMEM((keys, width), F32),
                pltpu.VMEM((keys, width), F32),
            ],
            attn_flops, 14 << 20, "attend_back", [SM, SM] + [VM] * (18 + len(halos)),
        )(now, page_lengths, cot_in, normed, inverse, params, *saved, *halos, mine, far, *near, *far_pieces)

    def attend_weights(now, *args):
        return call(
            functools.partial(attention_weights, half_axis),
            [attn_half, attn_half], [pltpu.VMEM((keys, width), BF)],
            attn_flops, 10 << 20, "attend_weights", [SM] + [VM] * 9,
        )(now, *args)

    def place_hidden(now, *sources):
        return call(
            functools.partial(place_pieces, half_axis, None), struct((2, PIECES, piece_rows, width), F32), wide,
            0, 7 << 20, "place_hidden", [SM] + [VM] * 4, ANY,
        )(now, *sources)

    attn_shapes = [struct((2, 2, 3, shard, width), F32), struct((2, 2, shard, width), F32)]

    def place_layer(now, layer, sources, previous):
        return call(
            functools.partial(place_pieces, half_axis, layer), attn_shapes, wide, 0, 7 << 20, "place_layer",
            [SM] + [VM] * 4 + [ANY] * len(previous), [ANY, ANY], {5: 0, 6: 1} if previous else None,
        )(now, *sources, *previous)

    def place_gate_call(now, *args):
        return call(
            functools.partial(place_gate, half_axis, 0), struct((4 * PIECES, gate_piece, width), F32),
            [pltpu.VMEM((4 * PIECES, gate_piece, width), F32), pltpu.SemaphoreType.DMA((4 * PIECES,))],
            0, 7 << 20, "place_gate", [SM] + [VM] * 7, ANY,
        )(now, *args)

    def small_call(run, shape, name):
        return lambda now, *args: call(
            run, shape, [], 1 << 16, 1 << 18, name, [SM] + [VM] * len(args), limit=SMALL_LIMIT
        )(now, *args)

    got = {"act_diagonal": act_diagonal}

    class Event:
        def act_relay():
            got["act_relay"] = mp(mark(event(got["act_diagonal"])), 1)

        def united_first():
            blocks = united.reshape(half_axis, slice_rows, width)
            moved = jnp.stack([pick(event(blocks), index ^ sequence) for index in range(half_axis)])
            view = moved.reshape((half_axis // 2, 2) + moved.shape[1:])
            got["united"] = view[:, 0], dp(mark(view[:, 1]), 1)

        def united_rest():
            kept, other = event(*got["united"])
            moved = jnp.stack([kept, other], axis=1).reshape(half_axis, slice_rows, width)
            for bit in range(1, group_bits):
                view = moved.reshape((half_axis >> (bit + 1), 2, 1 << bit) + moved.shape[1:])
                moved = jnp.stack([view[:, 0], dp(mark(view[:, 1]), 1 << bit)], axis=1).reshape(moved.shape)
            got["united"] = moved

        def gate_over():
            got["gate"] = mp(mark(event(gate_sent)), 2)

        def branch_x():
            got["branch_x"] = mp(mark(event(branch)), 2)

        def branch_core():
            got["branch_core"] = mp(mark(event(branch)), 1)

        def branch_relay():
            got["branch_x"] = event(got["branch_x"])
            got["branch_relay"] = mp(mark(got["branch_x"]), 1)

        def ffn_back():
            got["cot_2"], got["own"], got["over"], got["core"], got["bias"] = kernel(ffn_back, back_3, branch, slope, *hidden_weights)

        def pre_x():
            got["over"] = mp(mark(event(got["over"])), 2)

        def pre_core():
            got["core"] = mp(mark(event(got["core"])), 1)

        def pre_relay():
            got["over"] = event(got["over"])
            got["relay"] = mp(mark(got["over"]), 1)

        def down_weights():
            got["down"] = kernel(
                functools.partial(weight_product, "down_weights", down_sum), act_own, act_x, act_core, got["act_relay"],
                branch, got["branch_x"], got["branch_core"], got["branch_relay"],
            )

        def up_weights():
            got["up"] = kernel(
                functools.partial(weight_product, "up_weights", up_sum), got["own"], got["over"], got["core"], got["relay"],
                low_2, low_x, low_core, low_relay,
            )

        def self_back():
            got["self"] = kernel(
                attend_back, True, got["cot_2"], (), norm_2, inv_2, 1, (self_q, self_k, self_v, self_log), self_near, self_far
            )

        def self_halo():
            left, right = event(got["self"][1], got["self"][2])
            got["halos"] = to_next(mark(right)), to_previous(left)

        def self_weights():
            low, dq, dk, dv = got["self"][5:9]
            got["self_grads"] = kernel(attend_weights, self_o, low, dq, dk, dv, low_1, left_1, low_1, right_1)

        def self_core():
            self_sum.core(*got["self_grads"])

        def cross_back():
            got["cross"] = kernel(
                attend_back, False, got["self"][0], got["halos"], norm_1, inv_1, 0,
                (cross_q, cross_k, cross_v, cross_log), cross_near, cross_far,
            )

        def cross_halo():
            left, right = event(got["cross"][1], got["cross"][2])
            got["cross_halos"] = to_next(mark(right)), to_previous(left)

        def cross_weights():
            low, dq, dk, dv = got["cross"][5:9]
            got["cross_grads"] = kernel(attend_weights, cross_o, low, dq, dk, dv, own, partner_left, partner, partner_right)

        def cross_core():
            cross_sum.core(*got["cross_grads"])

        def small_core():
            got["small"] = kernel(
                small_call(pack_small, small_shape, "pack_small"), got["bias"],
                got["cross"][3], got["self"][3], gain_3, got["cross"][4], got["self"][4], shift_3, down_bias_part, gate_bias_part,
            )
            got["small_got"] = mp(got["small"], 1)

        def small_over():
            got["small"] = kernel(small_call(add_small, small_shape, "add_small"), got["small"], got["small_got"])
            got["small_got"] = mp(got["small"], 2)

        def self_first():
            self_sum.fold(got["small"], got["small_got"])

        def partner():
            cot = glue(add_halos, rows_b, got["cross"][9], *got["cross_halos"])
            got["partner"] = dp(cot, half_axis)

        def partner_end():
            got["stream"] = glue(add_rows, rows_f, got["cross"][0], got["partner"])[None]

        def down_first():
            down_sum.begin(*got["down"])

        def up_first():
            up_sum.begin(*got["up"])

        def cross_first():
            cross_sum.fold()

        def gate_first():
            gate_sum.begin(*glue(
                functools.partial(gate_fold, gate_sum.order), gate_sum.halves, gate_near, gate_got, got["gate"]
            ))

        def gate_x():
            near = glue(
                functools.partial(take_gate, 0), struct((PIECES, gate_piece, width), BF), *gate_sum.sources()
            )
            got["gate_near"], got["gate_x"] = near, mp(near, 2)

        def gate_core():
            got["gate_x"] = event(got["gate_x"])
            got["gate_core"] = mp(got["gate_near"], 1), mp(mark(got["gate_x"]), 1)

        def gate_place():
            got["gate_grad"] = kernel(place_gate_call, *gate_sum.sources(), got["gate_x"], *got["gate_core"])

        def up_place():
            got["up_grad"] = kernel(place_hidden, *up_sum.sources())

        def down_place():
            got["down_grad"] = kernel(place_hidden, *down_sum.sources())

        def self_place():
            got["attn"] = kernel(place_layer, 1, self_sum.sources(), got.get("attn", ()))

        def cross_place():
            got["attn"] = kernel(place_layer, 0, cross_sum.sources(), got.get("attn", ()))

    groups = {"gate": gate_sum, "down": down_sum, "up": up_sum, "self": self_sum, "cross": cross_sum}
    def arrived(key):
        owner, _, field = key.partition(".")
        holder = vars(groups[owner]) if field else got
        if (field or owner) not in holder:
            return
        value = holder[field or owner]
        if isinstance(value, tuple):
            holder[field or owner] = event(*value)
            mark(holder[field or owner][-1])
        else:
            holder[field or owner] = mark(event(value))

    for name in ORDER:
        if name.startswith("+"):
            arrived(name[1:])
        elif hasattr(Event, name):
            getattr(Event, name)()
        else:
            group, stage = name.split("_", 1)
            getattr(groups[group], stage)()
    united_out = jnp.stack([pick(got["united"], index ^ sequence) for index in range(half_axis)]).astype(F32)

    mine_small = self_sum.piece[shard : shard + 9].astype(F32)
    other_small = self_sum.other[shard : shard + 9].astype(F32)
    is_text = modality == 0
    pair = jnp.stack([jnp.where(is_text, mine_small, other_small), jnp.where(is_text, other_small, mine_small)])
    attn_in_grad, attn_out_grad = got["attn"]
    return (
        united_out[:, None],
        got["stream"],
        attn_in_grad,
        attn_out_grad,
        got["up_grad"].reshape(2, PIECES * piece_rows, width),
        pair[:, 8],
        got["down_grad"].reshape(2, PIECES * piece_rows, width),
        pair[:, 6],
        pair[:, 0:3],
        pair[:, 3:6],
        got["gate_grad"].reshape(2, width, width),
        mine_small[7] + other_small[7],
    )


def solution(mesh):
    placed = (
        P("dp", "mp", None),
        P(),
        P(None, None, None, "mp", None),
        P(None, None, "mp", None),
        P(None, "mp", None),
        P(None, "mp"),
        P(None, "mp", None),
        P(),
        P(),
        P(),
        P(),
        P(),
        P(None, "mp", "dp", None),
    )
    return jax.shard_map(
        body,
        mesh=mesh,
        in_specs=placed,
        out_specs=(
            P(None, "mp", "dp", None),
            P("dp", "mp", None),
            P(None, None, None, "mp", None),
            P(None, None, "mp", None),
            P(None, "mp", None),
            P(None, "mp"),
            P(None, "mp", None),
            P(),
            P(),
            P(),
            P(),
            P(),
        ),
        check_vma=False,
    )
```

```python
import functools

import jax
import jax.numpy as jnp
from jax import lax
from jax.experimental import pallas as pl
from jax.experimental.pallas import tpu as pltpu
from jax.sharding import PartitionSpec as P

DH = 64
L = 1024
PAGES = 16
EPS = 1e-05
SCALE = 0.125
LOG2E = 1.4426950408889634
MASKED = -1e30
HALO = 128
PIECES = 4
BF = jnp.bfloat16
F32 = jnp.float32
VMEM_LIMIT = 16 * 1024 * 1024
SMALL_LIMIT = 4 * 1024 * 1024

VM = pl.BlockSpec(memory_space=pltpu.VMEM)
SM = pl.BlockSpec(memory_space=pltpu.SMEM)
ANY = pl.BlockSpec(memory_space=pl.ANY)


def nn(a, b):
    return lax.dot_general(a, b, (((1,), (0,)), ((), ())), preferred_element_type=F32)


def nt(a, b):
    return lax.dot_general(a, b, (((1,), (1,)), ((), ())), preferred_element_type=F32)


def tn(a, b):
    return lax.dot_general(a, b, (((0,), (0,)), ((), ())), preferred_element_type=F32)


def call(body, outs, scratch=(), flops=0, traffic=0, name=None, specs=None, out_specs=None, aliases=None, limit=VMEM_LIMIT):
    def run(*args):
        return pl.pallas_call(
            body,
            out_shape=outs,
            in_specs=specs if specs is not None else [SM] + [VM] * (len(args) - 1),
            out_specs=out_specs if out_specs is not None else jax.tree.map(lambda _: VM, outs),
            scratch_shapes=list(scratch),
            input_output_aliases=aliases or {},
            compiler_params=pltpu.CompilerParams(vmem_limit_bytes=limit),
            cost_estimate=pl.CostEstimate(flops=flops, bytes_accessed=traffic, transcendentals=0),
            name=name,
        )(*args)

    return run


def struct(shape, dtype):
    return jax.ShapeDtypeStruct(shape, dtype)


def after(value, *deps):
    return lax.optimization_barrier((value,) + deps)[0]


class Where:
    def __init__(self, scal, half_axis):
        self.modality = scal[0] // half_axis
        self.sequence = scal[0] % half_axis
        self.turn = scal[0] % PIECES
        self.place = scal[1]


def page_ends(pages, sequence):
    ends = []
    used = jnp.int32(0)
    running = jnp.int32(0)
    for page in range(PAGES):
        running = running + pages[sequence, page]
        fits = running <= L
        ends.append(jnp.where(fits, running, 2 * L))
        used = jnp.where(fits, running, used)
    return ends, used


def segment_of(position, ends):
    segment = jnp.zeros_like(position)
    for end in ends:
        segment = segment + (end <= position).astype(jnp.int32)
    return segment


def block_bias(ends, base, block, keys):
    query = base + block * HALO + lax.broadcasted_iota(jnp.int32, (HALO, 1), 0)
    key = base + (block - 1) * HALO + lax.broadcasted_iota(jnp.int32, (1, keys), 1)
    query_seg = segment_of(query, ends)
    key_seg = segment_of(key, ends)
    key_seg = jnp.where((key >= 0) & (key < L), key_seg, -1)
    return jnp.where(query_seg == key_seg, 0.0, MASKED)


def normalise(residual, gain, shift):
    center = residual - jnp.mean(residual, axis=-1, keepdims=True)
    inverse = lax.rsqrt(jnp.mean(center * center, axis=-1, keepdims=True) + EPS)
    normed = center * inverse
    return normed * gain + shift, normed, inverse


def norm_back(cot, gain, normed, inverse):
    grad = cot * gain
    back = inverse * (
        grad
        - jnp.mean(grad, axis=-1, keepdims=True)
        - normed * jnp.mean(grad * normed, axis=-1, keepdims=True)
    )
    return back, jnp.sum(cot * normed, axis=0, keepdims=True), jnp.sum(cot, axis=0, keepdims=True)


def attention_matrices(layer, turn, mine, far, near_pieces, far_pieces, pieces):
    for relative in range(PIECES):
        pieces[0, relative ^ turn] = near_pieces[relative][...]
        pieces[1, relative ^ turn] = far_pieces[relative][...]

    def matrix(which):
        return jnp.concatenate([mine[layer, which], pieces[0, which], far[layer, which], pieces[1, which]], axis=0)

    return matrix


def stack_heads(pair, first):
    zero = jnp.zeros_like(pair)
    return jnp.concatenate([jnp.where(first, pair, zero), jnp.where(first, zero, pair)], axis=0)


def extend(left, own, right, extended):
    rows = own.shape[0]
    extended[0:HALO, :] = left[...]
    extended[HALO : HALO + rows, :] = own[...]
    extended[HALO + rows : 2 * HALO + rows, :] = right[...]


def attention_forward(half_axis, layer, *refs):
    scal, pages, query_in, left, own, right, resid, params = refs[:8]
    mine, far, near_pieces, far_pieces = refs[8], refs[9], refs[10:14], refs[14:18]
    q_out, k_out, v_out, o_out, log_out, norm_out, inv_out, full_out, low_out, head_out, tail_out = refs[18:29]
    extended, pieces = refs[29:]
    where = Where(scal, half_axis)
    rows, width = query_in.shape
    window = 3 * HALO
    matrix = attention_matrices(layer, where.turn, mine, far, near_pieces, far_pieces, pieces)
    extend(left, own, right, extended)
    ends, _ = page_ends(pages, where.sequence)
    base = where.place * rows
    q_out[...] = nt(query_in[...], matrix(0)).astype(BF)
    k_out[...] = nt(extended[...], matrix(1)).astype(BF)
    v_out[...] = nt(extended[...], matrix(2)).astype(BF)
    lane = lax.broadcasted_iota(jnp.int32, (1, 2 * DH), 1)
    first = lane < DH
    for block in range(rows // HALO):
        bias = block_bias(ends, base, block, window)
        bias = jnp.concatenate([bias, bias], axis=0)
        row = slice(block * HALO, (block + 1) * HALO)
        span = slice(block * HALO, block * HALO + window)
        logs = jnp.zeros((HALO, 2 * DH), F32)
        for pair in range(width // (2 * DH)):
            cols = slice(pair * 2 * DH, (pair + 1) * 2 * DH)
            scores = nt(stack_heads(q_out[row, cols], first), k_out[span, cols])
            scores = scores * (SCALE * LOG2E) + bias
            top = jnp.max(scores, axis=-1, keepdims=True)
            expo = jnp.exp2(scores - top)
            total = jnp.sum(expo, axis=-1, keepdims=True)
            mixed = nn(expo.astype(BF), v_out[span, cols]) / total
            log = top + jnp.log2(total)
            logs = jnp.where(lane == 2 * pair, log[:HALO], jnp.where(lane == 2 * pair + 1, log[HALO:], logs))
            o_out[row, cols] = jnp.where(first, mixed[:HALO], mixed[HALO:]).astype(BF)
        log_out[row, :] = logs
    residual = resid[...].astype(F32) + nn(o_out[...], matrix(3))
    full, normed, inverse = normalise(residual, params[layer : layer + 1, :], params[3 + layer : 4 + layer, :])
    norm_out[...] = normed
    inv_out[...] = inverse
    full_out[...] = full
    low = full.astype(BF)
    low_out[...] = low
    head_out[...] = low[:HALO]
    tail_out[...] = low[rows - HALO :]


def attention_backward(half_axis, layer, same_input, *refs):
    scal, pages, cot_in, normed, inverse, params = refs[:6]
    q_in, k_in, v_in, log_in = refs[6:10]
    refs = refs[10:]
    halos = ()
    if not same_input:
        halos, refs = refs[:2], refs[2:]
    mine, far, near_pieces, far_pieces = refs[0], refs[1], refs[2:6], refs[6:10]
    refs = refs[10:]
    query_cot, to_left, to_right, gain_out, shift_out, low, dq, dkl, dvl = refs[:9]
    refs = refs[9:]
    if not same_input:
        key_cot, refs = refs[0], refs[1:]
    pieces, o_cot, dk, dv = refs
    where = Where(scal, half_axis)
    rows, width = cot_in.shape
    keys = rows + 2 * HALO
    window = 3 * HALO
    matrix = attention_matrices(layer, where.turn, mine, far, near_pieces, far_pieces, pieces)
    cot = cot_in[...]
    if halos:
        cot = cot + jnp.concatenate([halos[0][...], halos[1][...]], axis=0).astype(F32)
    back, gain_grad, shift_grad = norm_back(cot, params[layer : layer + 1, :], normed[...], inverse[...])
    gain_out[...] = gain_grad
    shift_out[...] = shift_grad
    query_cot[...] = back
    low[...] = back.astype(BF)
    o_cot[...] = nt(low[...], matrix(3)).astype(BF)
    ends, _ = page_ends(pages, where.sequence)
    base = where.place * rows
    lane = lax.broadcasted_iota(jnp.int32, (1, 2 * DH), 1)
    first = lane < DH
    dk[...] = jnp.zeros_like(dk)
    dv[...] = jnp.zeros_like(dv)
    for block in range(rows // HALO):
        bias = block_bias(ends, base, block, window)
        bias = jnp.concatenate([bias, bias], axis=0)
        row = slice(block * HALO, (block + 1) * HALO)
        span = slice(block * HALO, block * HALO + window)
        logs = log_in[row, :]
        for pair in range(width // (2 * DH)):
            cols = slice(pair * 2 * DH, (pair + 1) * 2 * DH)
            queries = stack_heads(q_in[row, cols], first)
            cots = stack_heads(o_cot[row, cols], first)
            key_pair = k_in[span, cols]
            log = jnp.concatenate([logs[:, 2 * pair : 2 * pair + 1], logs[:, 2 * pair + 1 : 2 * pair + 2]], axis=0)
            weights = jnp.exp2(nt(queries, key_pair) * (SCALE * LOG2E) + bias - log)
            weight_cot = nt(cots, v_in[span, cols])
            inner = jnp.sum(weights * weight_cot, axis=-1, keepdims=True)
            score_cot = (weights * (weight_cot - inner)).astype(BF)
            grads = nn(score_cot, key_pair)
            dq[row, cols] = (jnp.where(first, grads[:HALO], grads[HALO:]) * SCALE).astype(BF)
            dk[span, cols] += tn(score_cot, queries)
            dv[span, cols] += tn(weights.astype(BF), cots)
    dkl[...] = (dk[...] * SCALE).astype(BF)
    dvl[...] = dv[...].astype(BF)
    back = nn(dkl[...], matrix(1)) + nn(dvl[...], matrix(2))
    to_left[...] = back[0:HALO, :].astype(BF)
    to_right[...] = back[HALO + rows : keys, :].astype(BF)
    middle = back[HALO : HALO + rows, :]
    direct = nn(dq[...], matrix(0))
    if same_input:
        query_cot[...] += direct + middle
    else:
        query_cot[...] += direct
        key_cot[...] = middle


def attention_weights(half_axis, scal, o_in, low, dq, dk, dv, query_in, left, own, right, near_out, far_out, extended):
    turn = Where(scal, half_axis).turn
    extend(left, own, right, extended)
    piece = near_out.shape[1]
    jobs = ((0, dq, query_in), (1, dk, extended), (2, dv, extended), (3, o_in, low))
    for which, cots, inputs in jobs:
        value = tn(cots[...], inputs[...]).astype(BF)
        for place, (target, start) in enumerate(((near_out, 0), (near_out, PIECES), (far_out, 0), (far_out, PIECES))):
            target[start + (which ^ turn)] = value[place * piece : (place + 1) * piece]


def gelu_parts(value):
    root = 0.7978845608028654
    square = value * value
    inner = jnp.tanh(root * (value + 0.044715 * value * square))
    half = 0.5 * (1.0 + inner)
    slope = half + 0.5 * value * (1.0 - inner * inner) * (root * (1.0 + 3.0 * 0.044715 * square))
    return value * half, slope


def hidden_matrices(turn, refs):
    whole, pieces = (refs[0], refs[1]), (refs[2:7], refs[7:12])

    def matrix(kind, place):
        if place % 2 == 0:
            parts = [whole[place // 2][kind, relative ^ turn] for relative in range(PIECES)]
        else:
            x, y, z, *last = pieces[place // 2]
            parts = [x[kind], y[kind], z[kind], last[kind][...]]
        return jnp.concatenate(parts, axis=0)

    return matrix


def ffn_forward(half_axis, *refs):
    scal, low, full, bias_own, bias_x, bias_far, params = refs[:7]
    acts, (slope_out, norm_out, inv_out, keep_out, send_out) = refs[19:23], refs[23:28]
    where = Where(scal, half_axis)
    matrix = hidden_matrices(where.turn, refs[7:19])
    rows, width = low.shape
    total = full[...] + params[6:7, :]
    biases = (bias_own[...], bias_x[...], bias_far[0:1, :], bias_far[1:2, :])
    for place in range(4):
        cols = slice(place * width, (place + 1) * width)
        pre = nt(low[...], matrix(0, place)) + biases[place]
        value, slope = gelu_parts(pre)
        value = value.astype(BF)
        acts[place][...] = value
        slope_out[:, cols] = slope
        total = total + nn(value, matrix(1, place))
    out, normed, inverse = normalise(total, params[2:3, :], params[5:6, :])
    norm_out[...] = normed
    inv_out[...] = inverse
    out = out.astype(BF)
    half = rows // 2
    is_text = where.modality == 0
    keep_out[...] = jnp.where(is_text, out[:half], out[half:])
    send_out[...] = jnp.where(is_text, out[half:], out[:half])


def last_norm_backward(half_axis, scal, keep, got, normed, inverse, params, back_out, branch_out, gain_out, shift_out, bias_out):
    where = Where(scal, half_axis)
    is_text = where.modality == 0
    kept, other = keep[...], got[...]
    cot = jnp.concatenate([jnp.where(is_text, kept, other), jnp.where(is_text, other, kept)], axis=0).astype(F32)
    back, gain_grad, shift_grad = norm_back(cot, params[2:3, :], normed[...], inverse[...])
    back_out[...] = back
    branch_out[...] = back.astype(BF)
    gain_out[...] = gain_grad
    shift_out[...] = shift_grad
    bias_out[...] = jnp.sum(back, axis=0, keepdims=True)


def ffn_backward(half_axis, *refs):
    scal, back, branch, slope = refs[:4]
    cot_out, pre_own, pre_over, pre_core, bias_out = refs[16:21]
    where = Where(scal, half_axis)
    matrix = hidden_matrices(where.turn, refs[4:16])
    rows, width = branch.shape
    total = back[...]
    for place in range(4):
        cols = slice(place * width, (place + 1) * width)
        act_cot = nt(branch[...], matrix(1, place))
        pre_cot = (act_cot * slope[:, cols]).astype(BF)
        if place % 2 == 0:
            (pre_own, pre_core)[place // 2][...] = pre_cot
        else:
            pre_over[place // 2] = pre_cot
        bias_out[:, cols] = jnp.sum(pre_cot.astype(F32), axis=0, keepdims=True)
        total = total + nn(pre_cot, matrix(0, place))
    cot_out[...] = total


def split_piece(order, relative):
    return (relative % 2, relative // 2) if order == "yz" else (relative // 2, relative % 2)


def rows_product(half_axis, order, scal, left_own, left_over, left_core, left_relay, *refs):
    rights, (keep, send, parts) = refs[:4], refs[4:]
    total = tn(left_own[...], rights[0][...])
    if len(left_over.shape) == 3:
        left_over, left_relay = left_over.at[0], left_relay.at[1]
    for left, right in ((left_over[...], rights[1]), (left_core[...], rights[2]), (left_relay[...], rights[3])):
        total = total + tn(left, right[...])
    rows = parts.shape[1]
    for piece in range(PIECES):
        parts[piece] = total[piece * rows : (piece + 1) * rows].astype(BF)
    for relative in range(PIECES):
        side, index = split_piece(order, relative)
        target = (keep, send)[side]
        target[index, 0:rows, :] = parts[relative]


def sum_sent(scal, near, got, *outs):
    start = PIECES
    for out in outs:
        stop = start + out.shape[0]
        out[...] = (near[start:stop].astype(F32) + got[start:stop].astype(F32)).astype(BF)
        start = stop


def canonical(row, turn, piece):
    row = jnp.broadcast_to(row, (8, row.shape[1]))
    lane = lax.broadcasted_iota(jnp.int32, row.shape, 1)
    width = row.shape[1]
    swapped = jnp.where((lane // piece) % 2 == 0, pltpu.roll(row, width - piece, 1), pltpu.roll(row, piece, 1))
    row = jnp.where(turn % 2 == 1, swapped, row)
    return jnp.where(turn // 2 == 1, pltpu.roll(row, 2 * piece, 1), row)[0:1]


def sum_fold(order, scal, near, got, over_a, over_b, *refs):
    keep, send = refs[-2:]
    rows = near.shape[1]
    small = None
    if len(refs) > 2:
        mine, other = refs[:2]
        total = mine[4:12, :] + other[4:12, :]
        bias = canonical(mine[0:1, :] + other[1:2, :], scal[0] % PIECES, rows)
        small = jnp.concatenate([total, bias, jnp.zeros((7, total.shape[1]), F32)], axis=0).astype(BF)
    for relative in range(PIECES):
        side, index = split_piece(order, relative)
        target = (keep, send)[side]
        over = (over_a, over_b)[relative // 2][relative % 2]
        summed = near[relative].astype(F32) + got[relative].astype(F32) + over.astype(F32)
        target[index, 0:rows, :] = summed.astype(BF)
        if small is not None:
            target[index, rows : rows + 16, :] = small


def gate_fold(order, scal, near, got, over, keep, send):
    for relative in range(PIECES):
        side, index = split_piece(order, relative)
        summed = near[relative].astype(F32) + got[relative].astype(F32) + over[relative].astype(F32)
        (keep, send)[side][index] = summed.astype(BF)


def sum_second(scal, keep, got, kept, send):
    kept[...] = keep[0].astype(F32) + got[0].astype(F32)
    send[...] = (keep[1].astype(F32) + got[1].astype(F32)).astype(BF)


def sum_third(scal, kept, got, piece):
    piece[...] = (kept[...] + got[...].astype(F32)).astype(BF)


def join_pair(rows, scal, piece, other, pair):
    if rows:
        pair[0:rows, :] = piece[0:rows, :]
        pair[rows : 2 * rows, :] = other[0:rows, :]
    else:
        pair[...] = (piece[...].astype(F32) + other[...].astype(F32)).astype(BF)


def take_gate(start, scal, *refs):
    for piece, source in enumerate(refs[:PIECES]):
        refs[PIECES][piece] = source[start:, :]


def take_half(kind, scal, source, out):
    out[...] = source[kind]


def add_halos(scal, middle, left, right, out):
    out[0:HALO, :] = (middle[0:HALO, :] + left[...].astype(F32)).astype(BF)
    out[HALO:, :] = (middle[HALO:, :] + right[...].astype(F32)).astype(BF)


def add_rows(scal, left, right, out):
    out[...] = left[...] + right[...].astype(F32)


def gate_kernel(
    half_axis, scal, pages, keep, got, weight, params, cot_in,
    united, keep_out, send_out, near_out, far_out, bias_out, grads,
):
    where = Where(scal, half_axis)
    is_text = where.modality == 0
    kept, other = keep[...], got[...]
    text_low = jnp.where(is_text, kept, other)
    vision_low = jnp.where(is_text, other, kept)
    half, width = kept.shape
    _, used = page_ends(pages, where.sequence)
    position = where.place * (2 * half) + where.modality * half + lax.broadcasted_iota(jnp.int32, (half, 1), 0)
    mask = (position < used).astype(F32)
    gate = jax.nn.sigmoid(nt(text_low, weight[0]) + nt(vision_low, weight[1]) + params[7:8, :])
    text_full = text_low.astype(F32)
    vision_full = vision_low.astype(F32)
    united[...] = (mask * (gate * text_full + (1.0 - gate) * vision_full)).astype(BF)
    cot = cot_in[...].astype(F32) * mask
    gate_cot = (cot * (text_full - vision_full) * gate * (1.0 - gate)).astype(BF)
    text_cot = (cot * gate + nn(gate_cot, weight[0])).astype(BF)
    vision_cot = (cot * (1.0 - gate) + nn(gate_cot, weight[1])).astype(BF)
    keep_out[...] = jnp.where(is_text, text_cot, vision_cot)
    send_out[...] = jnp.where(is_text, vision_cot, text_cot)
    bias_out[...] = jnp.sum(gate_cot.astype(F32), axis=0, keepdims=True)
    grads[0:width, :] = tn(gate_cot, text_low)
    grads[width : 2 * width, :] = tn(gate_cot, vision_low)
    rows = near_out.shape[1]
    for spot, (target, start) in enumerate(((near_out, 0), (near_out, PIECES), (far_out, 0), (far_out, PIECES))):
        shard = where.place ^ (0, 2, 1, 3)[spot]
        for piece in range(PIECES):
            at = pl.multiple_of((shard * PIECES + (piece ^ where.turn)) * rows, rows)
            target[start + piece] = grads[pl.ds(at, rows), :].astype(BF)


def place_gate(half_axis, start, scal, *refs):
    near, over, far, far_over, out, wide, sems = refs[:4], *refs[4:]
    where = Where(scal, half_axis)
    rows = over.shape[1]
    copies = []
    for spot in range(4):
        shard = where.place ^ (0, 2, 1, 3)[spot]
        for piece in range(PIECES):
            if spot == 0:
                source = near[piece][start : start + rows, :]
            else:
                source = (over[piece], far[piece], far_over[piece])[spot - 1]
            slot = spot * PIECES + piece
            wide[slot] = source.astype(F32)
            copy = pltpu.make_async_copy(wide.at[slot], out.at[shard * PIECES + (piece ^ where.turn)], sems.at[slot])
            copy.start()
            copies.append(copy)
    for copy in copies:
        copy.wait()


def place_pieces(half_axis, layer, scal, *refs):
    wide, sems = refs[-2:]
    where = Where(scal, half_axis)
    sources, outs = refs[:4], refs[-3:-2] if layer is None else refs[-4:-2]
    rows = wide.shape[1]
    for relative, source in enumerate(sources):
        piece = relative ^ where.turn
        for kind in range(2):
            slot = relative * 2 + kind
            target = kind ^ where.modality
            wide[slot] = source[kind * rows : (kind + 1) * rows, :].astype(F32)

            def send(place, slot=slot):
                pltpu.make_async_copy(wide.at[slot], place, sems.at[slot]).start()

            if layer is None:
                send(outs[0].at[target, piece])
            else:
                pl.when(piece < 3)(lambda: send(outs[0].at[target, layer, piece]))
                pl.when(piece == 3)(lambda: send(outs[1].at[target, layer]))
    for slot in range(8):
        landing = outs[0].at[0, 0] if layer is None else outs[1].at[0, layer]
        pltpu.make_async_copy(wide.at[slot], landing, sems.at[slot]).wait()


def pack_small(scal, bias, *refs):
    out = refs[-1]
    width = out.shape[1]
    out[...] = jnp.zeros_like(out)
    for shard in range(4):
        out[shard : shard + 1, :] = bias[:, shard * width : (shard + 1) * width]
    for row, ref in enumerate(refs[:-1]):
        out[4 + row : 5 + row, :] = ref[...]


def add_small(scal, mine, got, out):
    out[...] = jnp.zeros_like(out)
    out[0:2, :] = mine[0:2, :] + got[2:4, :]
    out[4:12, :] = mine[4:12, :] + got[4:12, :]


SELF_ORDER = ("yz", "z")
CROSS_ORDER = ("zy", "y")
ORDER = (
    "branch_x", "branch_core", "act_relay", "ffn_back", "+branch_core", "+act_relay", "+branch_x", "branch_relay",
    "pre_x", "pre_core", "+branch_relay", "down_weights", "down_first", "self_back", "+core", "+down.got",
    "+over", "self_halo", "pre_relay", "down_second", "gate_over", "self_weights", "+halos", "+relay",
    "self_core", "up_weights", "+self.got", "up_first", "self_over", "cross_back", "+gate", "+self.from_x",
    "+down.got", "+up.got", "self_rest_over", "down_third", "up_second", "small_core", "gate_first", "small_over",
    "cross_weights", "up_third", "+small_got", "united_first", "cross_core", "gate_second", "+cross.got",
    "down_fourth", "+gate.got", "+up.other", "cross_over", "self_first", "+down.y", "up_fourth", "+down.z",
    "cross_rest_over", "+cross.from_x", "gate_third", "self_second", "+up.z", "down_fifth", "cross_first",
    "+self.got", "gate_fourth", "+up.y", "cross_halo", "+cross_halos", "united_rest", "self_third",
    "cross_second", "gate_fifth", "+down.far", "up_fifth", "cross_third", "+gate.y", "self_fourth", "+gate.far",
    "cross_fourth", "down_place", "+up.far", "gate_x", "self_fifth", "+self.z", "partner", "cross_fifth",
    "+cross.y", "gate_core", "up_place", "gate_place", "partner_end", "self_place", "cross_place",
)


def body(
    streams, page_lengths, attn_in, attn_out, ffn_in, ffn_bias, ffn_out, out_bias,
    norm_gain, norm_bias, gate_weight, gate_bias, united_grad,
):
    devices = lax.axis_size("dp")
    half_axis = devices // 2
    group_bits = half_axis.bit_length() - 1
    data_index = lax.axis_index("dp")
    place = lax.axis_index("mp")
    modality = data_index // half_axis
    sequence = data_index % half_axis
    turn = data_index % PIECES
    own = streams[0]
    rows, width = own.shape
    keys = rows + 2 * HALO
    shard = attn_in.shape[3]

    def swap(value, axis, mask):
        pairs = [(source, source ^ mask) for source in range(lax.axis_size(axis))]
        return lax.ppermute(value, axis, pairs)

    def mp(value, mask):
        return swap(value, "mp", mask)

    def dp(value, mask):
        return swap(value, "dp", mask)

    count = lax.axis_size("mp")

    def to_next(value):
        return lax.ppermute(value, "mp", [(index, index + 1) for index in range(count - 1)])

    def to_previous(value):
        return lax.ppermute(value, "mp", [(index + 1, index) for index in range(count - 1)])

    def pick(stacked, index):
        return lax.dynamic_index_in_dim(stacked, index, 0, keepdims=False)

    scal = jnp.stack([data_index, place]).astype(jnp.int32)
    clock = [scal]

    def event(*values):
        fenced = lax.optimization_barrier(values + (clock[0],))[:-1]
        return fenced if len(fenced) > 1 else fenced[0]

    def mark(value):
        clock[0] = value
        return value

    def kernel(run, *args, due=()):
        now = after(scal, clock[0], *due)
        results = run(now, *args)
        mark(results[-1] if isinstance(results, (list, tuple)) else results)
        return results

    def add(left, right):
        return (left.astype(F32) + right.astype(F32)).astype(BF)

    def glue(run, outs, *args, due=()):
        def launch(now, *operands):
            return call(
                run, outs, [], 1 << 16, 1 << 18, getattr(run, "func", run).__name__, [SM] + [VM] * len(operands), limit=SMALL_LIMIT
            )(now, *operands)

        return kernel(launch, *args, due=due)

    piece_rows = ffn_in.shape[1] // PIECES
    half_rows = rows // 2
    slice_rows = united_grad.shape[2]

    def attention_piece(layer, index):
        inner = lax.dynamic_slice(
            attn_in, (index, layer, jnp.minimum(turn, 2), 0, 0), (1, 1, 1, shard, width)
        ).reshape(shard, width)
        outer = lax.dynamic_slice(attn_out, (index, layer, 0, 0), (1, 1, shard, width)).reshape(shard, width)
        return jnp.where(turn < 3, inner, outer)

    def group_exchange(blocks):
        moved = jnp.stack([pick(blocks, index ^ sequence) for index in range(half_axis)])
        shape = moved.shape
        for bit in range(group_bits):
            view = moved.reshape((half_axis >> (bit + 1), 2, 1 << bit) + shape[1:])
            got = dp(view[:, 1], 1 << bit)
            moved = jnp.stack([view[:, 0], got], axis=1).reshape(shape)
        return jnp.stack([pick(moved, index ^ sequence) for index in range(half_axis)])

    cross_x = mp(mark(attention_piece(0, modality)), 2)
    partner = dp(own, half_axis)
    self_x = mp(mark(attention_piece(1, event(modality))), 2)
    index = event(modality)
    hidden_part = jnp.stack([
        lax.dynamic_slice(weight, (index, turn * piece_rows, 0), (1, piece_rows, width))[0] for weight in (ffn_in, ffn_out)
    ])
    cross_x, hidden_part = event(cross_x, hidden_part)
    cross_y, cross_z = dp(mark(cross_x), 1), dp(cross_x, 2)
    hidden_x = mp(hidden_part, 2)
    index = event(modality)
    mine = mark(jnp.concatenate([pick(attn_in, index), pick(attn_out, index)[:, None]], axis=1))
    partner, cross_y = event(partner, cross_y)
    partner_left = to_next(partner[rows - HALO :])
    partner_right = to_previous(mark(partner[:HALO]))
    cross_yz = dp(cross_y, 2)
    self_x = mark(event(self_x))
    self_y, self_z = dp(self_x, 1), dp(self_x, 2)
    far = mp(event(mine), 1)
    cross_near = (cross_x, cross_y, cross_z, cross_yz)
    cross_far = tuple(mp(mark(event(piece)), 1) for piece in cross_near)
    index = event(modality)
    hidden_mine = mark(jnp.stack([pick(ffn_in, index), pick(ffn_out, index)]).reshape(2, PIECES, piece_rows, width))
    bias_own = jnp.concatenate([
        lax.dynamic_slice(ffn_bias, (index, (relative ^ turn) * piece_rows), (1, piece_rows)) for relative in range(PIECES)
    ], axis=1)
    params = jnp.concatenate(
        [pick(norm_gain, index), pick(norm_bias, index), pick(out_bias, index)[None], gate_bias[None]], axis=0
    )
    bias_x = mp(mark(bias_own), 2)
    gate_cot_in = mark(group_exchange(event(united_grad[:, 0])).reshape(half_rows, width))
    bias_x = event(bias_x)
    bias_far = mp(mark(jnp.concatenate([bias_own, bias_x], axis=0)), 1)
    hidden_x, self_y, self_z = event(hidden_x, self_y, self_z)
    self_yz = dp(mark(self_z), 1)
    hidden_y, hidden_z = dp(mark(event(hidden_x)), 1), dp(hidden_x, 2)
    self_near_three = tuple(mp(event(piece), 1) for piece in (self_x, self_y, self_z))

    rows_f = struct((rows, width), F32)
    rows_b = struct((rows, width), BF)
    keys_b = struct((keys, width), BF)
    row_f = struct((1, width), F32)
    column_f = struct((rows, 1), F32)
    halo_b = struct((HALO, width), BF)
    half_b = struct((half_rows, width), BF)
    attn_flops = 2 * width * width * (2 * rows + 2 * keys)
    matrix_scratch = [pltpu.VMEM((2, PIECES, shard, width), BF)]

    def attend(now, query_in, left, own_rows, right, resid, layer, near, far_pieces):
        return call(
            functools.partial(attention_forward, half_axis, layer),
            [rows_b, keys_b, keys_b, rows_b, struct((rows, 2 * DH), F32), rows_f, column_f, rows_f, rows_b, halo_b, halo_b],
            [pltpu.VMEM((keys, width), BF)] + matrix_scratch,
            attn_flops, 12 << 20, "attend", [SM, SM] + [VM] * 16,
        )(now, page_lengths, query_in, left, own_rows, right, resid, params, mine, far, *near, *far_pieces)

    cross_q, cross_k, cross_v, cross_o, cross_log, norm_1, inv_1, full_1, low_1, head_1, tail_1 = kernel(
        attend, own, partner_left, partner, partner_right, own, 0, cross_near, cross_far
    )
    self_yz, tail_1, head_1 = event(self_yz, tail_1, head_1)
    left_1 = to_next(mark(tail_1))
    right_1 = to_previous(head_1)
    self_near = (self_x, self_y, self_z, self_yz)
    self_far = self_near_three + (mp(self_yz, 1),)
    left_1, right_1 = event(left_1, right_1)
    hidden_y, hidden_z, left_1 = event(hidden_y, hidden_z, left_1)
    mark(left_1)
    piece_shape = struct((piece_rows, width), BF)
    up_yz = dp(glue(functools.partial(take_half, 0), piece_shape, hidden_y), 2)
    down_yz = dp(glue(functools.partial(take_half, 1), piece_shape, hidden_z), 1)
    hidden_far_mine, hidden_far_x = mp(event(hidden_mine), 1), mp(hidden_x, 1)
    self_q, self_k, self_v, self_o, self_log, norm_2, inv_2, full_2, low_2, _, _ = kernel(
        attend, low_1, left_1, low_1, right_1, full_1, 1, self_near, self_far
    )
    up_yz, down_yz, hidden_far_mine, hidden_far_x = event(up_yz, down_yz, hidden_far_mine, hidden_far_x)
    mark(up_yz)
    hidden_far = (hidden_far_x, mp(hidden_y, 1), mp(hidden_z, 1), mp(up_yz, 1), mp(down_yz, 1))

    hidden = 4 * PIECES * piece_rows
    hidden_weights = (
        hidden_mine, hidden_far_mine, hidden_x, hidden_y, hidden_z, up_yz, down_yz, *hidden_far
    )
    over_b = struct((2, rows, width), BF)

    def feed_forward(now, *args):
        return call(
            functools.partial(ffn_forward, half_axis),
            [rows_b] * 4 + [struct((rows, hidden), F32), rows_f, column_f, half_b, half_b],
            [], 4 * rows * hidden * width, 18 << 20, "feed_forward", [SM] + [VM] * 18,
        )(now, *args)

    low_x, low_core = mp(low_2, 2), mp(low_2, 1)
    act_own, act_x, act_core, act_diagonal, slope, norm_3, inv_3, keep_3, send_3 = kernel(
        feed_forward, low_2, full_2, bias_own, bias_x, bias_far, params, *hidden_weights
    )

    got_3 = dp(send_3, half_axis)
    act_x = mp(event(act_x), 2)
    gate_piece = 2 * width // (4 * PIECES)
    gate_half = struct((2 * PIECES, gate_piece, width), BF)

    def gate_call(now, *args):
        return call(
            functools.partial(gate_kernel, half_axis),
            [half_b, half_b, half_b, gate_half, gate_half, row_f],
            [pltpu.VMEM((2 * width, width), F32)],
            12 * half_rows * width * width, 8 << 20, "gate", [SM, SM] + [VM] * 5,
        )(now, *args)

    united, keep_cot, send_cot, gate_near, gate_far, gate_bias_part = kernel(
        gate_call, page_lengths, keep_3, got_3, gate_weight, params, gate_cot_in, due=(low_core, low_x, act_x)
    )
    got_cot = dp(send_cot, half_axis)
    gate_got = mp(gate_far, 1)
    act_diagonal, act_core, low_sent = event(act_diagonal, act_core, low_x)
    act_diagonal = mp(act_diagonal, 2)
    act_core = mp(act_core, 1)
    low_relay = mp(low_sent, 1)
    gate_sent = glue(sum_sent, struct((PIECES, gate_piece, width), BF), gate_near, gate_got)

    def last_norm(now, *args):
        return call(
            functools.partial(last_norm_backward, half_axis),
            [rows_f, rows_b, row_f, row_f, row_f], [], 1 << 20, 3 << 20, "last_norm_back", [SM] + [VM] * 5,
        )(now, *args)

    back_3, branch, gain_3, shift_3, down_bias_part = kernel(last_norm, keep_cot, got_cot, norm_3, inv_3, params, due=(act_diagonal, act_core, low_relay))

    class Sum:
        def __init__(self, order, last, extra=0, main=piece_rows):
            self.order, self.last, self.main = order, last, main
            self.rows = main + extra
            self.halves = [struct((2, self.rows, width), BF)] * 2

        def core(self, near, far):
            self.near = near
            self.got = mp(mark(event(far)), 1)

        def over(self):
            half = struct((2, piece_rows, width), BF)
            first, self.rest = glue(sum_sent, [half, half], self.near, self.got)
            self.from_x = mp(first, 2)

        def rest_over(self):
            self.rest_x = mp(mark(event(self.rest)), 2)

        def fold(self, *small):
            self.begin(*glue(
                functools.partial(sum_fold, self.order), self.halves, self.near, self.got, self.from_x, self.rest_x, *small
            ))

        def begin(self, keep, send):
            self.keep = keep
            self.got = dp(send, 1 if self.order == "yz" else 2)

        def second(self):
            self.kept, send = glue(
                sum_second, [struct((self.rows, width), F32), struct((self.rows, width), BF)], self.keep, self.got
            )
            self.got = dp(send, 2 if self.order == "yz" else 1)

        def third(self):
            piece = glue(sum_third, struct((self.rows, width), BF), self.kept, self.got)
            for bit in range(2, group_bits):
                piece = add(piece, dp(piece, 1 << bit))
            self.piece = mark(piece)
            self.other = dp(piece, half_axis)

        def fourth(self):
            self.pair = glue(
                functools.partial(join_pair, self.main), struct((2 * self.main or self.rows, width), BF), self.piece, self.other
            )
            self.y, self.z = dp(self.pair, 1), dp(self.pair, 2)

        def fifth(self):
            if self.last == "y":
                self.z = event(self.z)
                self.far = dp(mark(self.z), 1)
            else:
                self.y = event(self.y)
                self.far = dp(mark(self.y), 2)

        def sources(self):
            return self.pair, self.y, self.z, self.far

    down_sum, up_sum, self_sum, cross_sum = Sum("yz", "y"), Sum("zy", "y"), Sum(*SELF_ORDER, 16), Sum(*CROSS_ORDER)
    gate_sum = Sum("zy", "y", gate_piece, 0)
    attn_half = struct((2 * PIECES, shard, width), BF)
    small_shape = struct((16, width), F32)
    wide = [pltpu.VMEM((8, piece_rows, width), F32), pltpu.SemaphoreType.DMA((8,))]

    def ffn_back(now, *args):
        return call(
            functools.partial(ffn_backward, half_axis),
            [rows_f, rows_b, over_b, rows_b, struct((1, hidden), F32)],
            [], 4 * rows * hidden * width, 16 << 20, "feed_forward_back", [SM] + [VM] * 15,
        )(now, *args)

    def weight_product(name, group, now, *args):
        return call(
            functools.partial(rows_product, half_axis, group.order), group.halves,
            [pltpu.VMEM((PIECES, piece_rows, width), BF)], 8 * rows * width * width, 5 << 20, name, [SM] + [VM] * len(args),
        )(now, *args)

    def attend_back(now, same_input, cot_in, halos, normed, inverse, layer, saved, near, far_pieces):
        outs = [rows_f, halo_b, halo_b, row_f, row_f, rows_b, rows_b, keys_b, keys_b] + [rows_f] * (not same_input)
        return call(
            functools.partial(attention_backward, half_axis, layer, same_input),
            outs,
            [
                pltpu.VMEM((2, PIECES, shard, width), BF), pltpu.VMEM((rows, width), BF), pltpu.VMEM((keys, width), F32),
                pltpu.VMEM((keys, width), F32),
            ],
            attn_flops, 14 << 20, "attend_back", [SM, SM] + [VM] * (18 + len(halos)),
        )(now, page_lengths, cot_in, normed, inverse, params, *saved, *halos, mine, far, *near, *far_pieces)

    def attend_weights(now, *args):
        return call(
            functools.partial(attention_weights, half_axis),
            [attn_half, attn_half], [pltpu.VMEM((keys, width), BF)],
            attn_flops, 10 << 20, "attend_weights", [SM] + [VM] * 9,
        )(now, *args)

    def place_hidden(now, *sources):
        return call(
            functools.partial(place_pieces, half_axis, None), struct((2, PIECES, piece_rows, width), F32), wide,
            0, 7 << 20, "place_hidden", [SM] + [VM] * 4, ANY,
        )(now, *sources)

    attn_shapes = [struct((2, 2, 3, shard, width), F32), struct((2, 2, shard, width), F32)]

    def place_layer(now, layer, sources, previous):
        return call(
            functools.partial(place_pieces, half_axis, layer), attn_shapes, wide, 0, 7 << 20, "place_layer",
            [SM] + [VM] * 4 + [ANY] * len(previous), [ANY, ANY], {5: 0, 6: 1} if previous else None,
        )(now, *sources, *previous)

    def place_gate_call(now, *args):
        return call(
            functools.partial(place_gate, half_axis, 0), struct((4 * PIECES, gate_piece, width), F32),
            [pltpu.VMEM((4 * PIECES, gate_piece, width), F32), pltpu.SemaphoreType.DMA((4 * PIECES,))],
            0, 7 << 20, "place_gate", [SM] + [VM] * 7, ANY,
        )(now, *args)

    def small_call(run, shape, name):
        return lambda now, *args: call(
            run, shape, [], 1 << 16, 1 << 18, name, [SM] + [VM] * len(args), limit=SMALL_LIMIT
        )(now, *args)

    got = {"act_diagonal": act_diagonal}

    class Event:
        def act_relay():
            got["act_relay"] = mp(mark(event(got["act_diagonal"])), 1)

        def united_first():
            blocks = united.reshape(half_axis, slice_rows, width)
            moved = jnp.stack([pick(event(blocks), index ^ sequence) for index in range(half_axis)])
            view = moved.reshape((half_axis // 2, 2) + moved.shape[1:])
            got["united"] = view[:, 0], dp(mark(view[:, 1]), 1)

        def united_rest():
            kept, other = event(*got["united"])
            moved = jnp.stack([kept, other], axis=1).reshape(half_axis, slice_rows, width)
            for bit in range(1, group_bits):
                view = moved.reshape((half_axis >> (bit + 1), 2, 1 << bit) + moved.shape[1:])
                moved = jnp.stack([view[:, 0], dp(mark(view[:, 1]), 1 << bit)], axis=1).reshape(moved.shape)
            got["united"] = moved

        def gate_over():
            got["gate"] = mp(mark(event(gate_sent)), 2)

        def branch_x():
            got["branch_x"] = mp(mark(event(branch)), 2)

        def branch_core():
            got["branch_core"] = mp(mark(event(branch)), 1)

        def branch_relay():
            got["branch_x"] = event(got["branch_x"])
            got["branch_relay"] = mp(mark(got["branch_x"]), 1)

        def ffn_back():
            got["cot_2"], got["own"], got["over"], got["core"], got["bias"] = kernel(ffn_back, back_3, branch, slope, *hidden_weights)

        def pre_x():
            got["over"] = mp(mark(event(got["over"])), 2)

        def pre_core():
            got["core"] = mp(mark(event(got["core"])), 1)

        def pre_relay():
            got["over"] = event(got["over"])
            got["relay"] = mp(mark(got["over"]), 1)

        def down_weights():
            got["down"] = kernel(
                functools.partial(weight_product, "down_weights", down_sum), act_own, act_x, act_core, got["act_relay"],
                branch, got["branch_x"], got["branch_core"], got["branch_relay"],
            )

        def up_weights():
            got["up"] = kernel(
                functools.partial(weight_product, "up_weights", up_sum), got["own"], got["over"], got["core"], got["relay"],
                low_2, low_x, low_core, low_relay,
            )

        def self_back():
            got["self"] = kernel(
                attend_back, True, got["cot_2"], (), norm_2, inv_2, 1, (self_q, self_k, self_v, self_log), self_near, self_far
            )

        def self_halo():
            left, right = event(got["self"][1], got["self"][2])
            got["halos"] = to_next(mark(right)), to_previous(left)

        def self_weights():
            low, dq, dk, dv = got["self"][5:9]
            got["self_grads"] = kernel(attend_weights, self_o, low, dq, dk, dv, low_1, left_1, low_1, right_1)

        def self_core():
            self_sum.core(*got["self_grads"])

        def cross_back():
            got["cross"] = kernel(
                attend_back, False, got["self"][0], got["halos"], norm_1, inv_1, 0,
                (cross_q, cross_k, cross_v, cross_log), cross_near, cross_far,
            )

        def cross_halo():
            left, right = event(got["cross"][1], got["cross"][2])
            got["cross_halos"] = to_next(mark(right)), to_previous(left)

        def cross_weights():
            low, dq, dk, dv = got["cross"][5:9]
            got["cross_grads"] = kernel(attend_weights, cross_o, low, dq, dk, dv, own, partner_left, partner, partner_right)

        def cross_core():
            cross_sum.core(*got["cross_grads"])

        def small_core():
            got["small"] = kernel(
                small_call(pack_small, small_shape, "pack_small"), got["bias"],
                got["cross"][3], got["self"][3], gain_3, got["cross"][4], got["self"][4], shift_3, down_bias_part, gate_bias_part,
            )
            got["small_got"] = mp(got["small"], 1)

        def small_over():
            got["small"] = kernel(small_call(add_small, small_shape, "add_small"), got["small"], got["small_got"])
            got["small_got"] = mp(got["small"], 2)

        def self_first():
            self_sum.fold(got["small"], got["small_got"])

        def partner():
            cot = glue(add_halos, rows_b, got["cross"][9], *got["cross_halos"])
            got["partner"] = dp(cot, half_axis)

        def partner_end():
            got["stream"] = glue(add_rows, rows_f, got["cross"][0], got["partner"])[None]

        def down_first():
            down_sum.begin(*got["down"])

        def up_first():
            up_sum.begin(*got["up"])

        def cross_first():
            cross_sum.fold()

        def gate_first():
            gate_sum.begin(*glue(
                functools.partial(gate_fold, gate_sum.order), gate_sum.halves, gate_near, gate_got, got["gate"]
            ))

        def gate_x():
            near = glue(
                functools.partial(take_gate, 0), struct((PIECES, gate_piece, width), BF), *gate_sum.sources()
            )
            got["gate_near"], got["gate_x"] = near, mp(near, 2)

        def gate_core():
            got["gate_x"] = event(got["gate_x"])
            got["gate_core"] = mp(got["gate_near"], 1), mp(mark(got["gate_x"]), 1)

        def gate_place():
            got["gate_grad"] = kernel(place_gate_call, *gate_sum.sources(), got["gate_x"], *got["gate_core"])

        def up_place():
            got["up_grad"] = kernel(place_hidden, *up_sum.sources())

        def down_place():
            got["down_grad"] = kernel(place_hidden, *down_sum.sources())

        def self_place():
            got["attn"] = kernel(place_layer, 1, self_sum.sources(), got.get("attn", ()))

        def cross_place():
            got["attn"] = kernel(place_layer, 0, cross_sum.sources(), got.get("attn", ()))

    groups = {"gate": gate_sum, "down": down_sum, "up": up_sum, "self": self_sum, "cross": cross_sum}
    def arrived(key):
        owner, _, field = key.partition(".")
        holder = vars(groups[owner]) if field else got
        if (field or owner) not in holder:
            return
        value = holder[field or owner]
        if isinstance(value, tuple):
            holder[field or owner] = event(*value)
            mark(holder[field or owner][-1])
        else:
            holder[field or owner] = mark(event(value))

    for name in ORDER:
        if name.startswith("+"):
            arrived(name[1:])
        elif hasattr(Event, name):
            getattr(Event, name)()
        else:
            group, stage = name.split("_", 1)
            getattr(groups[group], stage)()
    united_out = jnp.stack([pick(got["united"], index ^ sequence) for index in range(half_axis)]).astype(F32)

    mine_small = self_sum.piece[shard : shard + 9].astype(F32)
    other_small = self_sum.other[shard : shard + 9].astype(F32)
    is_text = modality == 0
    pair = jnp.stack([jnp.where(is_text, mine_small, other_small), jnp.where(is_text, other_small, mine_small)])
    attn_in_grad, attn_out_grad = got["attn"]
    return (
        united_out[:, None],
        got["stream"],
        attn_in_grad,
        attn_out_grad,
        got["up_grad"].reshape(2, PIECES * piece_rows, width),
        pair[:, 8],
        got["down_grad"].reshape(2, PIECES * piece_rows, width),
        pair[:, 6],
        pair[:, 0:3],
        pair[:, 3:6],
        got["gate_grad"].reshape(2, width, width),
        mine_small[7] + other_small[7],
    )


def solution(mesh):
    placed = (
        P("dp", "mp", None),
        P(),
        P(None, None, None, "mp", None),
        P(None, None, "mp", None),
        P(None, "mp", None),
        P(None, "mp"),
        P(None, "mp", None),
        P(),
        P(),
        P(),
        P(),
        P(),
        P(None, "mp", "dp", None),
    )
    return jax.shard_map(
        body,
        mesh=mesh,
        in_specs=placed,
        out_specs=(
            P(None, "mp", "dp", None),
            P("dp", "mp", None),
            P(None, None, None, "mp", None),
            P(None, None, "mp", None),
            P(None, "mp", None),
            P(None, "mp"),
            P(None, "mp", None),
            P(),
            P(),
            P(),
            P(),
            P(),
        ),
        check_vma=False,
    )
```
